128 devices in a mesh: dp: 4 (over z_lo, core), seq: 32 (over z_hi, y, x).
Axes of the slice: x: 4, y: 4, z: 4 (z_hi: 2, z_lo: 2; z = z_hi * 2 + z_lo), core: 2. Of those that a mesh axis runs over, the one named last changes fastest.
Arguments:
- tokens: bfloat16 [4, 4096, 2048], P('dp', 'seq'), may hold values from -40 to 40
- cotangent: bfloat16 [4, 4096, 2048], P('dp', 'seq'), may hold values from -6 to 6
- w_qkv: bfloat16 [2048, 3072], replicated
- w_out: bfloat16 [2048, 1024], replicated, may hold values from -0.1875 to 0.1875
- key_blocks: int32 [32, 3], replicated, may hold values from 0 to 31, as said below
- key_count: int32 [32], replicated, may hold values from 1 to 3, as said below
Outputs:
- layer_out: bfloat16 [4, 4096, 2048], P('dp', 'seq')
- grad_tokens: bfloat16 [4, 4096, 2048], P('dp', 'seq')
- grad_w_qkv: float32 [2048, 3072], P('seq')
- grad_w_out: float32 [2048, 1024], P('seq')
The draws below stay inside these ranges and needn't reach their ends.
Inputs may be any that keep to these rules, and one draw needn't show every extreme that they name: Query block b uses the first key_count[b] entries of row b of key_blocks; 3 is reached in every draw. `key_blocks`: the first key_count[b] entries of row b are distinct; every entry e of row b satisfies |e - b| <= 1; among its used entries, the last block of every run of 1 block lists the block after it and the first block of every run lists the block before it, where those exist.
All inputs are finite; a program needn't handle non-finite values.
Results may differ from the reference program's by a relative error of at most 0.034.
Values may be sent and summed in bfloat16 or wider, within the bound.
A program may use at most 128 MiB of HBM per device.

```python
import math
import jax
import jax.numpy as jnp
from jax import lax

D = 2048
LOCAL_HEADS = 8
HEAD = 128
INNER = 1024
MASK_BLOCK_SIZE = 128
TOK_DEV = 128
BLOCKS_DEV = 1
MASK_BLOCKS = 3
SEQ_LEN = 4096
BLOCKS = 32
SEQS = 4
ALL_TOKENS = 16384
N_SEQ = 32


def draw_tokens(key, part):
    full_shape = (SEQS, SEQ_LEN, D)
    subkeys = jax.random.split(jax.random.fold_in(key, 11), 1)
    drawn = jnp.clip(jax.random.normal(subkeys[0], full_shape, jnp.float32), -6.0, 6.0)
    return drawn.astype(jnp.bfloat16)


def draw_w_qkv(key, part):
    subkeys = jax.random.split(jax.random.fold_in(key, 23), 1)
    inner = LOCAL_HEADS * HEAD
    spread = D ** (-0.5)
    drawn_draw = jnp.clip(jax.random.normal(subkeys[0], (D, 3 * inner), jnp.float32), -4.0, 4.0) * spread
    return drawn_draw.astype(jnp.bfloat16)


def mask_tables(key):
    subkeys = jax.random.split(jax.random.fold_in(key, 7), 4)
    block_ids = jnp.arange(BLOCKS, dtype=jnp.int32)
    devices = BLOCKS // BLOCKS_DEV
    device = block_ids // BLOCKS_DEV
    slot_ids = jnp.arange(MASK_BLOCKS, dtype=jnp.int32)
    group_ids = slot_ids // BLOCKS_DEV
    within = slot_ids % BLOCKS_DEV
    block_offsets = jnp.where(group_ids == 1, -1, jnp.where(group_ids == 2, 1, 0))
    near_device = device[:, None] + block_offsets[None, :]
    candidates = near_device * BLOCKS_DEV + within[None, :]
    usable = (near_device >= 0) & (near_device < devices)
    is_self = candidates == block_ids[:, None]
    last_of_run = block_ids % BLOCKS_DEV == BLOCKS_DEV - 1
    first_of_run = block_ids % BLOCKS_DEV == 0
    has_upper = last_of_run & (block_ids + 1 < BLOCKS)
    has_lower = first_of_run & (block_ids > 0)
    needs_upper = has_upper[:, None] & (candidates == block_ids[:, None] + 1) & usable
    needs_lower = has_lower[:, None] & (candidates == block_ids[:, None] - 1) & usable
    required = needs_upper | needs_lower
    jitter = jax.random.randint(subkeys[0], (BLOCKS, MASK_BLOCKS), 0, 4096)
    ranking = jitter * MASK_BLOCKS + slot_ids[None, :]
    ranking = jnp.where(usable, ranking, 4096 * MASK_BLOCKS + slot_ids[None, :])
    ranking = jnp.where(required, -1, ranking)
    ranking = jnp.where(is_self, -2, ranking)
    ordering = jnp.argsort(ranking, axis=1, stable=True)
    filled = jnp.where(usable, candidates, block_ids[:, None])
    listed = jnp.take_along_axis(filled, ordering, axis=1)
    usable_count = jnp.sum(usable.astype(jnp.int32), axis=1)
    need = 1 + has_upper.astype(jnp.int32) + has_lower.astype(jnp.int32)
    dense_row = jax.random.randint(subkeys[1], (BLOCKS,), 0, 4) == 0
    extra_count = jax.random.randint(subkeys[2], (BLOCKS,), 1, 3)
    sparse_count = jnp.minimum(need + extra_count, usable_count)
    counts = jnp.where(dense_row, usable_count, sparse_count)
    counts = jnp.maximum(counts, need)
    chosen = jax.random.randint(subkeys[3], (), BLOCKS_DEV, BLOCKS - BLOCKS_DEV)
    counts = jnp.where(block_ids == chosen, MASK_BLOCKS, counts)
    return (listed.astype(jnp.int32), counts.astype(jnp.int32))


def draw_key_blocks(key, part):
    return mask_tables(key)[0]


def draw_key_count(key, part):
    return mask_tables(key)[1]


def steps_of(own_key, dims, cuts, smallest, top_value):
    factor_of = 1.0
    for axis_at, blocks in cuts:
        heights = jax.random.uniform(jax.random.fold_in(jax.random.fold_in(own_key, 6), axis_at), (blocks,), jnp.float32, smallest / len(cuts), top_value / len(cuts))
        factor_of = factor_of * jnp.repeat(jnp.exp(heights), dims[axis_at] // blocks).reshape((-1,) + (1,) * (len(dims) - 1 - axis_at))
    return factor_of


def normal_values(rng, shape, scale, limit, pieces=(), kind=jnp.bfloat16):
    values = jax.random.normal(rng, shape, jnp.float32) * scale
    if len(pieces) > 0:
        values = steps_of(rng, shape, pieces, -0.22, 0.18) * values
    return jnp.clip(values, min=-limit, max=limit).astype(kind)


def setup_inputs(seed: int = 0) -> dict:
    splits = jax.random.split(jax.random.key(seed), 7)
    return {
        "tokens": draw_tokens(jax.random.fold_in(splits[6], 71), 0),
        "cotangent": normal_values(splits[1], (SEQS, SEQ_LEN, D), 1.0, 6.0, ((0, 4), (1, 32))),
        "w_qkv": draw_w_qkv(jax.random.fold_in(splits[6], 71), 0),
        "w_out": normal_values(splits[3], (D, INNER), INNER ** -0.5, 0.1875),
        "key_blocks": draw_key_blocks(jax.random.fold_in(splits[6], 71), 0),
        "key_count": draw_key_count(jax.random.fold_in(splits[6], 71), 0),
    }


epsilon = 1e-06

def rounded(values):
    return lax.optimization_barrier(values.astype(jnp.bfloat16)).astype(jnp.float32)

def one_sequence(tokens, cotangent, w_qkv, w_out, key_blocks, key_count):
    inner = LOCAL_HEADS * HEAD
    score_scale = HEAD ** (-0.5)
    wide_tokens = tokens.astype(jnp.float32)
    inv_rms = lax.rsqrt(lax.optimization_barrier(jnp.mean(wide_tokens * wide_tokens, axis=1, keepdims=True)) + epsilon)
    normed_wide = wide_tokens * inv_rms
    normed = normed_wide.astype(jnp.bfloat16)
    qkv = jnp.dot(normed, w_qkv, preferred_element_type=jnp.float32).astype(jnp.bfloat16)
    block_shape = (BLOCKS, MASK_BLOCK_SIZE, LOCAL_HEADS, HEAD)
    query = qkv[:, :inner].reshape(block_shape)
    keys = qkv[:, inner:2 * inner].reshape(block_shape)
    values = qkv[:, 2 * inner:].reshape(block_shape)
    slot_ids = jnp.arange(MASK_BLOCKS, dtype=jnp.int32)

    def block_scores(block):
        listed = key_blocks[block]
        active = slot_ids < key_count[block]
        key_rows = keys[listed].astype(jnp.float32)
        scores = jnp.einsum('qhe,mkhe->hqmk', query[block].astype(jnp.float32), key_rows) * score_scale
        return (jnp.where(active[None, None, :, None], scores, -jnp.inf), listed, key_rows)

    def forward_block(block):
        scores, listed, key_rows = block_scores(block)
        running_max = lax.optimization_barrier(jnp.max(scores, axis=(2, 3), keepdims=True))
        log_total = running_max + jnp.log(lax.optimization_barrier(jnp.sum(jnp.exp(scores - running_max), axis=(2, 3), keepdims=True)))
        weights = rounded(jnp.exp(scores - log_total))
        output = jnp.einsum('hqmk,mkhe->qhe', weights, values[listed].astype(jnp.float32))
        return (output.astype(jnp.bfloat16), log_total[:, :, 0, 0])
    attended_blocks, log_totals = lax.map(forward_block, jnp.arange(BLOCKS, dtype=jnp.int32))
    attended = attended_blocks.reshape(SEQ_LEN, inner)
    layer_out = (wide_tokens + jnp.dot(attended, w_out.T, preferred_element_type=jnp.float32)).astype(jnp.bfloat16)
    grad_att = jnp.dot(cotangent, w_out, preferred_element_type=jnp.float32).astype(jnp.bfloat16)
    grad_blocks = grad_att.reshape(block_shape)
    row_delta = lax.optimization_barrier(jnp.sum(grad_blocks.astype(jnp.float32) * attended_blocks.astype(jnp.float32), axis=3))

    def backward_block(carry, block):
        grad_keys, grad_values = carry
        scores, listed, key_rows = block_scores(block)
        probability = jnp.exp(scores - log_totals[block][:, :, None, None])
        weights = rounded(probability)
        grad_rows = grad_blocks[block].astype(jnp.float32)
        value_rows = values[listed].astype(jnp.float32)
        value_part = jnp.einsum('hqmk,qhe->mkhe', weights, grad_rows)
        grad_prob = jnp.einsum('qhe,mkhe->hqmk', grad_rows, value_rows)
        score_gradient = rounded(probability * (grad_prob - row_delta[block].T[:, :, None, None]) * score_scale)
        grad_query = jnp.einsum('hqmk,mkhe->qhe', score_gradient, key_rows).astype(jnp.bfloat16)
        key_part = jnp.einsum('hqmk,qhe->mkhe', score_gradient, query[block].astype(jnp.float32))
        return ((grad_keys.at[listed].add(key_part), grad_values.at[listed].add(value_part)), grad_query)
    empty_grads = jnp.zeros(block_shape, jnp.float32)
    (grad_keys, grad_values), grad_query = lax.scan(backward_block, (empty_grads, empty_grads), jnp.arange(BLOCKS, dtype=jnp.int32))
    grad_qkv = jnp.concatenate([grad_query.reshape(SEQ_LEN, inner), grad_keys.astype(jnp.bfloat16).reshape(SEQ_LEN, inner), grad_values.astype(jnp.bfloat16).reshape(SEQ_LEN, inner)], axis=1)
    grad_normed = jnp.dot(grad_qkv, w_qkv.T, preferred_element_type=jnp.float32)
    branch_choice = inv_rms * (grad_normed - normed_wide * lax.optimization_barrier(jnp.mean(grad_normed * normed_wide, axis=1, keepdims=True)))
    grad_tokens = (cotangent.astype(jnp.float32) + branch_choice).astype(jnp.bfloat16)
    device_runs = (normed.reshape(N_SEQ, TOK_DEV, D), grad_qkv.reshape(N_SEQ, TOK_DEV, 3 * inner), cotangent.reshape(N_SEQ, TOK_DEV, D), attended.reshape(N_SEQ, TOK_DEV, inner))

    def add_run(carry, device_run):
        sum_qkv, sum_out = carry
        run_normed, run_grad, run_upstream, run_attended = device_run
        term_qkv = rounded(jnp.dot(run_normed.T, run_grad, preferred_element_type=jnp.float32))
        term_out = rounded(jnp.dot(run_upstream.T, run_attended, preferred_element_type=jnp.float32))
        return ((sum_qkv + term_qkv, sum_out + term_out), None)
    start_sums = (jnp.zeros((D, 3 * inner), jnp.float32), jnp.zeros((D, inner), jnp.float32))
    (sum_qkv, sum_out), unused = lax.scan(add_run, start_sums, device_runs)
    return (layer_out, grad_tokens, sum_qkv, sum_out)

def reference(tokens, cotangent, w_qkv, w_out, key_blocks, key_count):

    def per_sequence(paired):
        return one_sequence(paired[0], paired[1], w_qkv, w_out, key_blocks, key_count)
    layer_out, grad_tokens, sums_qkv, sums_out = lax.map(per_sequence, (tokens, cotangent))
    factor = 1.0 / math.sqrt(ALL_TOKENS)
    return (layer_out, grad_tokens, lax.optimization_barrier(jnp.sum(sums_qkv, axis=0)) * factor, lax.optimization_barrier(jnp.sum(sums_out, axis=0)) * factor)
```

```python
import math

import jax
import jax.numpy as jnp
from jax import lax
from jax.experimental import pallas as pl
from jax.experimental.pallas import tpu as pltpu
from jax.sharding import PartitionSpec as P

LOCAL_HEADS = 8
HEAD = 128
INNER = LOCAL_HEADS * HEAD
D = 2048
TOK_DEV = 128
N_SEQ = 32
RING = 4
GROUP = 2 * RING
QKV_COLS = 3 * INNER // GROUP
OUT_COLS = INNER // GROUP
ROWS = D // N_SEQ
HALF_ROWS = ROWS // 2
LANES = 128
VMEM_LIMIT = 60 * 1024 * 1024

epsilon = 1e-06

BF16 = jnp.bfloat16
F32 = jnp.float32
CONTRACT_COLUMNS = (((1,), (1,)), ((), ()))
CONTRACT_ROWS = (((0,), (0,)), ((), ()))


def place():
    dp, seq = lax.axis_index("dp"), lax.axis_index("seq")
    return seq % 4, (seq // 4) % 4, (seq // 16) * 2 + dp // 2, dp % 2


def at(x, y, z, c):
    return {"dp": (z % 2) * 2 + c, "seq": (z // 2) * 16 + y * 4 + x}


class Copies:
    def __init__(self, send, recv):
        self.send, self.recv, self.used = send, recv, 0

    def start(self, src, dst, device):
        i = self.used
        self.used += 1
        copy = pltpu.make_async_remote_copy(
            src_ref=src,
            dst_ref=dst,
            send_sem=self.send.at[i],
            recv_sem=self.recv.at[i],
            device_id=device,
            device_id_type=pl.DeviceIdType.MESH,
        )
        copy.start()
        return copy


def meet(peers):
    barrier = pltpu.get_barrier_semaphore()
    for peer in peers:
        pl.semaphore_signal(
            barrier, inc=1, device_id=peer, device_id_type=pl.DeviceIdType.MESH
        )
    pl.semaphore_wait(barrier, len(peers))


def lanes(slot, width=LANES):
    return pl.ds(slot * width, width)


def ring_gather(copies, own, out, up, down, partner, local):
    half = out.shape[0] // 2
    low, high = pl.ds(0, half), pl.ds(half, half)
    stay = pltpu.make_async_copy(own, out.at[:, lanes(0)], local)
    stay.start()
    from_down = copies.start(own, out.at[:, lanes(2)], up)
    from_up = copies.start(own, out.at[:, lanes(6)], down)
    rest = [copies.start(own, out.at[:, lanes(1)], partner)]
    yield
    from_down.wait_recv()
    far_low = copies.start(out.at[low, lanes(2)], out.at[low, lanes(4)], up)
    rest.append(copies.start(out.at[:, lanes(2)], out.at[:, lanes(3)], partner))
    yield
    from_up.wait_recv()
    far_high = copies.start(out.at[high, lanes(6)], out.at[high, lanes(4)], down)
    rest.append(copies.start(out.at[:, lanes(6)], out.at[:, lanes(7)], partner))
    yield
    far_low.wait_recv()
    rest.append(copies.start(out.at[low, lanes(4)], out.at[low, lanes(5)], partner))
    yield
    far_high.wait_recv()
    rest.append(copies.start(out.at[high, lanes(4)], out.at[high, lanes(5)], partner))
    yield
    for copy in rest:
        copy.wait()
    for copy in (from_down, from_up, far_low, far_high):
        copy.wait_send()
    stay.wait()


def side_by_side(*steps):
    steps = list(steps)
    while steps:
        for step in list(steps):
            try:
                next(step)
            except StopIteration:
                steps.remove(step)


def gather_kernel(
    normed_t, upstream_t, kv, all_normed, all_upstream, before, after, send, recv, local
):
    x, y, z, c = place()
    dp, seq = lax.axis_index("dp"), lax.axis_index("seq")
    partner = at(x, y, z, 1 - c)
    z_up, z_down = at(x, y, (z + 1) % 4, c), at(x, y, (z + 3) % 4, c)
    y_up, y_down = at(x, (y + 1) % 4, z, c), at(x, (y + 3) % 4, z, c)
    following = {"dp": dp, "seq": (seq + 1) % N_SEQ}
    preceding = {"dp": dp, "seq": (seq + N_SEQ - 1) % N_SEQ}
    meet([partner, z_up, z_down, y_up, y_down, following, preceding])
    copies = Copies(send, recv)
    halo = [copies.start(kv, before, following), copies.start(kv, after, preceding)]
    side_by_side(
        ring_gather(copies, normed_t, all_normed, z_up, z_down, partner, local.at[0]),
        ring_gather(copies, upstream_t, all_upstream, y_up, y_down, partner, local.at[1]),
    )
    for copy in halo:
        copy.wait()


def vmem_specs(count):
    return [pl.BlockSpec(memory_space=pltpu.VMEM)] * count


def communicating(collective_id):
    return pltpu.CompilerParams(
        collective_id=collective_id, has_side_effects=True, vmem_limit_bytes=VMEM_LIMIT
    )


def gather_inputs(normed_t, upstream_t, kv):
    wide = jax.ShapeDtypeStruct((D, GROUP * TOK_DEV), BF16)
    near = jax.ShapeDtypeStruct(kv.shape, BF16)
    return pl.pallas_call(
        gather_kernel,
        out_shape=(wide, wide, near, near),
        in_specs=vmem_specs(3),
        out_specs=tuple(vmem_specs(4)),
        scratch_shapes=[
            pltpu.SemaphoreType.DMA((20,)),
            pltpu.SemaphoreType.DMA((20,)),
            pltpu.SemaphoreType.DMA((2,)),
        ],
        compiler_params=communicating(0),
        name="gather_inputs",
    )(normed_t, upstream_t, kv)


def attention_kernel(
    query, kv, before, after, grad_att, bias, attended, grad_query, own, to_before, to_after
):
    scale = HEAD ** (-0.5)
    for head in range(LOCAL_HEADS):
        cols = pl.ds(head * HEAD, HEAD)
        value_cols = pl.ds(INNER + head * HEAD, HEAD)
        q, grad = query[:, cols], grad_att[:, cols]
        keys = jnp.concatenate([before[:, cols], kv[:, cols], after[:, cols]], axis=0)
        values = jnp.concatenate(
            [before[:, value_cols], kv[:, value_cols], after[:, value_cols]], axis=0
        )
        scores = lax.dot_general(q, keys, CONTRACT_COLUMNS, preferred_element_type=F32)
        scores = scores * scale + bias[0:1, :]
        raised = jnp.exp(scores - jnp.max(scores, axis=1, keepdims=True))
        probability = raised / jnp.sum(raised, axis=1, keepdims=True)
        weights = probability.astype(BF16)
        output = jnp.dot(weights, values, preferred_element_type=F32).astype(BF16)
        attended[:, cols] = output
        delta = jnp.sum(grad.astype(F32) * output.astype(F32), axis=1, keepdims=True)
        grad_prob = lax.dot_general(grad, values, CONTRACT_COLUMNS, preferred_element_type=F32)
        grad_score = (probability * (grad_prob - delta) * scale).astype(BF16)
        grad_query[:, cols] = jnp.dot(grad_score, keys, preferred_element_type=F32).astype(BF16)
        grad_keys = lax.dot_general(grad_score, q, CONTRACT_ROWS, preferred_element_type=F32)
        grad_values = lax.dot_general(weights, grad, CONTRACT_ROWS, preferred_element_type=F32)
        for where, part in ((cols, grad_keys), (value_cols, grad_values)):
            to_before[:, where] = part[:TOK_DEV].astype(BF16)
            own[:, where] = part[TOK_DEV : 2 * TOK_DEV]
            to_after[:, where] = part[2 * TOK_DEV :].astype(BF16)


def attention(query, kv, before, after, grad_att, bias):
    narrow = jax.ShapeDtypeStruct((TOK_DEV, INNER), BF16)
    pair = (TOK_DEV, 2 * INNER)
    return pl.pallas_call(
        attention_kernel,
        out_shape=(
            narrow,
            narrow,
            jax.ShapeDtypeStruct(pair, F32),
            jax.ShapeDtypeStruct(pair, BF16),
            jax.ShapeDtypeStruct(pair, BF16),
        ),
        in_specs=vmem_specs(6),
        out_specs=tuple(vmem_specs(5)),
        compiler_params=pltpu.CompilerParams(vmem_limit_bytes=VMEM_LIMIT),
        name="attention",
    )(query, kv, before, after, grad_att, bias)


def return_kernel(to_before, to_after, from_after, from_before, send, recv):
    dp, seq = lax.axis_index("dp"), lax.axis_index("seq")
    following = {"dp": dp, "seq": (seq + 1) % N_SEQ}
    preceding = {"dp": dp, "seq": (seq + N_SEQ - 1) % N_SEQ}
    meet([following, preceding])
    copies = Copies(send, recv)
    pair = [
        copies.start(to_before, from_after, preceding),
        copies.start(to_after, from_before, following),
    ]
    for copy in pair:
        copy.wait()


def return_halo(to_before, to_after):
    shape = jax.ShapeDtypeStruct(to_before.shape, BF16)
    return pl.pallas_call(
        return_kernel,
        out_shape=(shape, shape),
        in_specs=vmem_specs(2),
        out_specs=tuple(vmem_specs(2)),
        scratch_shapes=[pltpu.SemaphoreType.DMA((2,)), pltpu.SemaphoreType.DMA((2,))],
        compiler_params=communicating(1),
        name="return_halo",
    )(to_before, to_after)


def added(first, *others):
    total = first.astype(F32)
    for other in others:
        total = total + other.astype(F32)
    return total.astype(BF16)


def weight_kernel(
    all_normed,
    all_upstream,
    grad_qkv,
    attended,
    sum_qkv,
    sum_out,
    grads,
    outs,
    part_qkv,
    part_out,
    x_first,
    y_first,
    z_first,
    x_summed,
    y_summed,
    z_summed,
    then_y,
    then_x,
    then_x_out,
    whole_qkv,
    whole_out,
    send,
    recv,
    local,
):
    x, y, z, c = place()
    z_hi, z_lo = z // 2, z % 2
    steps = range(1, RING)

    def in_z(o, other):
        return (z + o) % 4, (c + other) % 2

    def in_y(o, other):
        return (y + o) % 4, (c + other) % 2

    z_group = [(o, other) for o in range(RING) for other in range(2) if o + other]
    finals = [
        (o, lo, other)
        for o in range(RING)
        for lo in range(2)
        for other in range(2)
        if o + lo + other
    ]
    peers = [at((x + o) % 4, y, z, c) for o in steps]
    peers += [at(x, y, (1 - z_hi) * 2 + lo, core) for lo in range(2) for core in range(2)]
    peers += [
        at(x, (y + o) % 4, z_hi * 2 + (z_lo + lo) % 2, (c + other) % 2)
        for o, lo, other in finals
    ]
    meet(peers)
    copies = Copies(send, recv)

    slice_qkv, slice_out = z * 2 + c, y * 2 + c
    stay = [
        pltpu.make_async_copy(
            grad_qkv.at[:, lanes(slice_qkv, QKV_COLS)], grads.at[pl.ds(0, TOK_DEV)], local.at[0]
        ),
        pltpu.make_async_copy(
            attended.at[:, lanes(slice_out, OUT_COLS)], outs.at[pl.ds(0, TOK_DEV)], local.at[1]
        ),
    ]
    for copy in stay:
        copy.start()
    sent_outs, sent_grads = [], []
    for o, other in z_group:
        to, core = in_z(o, other)
        rows = pl.ds((2 * o + other) * TOK_DEV, TOK_DEV)
        sent_grads.append(
            copies.start(
                grad_qkv.at[:, lanes(to * 2 + core, QKV_COLS)], grads.at[rows], at(x, y, to, core)
            )
        )
        to, core = in_y(o, other)
        sent_outs.append(
            copies.start(
                attended.at[:, lanes(to * 2 + core, OUT_COLS)], outs.at[rows], at(x, to, z, core)
            )
        )
    for copy in stay + sent_outs:
        copy.wait()

    def out_chunk(i, carry):
        rows = pl.ds(pl.multiple_of(i * 256, 256), 256)
        product = jnp.dot(all_upstream[rows, :], outs[...], preferred_element_type=F32)
        part_out[i] = product.astype(BF16).reshape(4, ROWS, OUT_COLS)
        return carry

    lax.fori_loop(0, 8, out_chunk, 0)

    def out_part(to):
        return part_out.at[pl.ds((to // 2) * 4, 4), :, pl.ds((to % 2) * HALF_ROWS, HALF_ROWS)]

    z_sent = [
        copies.start(out_part((z + o) % 4), z_first.at[o - 1], at(x, y, (z + o) % 4, c))
        for o in steps
    ]
    for copy in sent_grads:
        copy.wait()

    def qkv_chunk(i, carry):
        rows = pl.ds(pl.multiple_of(i * 256, 256), 256)
        product = jnp.dot(all_normed[rows, :], grads[...], preferred_element_type=F32)
        part_qkv[i] = product.astype(BF16).reshape(4, ROWS, QKV_COLS)
        return carry

    lax.fori_loop(0, 8, qkv_chunk, 0)
    x_sent, y_sent = [], []
    for o in steps:
        to = (x + o) % 4
        x_sent.append(
            copies.start(part_qkv.at[pl.ds(0, 4), to], x_first.at[o - 1], at(to, y, z, c))
        )
        to = (y + o) % 4
        y_sent.append(copies.start(part_qkv.at[4 + to], y_first.at[o - 1], at(x, to, z, c)))

    for copy in z_sent:
        copy.wait()
    z_summed[...] = added(out_part(z)[...], z_first[0], z_first[1], z_first[2])
    out_sent = [
        copies.start(
            z_summed.at[:, (x + o) % 4], then_x_out.at[o - 1], at((x + o) % 4, y, z, c)
        )
        for o in steps
    ]

    for copy in x_sent:
        copy.wait()
    x_summed[...] = added(part_qkv[0:4, x], x_first[0], x_first[1], x_first[2])
    y_then = [
        copies.start(x_summed.at[(y + o) % 4], then_y.at[o - 1], at(x, (y + o) % 4, z, c))
        for o in steps
    ]
    for copy in y_sent:
        copy.wait()
    y_summed[...] = added(part_qkv[4 + y], y_first[0], y_first[1], y_first[2])
    x_then = [
        copies.start(y_summed.at[(x + o) % 4], then_x.at[o - 1], at((x + o) % 4, y, z, c))
        for o in steps
    ]

    for copy in out_sent:
        copy.wait()
    whole_out[...] = added(z_summed[:, x], then_x_out[0], then_x_out[1], then_x_out[2])
    last = []
    out_place = sum_out.at[pl.ds(z_lo * HALF_ROWS, HALF_ROWS), lanes(slice_out, OUT_COLS)]
    for o, lo, other in finals:
        to, core = in_y(o, other)
        last.append(
            copies.start(
                whole_out.at[to], out_place, at(x, to, z_hi * 2 + (z_lo + lo) % 2, core)
            )
        )
    mine = [pltpu.make_async_copy(whole_out.at[y], out_place, local.at[2])]

    for copy in y_then:
        copy.wait()
    whole_qkv[0] = added(x_summed[y], then_y[0], then_y[1], then_y[2])
    for copy in x_then:
        copy.wait()
    whole_qkv[1] = added(y_summed[x], then_x[0], then_x[1], then_x[2])
    qkv_place = sum_qkv.at[:, lanes(slice_qkv, QKV_COLS)]
    for o, other in z_group:
        to, core = in_z(o, other)
        last.append(copies.start(whole_qkv.at[to // 2], qkv_place, at(x, y, to, core)))
    mine.append(pltpu.make_async_copy(whole_qkv.at[z_hi], qkv_place, local.at[3]))
    for copy in mine:
        copy.start()
    for copy in last + mine:
        copy.wait()


def weight_grads(all_normed, all_upstream, grad_qkv, attended):
    tokens = GROUP * TOK_DEV
    scratch = [
        (tokens, QKV_COLS),
        (tokens, OUT_COLS),
        (8, 4, ROWS, QKV_COLS),
        (8, 4, ROWS, OUT_COLS),
        (3, 4, ROWS, QKV_COLS),
        (3, 4, ROWS, QKV_COLS),
        (3, 4, 4, HALF_ROWS, OUT_COLS),
        (4, ROWS, QKV_COLS),
        (4, ROWS, QKV_COLS),
        (4, 4, HALF_ROWS, OUT_COLS),
        (3, ROWS, QKV_COLS),
        (3, ROWS, QKV_COLS),
        (3, 4, HALF_ROWS, OUT_COLS),
        (2, ROWS, QKV_COLS),
        (4, HALF_ROWS, OUT_COLS),
    ]
    return pl.pallas_call(
        weight_kernel,
        out_shape=(
            jax.ShapeDtypeStruct((ROWS, 3 * INNER), BF16),
            jax.ShapeDtypeStruct((ROWS, INNER), BF16),
        ),
        in_specs=vmem_specs(4),
        out_specs=tuple(vmem_specs(2)),
        scratch_shapes=[pltpu.VMEM(shape, BF16) for shape in scratch]
        + [
            pltpu.SemaphoreType.DMA((54,)),
            pltpu.SemaphoreType.DMA((54,)),
            pltpu.SemaphoreType.DMA((4,)),
        ],
        compiler_params=communicating(2),
        name="weight_grads",
    )(all_normed, all_upstream, grad_qkv, attended)


def key_bias(key_blocks, key_count):
    position = lax.axis_index("seq")
    listed = lax.dynamic_index_in_dim(key_blocks, position, 0, keepdims=True)
    used = lax.broadcasted_iota(jnp.int32, listed.shape, 1) < key_count[position]
    block = position - 1 + lax.broadcasted_iota(jnp.int32, (3, 1), 0)
    attended = jnp.any((listed == block) & used, axis=1)
    bias = jnp.where(attended, 0.0, -jnp.inf).astype(F32)
    return jnp.broadcast_to(bias[:, None], (3, TOK_DEV)).reshape(1, 3 * TOK_DEV)


def body(tokens, cotangent, w_qkv, w_out, key_blocks, key_count):
    seq_devices = lax.axis_size("seq")
    factor = 1.0 / math.sqrt(lax.axis_size("dp") * seq_devices * TOK_DEV)
    wide_tokens = tokens[0].astype(F32)
    upstream = cotangent[0]
    inv_rms = lax.rsqrt(jnp.mean(wide_tokens * wide_tokens, axis=1, keepdims=True) + epsilon)
    normed_wide = wide_tokens * inv_rms
    normed = normed_wide.astype(BF16)
    qkv = jnp.dot(normed, w_qkv, preferred_element_type=F32).astype(BF16)
    query, key_value = qkv[:, :INNER], qkv[:, INNER:]
    grad_att = jnp.dot(upstream, w_out, preferred_element_type=F32).astype(BF16)
    all_normed, all_upstream, before, after = gather_inputs(normed.T, upstream.T, key_value)
    attended, grad_query, own, to_before, to_after = attention(
        query, key_value, before, after, grad_att, key_bias(key_blocks, key_count)
    )
    from_after, from_before = return_halo(to_before, to_after)
    grad_kv = own + from_after.astype(F32) + from_before.astype(F32)
    grad_qkv = jnp.concatenate([grad_query, grad_kv.astype(BF16)], axis=1)
    out_proj = lax.dot_general(attended, w_out, CONTRACT_COLUMNS, preferred_element_type=F32)
    layer_out = (wide_tokens + out_proj).astype(BF16)
    grad_normed = lax.dot_general(grad_qkv, w_qkv, CONTRACT_COLUMNS, preferred_element_type=F32)
    branch = inv_rms * (
        grad_normed - normed_wide * jnp.mean(grad_normed * normed_wide, axis=1, keepdims=True)
    )
    grad_tokens = (upstream.astype(F32) + branch).astype(BF16)
    sum_qkv, sum_out = weight_grads(all_normed, all_upstream, grad_qkv, attended)
    return (
        layer_out[None],
        grad_tokens[None],
        sum_qkv.astype(F32) * factor,
        sum_out.astype(F32) * factor,
    )


def solution(mesh):
    return jax.shard_map(
        body,
        mesh=mesh,
        in_specs=(P("dp", "seq", None), P("dp", "seq", None), P(), P(), P(), P()),
        out_specs=(P("dp", "seq", None), P("dp", "seq", None), P("seq", None), P("seq", None)),
        check_vma=False,
    )
```

```python
import functools
import math

import jax
import jax.numpy as jnp
from jax import lax
from jax.experimental import pallas as pl
from jax.experimental.pallas import tpu as pltpu
from jax.sharding import PartitionSpec as P

LOCAL_HEADS = 8
HEAD = 128
INNER = LOCAL_HEADS * HEAD
D = 2048
TOK_DEV = 128
N_SEQ = 32
RING = 4
GROUP = 2 * RING
WINDOW = 3 * TOK_DEV
ALL_TOK = GROUP * TOK_DEV
ROWS = D // N_SEQ
WIDE = 256
VMEM_LIMIT = 63 * 1024 * 1024

epsilon = 1e-06

BF16 = jnp.bfloat16
F32 = jnp.float32
CONTRACT_COLUMNS = (((1,), (1,)), ((), ()))
CONTRACT_ROWS = (((0,), (0,)), ((), ()))
STEPS = range(1, RING)
Z_GROUP = [(o, other) for o in range(RING) for other in range(2) if o + other]


def place():
    dp, seq = lax.axis_index("dp"), lax.axis_index("seq")
    return seq % 4, (seq // 4) % 4, (seq // 16) * 2 + dp // 2, dp % 2


def at(x, y, z, c):
    return {"dp": (z % 2) * 2 + c, "seq": (z // 2) * 16 + y * 4 + x}


def lanes(slot, width=HEAD):
    start = slot * width
    return pl.ds(start if isinstance(start, int) else pl.multiple_of(start, width), width)


def remote(src, dst, send, recv, device):
    return pltpu.make_async_remote_copy(
        src_ref=src,
        dst_ref=dst,
        send_sem=send,
        recv_sem=recv,
        device_id=device,
        device_id_type=pl.DeviceIdType.MESH,
    )


class Copies:
    def __init__(self, send, recv):
        self.send, self.recv, self.used = send, recv, 0

    def reserve(self, count):
        first = self.used
        self.used += count
        return first

    def start(self, src, dst, device):
        i = self.reserve(1)
        copy = remote(src, dst, self.send.at[i], self.recv.at[i], device)
        copy.start()
        return copy


def wait_all(copies):
    for copy in copies:
        copy.wait()


def signal_all(peers):
    barrier = pltpu.get_barrier_semaphore()
    for peer in peers:
        pl.semaphore_signal(
            barrier, inc=1, device_id=peer, device_id_type=pl.DeviceIdType.MESH
        )


def ring_gather(copies, view, up, down, partner):
    from_down = copies.start(view(0, None), view(2, None), up)
    from_up = copies.start(view(0, None), view(6, None), down)
    rest = [copies.start(view(0, None), view(1, None), partner)]
    yield
    from_down.wait_recv()
    far_low = copies.start(view(2, 0), view(4, 0), up)
    from_up.wait_recv()
    far_high = copies.start(view(6, 1), view(4, 1), down)
    rest.append(copies.start(view(2, None), view(3, None), partner))
    rest.append(copies.start(view(6, None), view(7, None), partner))
    yield
    far_low.wait_recv()
    rest.append(copies.start(view(4, 0), view(5, 0), partner))
    far_high.wait_recv()
    rest.append(copies.start(view(4, 1), view(5, 1), partner))
    yield
    wait_all(rest)
    for copy in (from_down, from_up, far_low, far_high):
        copy.wait_send()
    yield


def added(first, *others):
    total = first.astype(F32)
    for other in others:
        total = total + other.astype(F32)
    return total.astype(BF16)


def layer_kernel(
    tokens_hbm,
    upstream_hbm,
    w_qkv_hbm,
    w_out_hbm,
    key_blocks,
    key_count,
    layer_out,
    grad_tokens,
    sum_a,
    sum_b,
    sum_out,
    tokens,
    upstream,
    w_query,
    w_keys,
    w_values,
    w_out,
    inv_rms,
    normed,
    upstream_t,
    all_normed,
    cot_rows,
    all_attended,
    query,
    kv,
    before,
    after,
    grad_att,
    probability,
    attended,
    grad_query,
    grad_keys,
    grad_values,
    own,
    to_before,
    to_after,
    from_after,
    from_before,
    grad_normed,
    grads_a,
    grads_b,
    part_a,
    part_b,
    part_out,
    x_first_a,
    y_first_a,
    x_first_b,
    y_first_b,
    y_first_out,
    x_summed_a,
    y_summed_a,
    x_summed_b,
    y_summed_b,
    y_summed_out,
    then_y_a,
    then_x_a,
    then_y_b,
    then_x_b,
    then_x_out,
    whole_a,
    whole_b,
    whole_out,
    send,
    recv,
    local,
):
    x, y, z, c = place()
    dp, seq = lax.axis_index("dp"), lax.axis_index("seq")
    z_hi, z_lo = z // 2, z % 2
    mine = z * 2 + c
    following = {"dp": dp, "seq": (seq + 1) % N_SEQ}
    preceding = {"dp": dp, "seq": (seq + N_SEQ - 1) % N_SEQ}
    has_after, has_before = seq < N_SEQ - 1, seq > 0
    scale = HEAD ** (-0.5)
    copies = Copies(send, recv)

    loads = {}
    for i, (name, src, dst) in enumerate(
        [
            ("tokens", tokens_hbm, tokens),
            ("keys", w_qkv_hbm.at[:, pl.ds(INNER, INNER)], w_keys),
            ("values", w_qkv_hbm.at[:, pl.ds(2 * INNER, INNER)], w_values),
            ("upstream", upstream_hbm, upstream),
            ("query", w_qkv_hbm.at[:, pl.ds(0, INNER)], w_query),
            ("out", w_out_hbm, w_out),
        ]
    ):
        loads[name] = pltpu.make_async_copy(src, dst, local.at[i])
        loads[name].start()

    peers = [
        at(x, (y + o) % 4, z_hi * 2 + (z_lo + lo) % 2, (c + other) % 2)
        for o in range(RING)
        for lo in range(2)
        for other in range(2)
        if o + lo + other
    ]
    peers += [at(x, y, (1 - z_hi) * 2 + lo, core) for lo in range(2) for core in range(2)]
    peers += [at((x + o) % 4, y, z, c) for o in STEPS]
    peers += [following, preceding]
    signal_all(peers)

    zero_block = jnp.zeros((TOK_DEV, 2 * INNER), BF16)

    @pl.when(jnp.logical_not(has_before))
    def _():
        before[...] = zero_block
        from_before[...] = zero_block

    @pl.when(jnp.logical_not(has_after))
    def _():
        after[...] = zero_block
        from_after[...] = zero_block

    count = key_count[seq]
    listed = [key_blocks[seq * 3 + j] for j in range(3)]
    biases = []
    for shift in (-1, 0, 1):
        used = jnp.int32(0)
        for j in range(3):
            hit = jnp.where(listed[j] == seq + shift, 1, 0) * jnp.where(j < count, 1, 0)
            used = used + hit
        used = jnp.full((1, TOK_DEV), used, jnp.int32)
        biases.append(jnp.where(used > 0, 0.0, -jnp.inf).astype(F32))
    bias = jnp.concatenate(biases, axis=1)

    loads["tokens"].wait()
    wide_tokens = tokens[...].astype(F32)
    inv_rms[...] = lax.rsqrt(jnp.mean(wide_tokens * wide_tokens, axis=1, keepdims=True) + epsilon)
    normed[...] = (wide_tokens * inv_rms[...]).astype(BF16)

    def project(rows, weight, out, first):
        def chunk(i, carry):
            product = jnp.dot(rows[...], weight[:, lanes(i, WIDE)], preferred_element_type=F32)
            out[:, lanes(i + first, WIDE)] = product.astype(BF16)
            return carry

        lax.fori_loop(0, INNER // WIDE, chunk, 0)

    def halo(i, part):
        cols = pl.ds(part * INNER, INNER)
        return (
            remote(kv.at[:, cols], before.at[:, cols], send.at[i], recv.at[i], following),
            remote(kv.at[:, cols], after.at[:, cols], send.at[i + 1], recv.at[i + 1], preceding),
        )

    halo_at = [copies.reserve(2), copies.reserve(2)]

    def send_halo(part):
        forth, back = halo(halo_at[part], part)

        @pl.when(has_after)
        def _():
            forth.start()

        @pl.when(has_before)
        def _():
            back.start()

    def take_halo(part):
        forth, back = halo(halo_at[part], part)

        @pl.when(has_after)
        def _():
            forth.wait_send()
            back.wait_recv()

        @pl.when(has_before)
        def _():
            back.wait_send()
            forth.wait_recv()

    loads["keys"].wait()
    project(normed, w_keys, kv, 0)
    pl.semaphore_wait(pltpu.get_barrier_semaphore(), len(peers))
    send_halo(0)
    loads["values"].wait()
    project(normed, w_values, kv, INNER // WIDE)
    send_halo(1)

    def turn(rows, out):
        def chunk(i, carry):
            out[pl.ds(pl.multiple_of(i * WIDE, WIDE), WIDE), pl.ds(0, TOK_DEV)] = jnp.transpose(
                rows[:, lanes(i, WIDE)]
            )
            return carry

        lax.fori_loop(0, D // WIDE, chunk, 0)

    partner = at(x, y, z, 1 - c)
    z_up, z_down = at(x, y, (z + 1) % 4, c), at(x, y, (z + 3) % 4, c)

    def in_z(o, other):
        return (z + o) % 4, (c + other) % 2

    def normed_view(slot, part):
        rows = pl.ds(0, D) if part is None else pl.ds(part * (D // 2), D // 2)
        return all_normed.at[rows, lanes(slot)]

    def attended_view(slot, part):
        cols = pl.ds(0, INNER) if part is None else pl.ds(part * (INNER // 2), INNER // 2)
        return all_attended.at[lanes(slot), cols]

    def exchange(src_view, dst_view):
        sent = []
        for o, other in Z_GROUP:
            to, core = in_z(o, other)
            sent.append(
                copies.start(src_view(to * 2 + core), dst_view(2 * o + other), at(x, y, to, core))
            )
        return sent

    turn(normed, all_normed)
    normed_ring = ring_gather(copies, normed_view, z_up, z_down, partner)
    next(normed_ring)
    loads["upstream"].wait()
    turn(upstream, upstream_t)

    def turned(index):
        return upstream_t.at[pl.ds(pl.multiple_of(index * WIDE, WIDE), WIDE), :]

    keep = [pltpu.make_async_copy(turned(mine), cot_rows.at[:, lanes(0)], local.at[6])]
    keep[0].start()
    sent_cot = exchange(turned, lambda slot: cot_rows.at[:, lanes(slot)])
    loads["query"].wait()
    project(normed, w_query, query, 0)
    loads["out"].wait()
    project(upstream, w_out, grad_att, 0)

    def pairs(body):
        def step(i, carry):
            for head in (2 * i, 2 * i + 1):
                body(head)
            return carry

        return step

    def window(cols):
        return jnp.concatenate([before[:, cols], kv[:, cols], after[:, cols]], axis=0)

    def value_cols(head):
        return lanes(head + LOCAL_HEADS)

    def weigh(head):
        cols = lanes(head)
        scores = lax.dot_general(
            query[:, cols], window(cols), CONTRACT_COLUMNS, preferred_element_type=F32
        )
        scores = scores * scale + bias
        raised = jnp.exp(scores - jnp.max(scores, axis=1, keepdims=True))
        probability[head] = raised / jnp.sum(raised, axis=1, keepdims=True)

    def give_back(part, cols):
        to_before[:, cols] = part[:TOK_DEV].astype(BF16)
        own[:, cols] = part[TOK_DEV : 2 * TOK_DEV]
        to_after[:, cols] = part[2 * TOK_DEV :].astype(BF16)

    def attend(head):
        cols = lanes(head)
        weights = probability[head].astype(BF16)
        output = jnp.dot(weights, window(value_cols(head)), preferred_element_type=F32)
        attended[:, cols] = output.astype(BF16)
        part = lax.dot_general(
            weights, grad_att[:, cols], CONTRACT_ROWS, preferred_element_type=F32
        )
        give_back(part, value_cols(head))

    def attend_back(head):
        cols = lanes(head)
        grad = grad_att[:, cols]
        keys = window(cols)
        delta = jnp.sum(
            grad.astype(F32) * attended[:, cols].astype(F32), axis=1, keepdims=True
        )
        grad_prob = lax.dot_general(
            grad, window(value_cols(head)), CONTRACT_COLUMNS, preferred_element_type=F32
        )
        grad_score = (probability[head] * (grad_prob - delta) * scale).astype(BF16)
        grad_query[:, cols] = jnp.dot(grad_score, keys, preferred_element_type=F32).astype(BF16)
        part = lax.dot_general(
            grad_score, query[:, cols], CONTRACT_ROWS, preferred_element_type=F32
        )
        give_back(part, cols)

    pair_count = LOCAL_HEADS // 2
    back_at = copies.reserve(4 * pair_count)

    def returned(i):
        cols = lanes(i, 2 * HEAD)
        down, up = back_at + i, back_at + 2 * pair_count + i
        return (
            remote(
                to_before.at[:, cols], from_after.at[:, cols], send.at[down], recv.at[down], preceding
            ),
            remote(
                to_after.at[:, cols], from_before.at[:, cols], send.at[up], recv.at[up], following
            ),
        )

    def send_back(i):
        down, up = returned(i)

        @pl.when(has_before)
        def _():
            down.start()

        @pl.when(has_after)
        def _():
            up.start()

    def take_back(first):
        @pl.when(has_after)
        def _():
            for i in range(first, first + pair_count):
                down, up = returned(i)
                down.wait_recv()
                up.wait_send()

        @pl.when(has_before)
        def _():
            for i in range(first, first + pair_count):
                down, up = returned(i)
                down.wait_send()
                up.wait_recv()

    def settle(out, first):
        cols = pl.ds(first, INNER)
        out[...] = added(own[:, cols], from_after[:, cols], from_before[:, cols])

    take_halo(0)
    lax.fori_loop(0, pair_count, pairs(weigh), 0)
    take_halo(1)

    def attend_pair(i, carry):
        pairs(attend)(i, carry)
        send_back(i + pair_count)
        return carry

    lax.fori_loop(0, pair_count, attend_pair, 0)
    all_attended[pl.ds(0, TOK_DEV), :] = attended[...]
    next(normed_ring)
    attended_ring = ring_gather(copies, attended_view, z_up, z_down, partner)
    next(attended_ring)

    def back_pair(i, carry):
        pairs(attend_back)(i, carry)
        send_back(i)
        return carry

    lax.fori_loop(0, pair_count, back_pair, 0)

    def swap_columns(src, dst, cols, i):
        stay = pltpu.make_async_copy(
            src.at[:, lanes(mine)], dst.at[pl.ds(0, TOK_DEV), cols], local.at[i]
        )
        stay.start()
        return [stay] + exchange(
            lambda index: src.at[:, lanes(index)], lambda slot: dst.at[lanes(slot), cols]
        )

    sent_query = swap_columns(grad_query, grads_a, pl.ds(0, HEAD), 7)

    def out_chunk(i, carry):
        cols = lanes(i, WIDE)
        rows = pl.ds(pl.multiple_of(i * WIDE, WIDE), WIDE)
        product = lax.dot_general(
            attended[...], w_out[rows, :], CONTRACT_COLUMNS, preferred_element_type=F32
        )
        layer_out[:, cols] = (tokens[:, cols].astype(F32) + product).astype(BF16)
        return carry

    lax.fori_loop(0, D // WIDE, out_chunk, 0)
    next(normed_ring)
    next(attended_ring)

    take_back(pair_count)
    settle(grad_values, INNER)
    sent_values = swap_columns(grad_values, grads_a, pl.ds(HEAD, HEAD), 8)

    def grad_chunk_a(i, carry):
        rows = pl.ds(pl.multiple_of(i * WIDE, WIDE), WIDE)
        grad_normed[:, lanes(i, WIDE)] = lax.dot_general(
            grad_query[...], w_query[rows, :], CONTRACT_COLUMNS, preferred_element_type=F32
        ) + lax.dot_general(
            grad_values[...], w_values[rows, :], CONTRACT_COLUMNS, preferred_element_type=F32
        )
        return carry

    lax.fori_loop(0, D // WIDE, grad_chunk_a, 0)
    take_back(0)
    settle(grad_keys, 0)
    sent_keys = swap_columns(grad_keys, grads_b, pl.ds(0, HEAD), 9)
    next(normed_ring)
    next(attended_ring)

    def multiply(grads, part, width, first):
        def chunk(i, carry):
            rows = pl.ds(pl.multiple_of(i * WIDE, WIDE), WIDE)
            product = jnp.dot(all_normed[rows, :], grads[...], preferred_element_type=F32)
            part[i] = product.astype(BF16).reshape(4, ROWS, width)
            return carry

        lax.fori_loop(first, first + 4, chunk, 0)

    def scatter(grads, part, width, x_first, y_first):
        multiply(grads, part, width, 0)
        x_sent = [
            copies.start(
                part.at[pl.ds(0, 4), (x + o) % 4], x_first.at[o - 1], at((x + o) % 4, y, z, c)
            )
            for o in STEPS
        ]
        multiply(grads, part, width, 4)
        y_sent = [
            copies.start(part.at[4 + (y + o) % 4], y_first.at[o - 1], at(x, (y + o) % 4, z, c))
            for o in STEPS
        ]
        return x_sent, y_sent

    def scatter_on(sent, part, x_first, y_first, x_summed, y_summed, then_y, then_x):
        x_sent, y_sent = sent
        wait_all(x_sent)
        x_summed[...] = added(part[0:4, x], x_first[0], x_first[1], x_first[2])
        y_then = [
            copies.start(x_summed.at[(y + o) % 4], then_y.at[o - 1], at(x, (y + o) % 4, z, c))
            for o in STEPS
        ]
        wait_all(y_sent)
        y_summed[...] = added(part[4 + y], y_first[0], y_first[1], y_first[2])
        x_then = [
            copies.start(y_summed.at[(x + o) % 4], then_x.at[o - 1], at((x + o) % 4, y, z, c))
            for o in STEPS
        ]
        return y_then, x_then

    def gather_sums(sent, x_summed, y_summed, then_y, then_x, whole, out, width, i):
        y_then, x_then = sent
        wait_all(y_then)
        whole[0] = added(x_summed[y], then_y[0], then_y[1], then_y[2])
        wait_all(x_then)
        whole[1] = added(y_summed[x], then_x[0], then_x[1], then_x[2])
        own_place = out.at[:, lanes(mine, width)]
        stay = pltpu.make_async_copy(whole.at[z_hi], own_place, local.at[i])
        stay.start()
        last = [stay]
        for o, other in Z_GROUP:
            to, core = in_z(o, other)
            last.append(copies.start(whole.at[to // 2], own_place, at(x, y, to, core)))
        return last

    wait_all(sent_query + sent_values)
    sent_a = scatter(grads_a, part_a, 2 * HEAD, x_first_a, y_first_a)

    wait_all(keep + sent_cot)
    next(attended_ring)

    def out_part(i, carry):
        cols = lanes(i, WIDE)
        product = jnp.dot(cot_rows[...], all_attended[:, cols], preferred_element_type=F32)
        part_out[:, :, cols] = product.astype(BF16).reshape(4, ROWS, WIDE)
        return carry

    lax.fori_loop(0, INNER // WIDE, out_part, 0)
    y_sent_out = [
        copies.start(
            part_out.at[:, :, lanes((y + o) % 4, WIDE)],
            y_first_out.at[o - 1],
            at(x, (y + o) % 4, z, c),
        )
        for o in STEPS
    ]

    wait_all(sent_keys)
    sent_b = scatter(grads_b, part_b, HEAD, x_first_b, y_first_b)

    def grad_chunk_b(i, total):
        rows, cols = pl.ds(pl.multiple_of(i * WIDE, WIDE), WIDE), lanes(i, WIDE)
        product = grad_normed[:, cols] + lax.dot_general(
            grad_keys[...], w_keys[rows, :], CONTRACT_COLUMNS, preferred_element_type=F32
        )
        grad_normed[:, cols] = product
        along = product * (tokens[:, cols].astype(F32) * inv_rms[...])
        return total + jnp.sum(along, axis=1, keepdims=True)

    total = lax.fori_loop(0, D // WIDE, grad_chunk_b, jnp.zeros((TOK_DEV, 1), F32))
    mean = total * (1.0 / D)

    def tokens_chunk(i, carry):
        cols = lanes(i, WIDE)
        normed_wide = tokens[:, cols].astype(F32) * inv_rms[...]
        branch = inv_rms[...] * (grad_normed[:, cols] - normed_wide * mean)
        grad_tokens[:, cols] = (upstream[:, cols].astype(F32) + branch).astype(BF16)
        return carry

    then_a = scatter_on(
        sent_a, part_a, x_first_a, y_first_a, x_summed_a, y_summed_a, then_y_a, then_x_a
    )
    wait_all(y_sent_out)
    y_summed_out[...] = added(
        part_out[:, :, lanes(y, WIDE)], y_first_out[0], y_first_out[1], y_first_out[2]
    )
    x_then_out = [
        copies.start(
            y_summed_out.at[(x + o) % 4], then_x_out.at[o - 1], at((x + o) % 4, y, z, c)
        )
        for o in STEPS
    ]
    lax.fori_loop(0, D // WIDE, tokens_chunk, 0)
    then_b = scatter_on(
        sent_b, part_b, x_first_b, y_first_b, x_summed_b, y_summed_b, then_y_b, then_x_b
    )
    last = gather_sums(
        then_a, x_summed_a, y_summed_a, then_y_a, then_x_a, whole_a, sum_a, 2 * HEAD, 10
    )

    wait_all(x_then_out)
    whole_out[...] = added(y_summed_out[x], then_x_out[0], then_x_out[1], then_x_out[2])
    final_at = copies.reserve(4)
    owner = 2 * z_lo + c
    holds_own = y == owner
    out_place = sum_out.at[:, lanes(y, WIDE)]
    outgoing = [
        remote(
            whole_out,
            out_place,
            send.at[final_at + 2 * lo + other],
            recv.at[final_at + y],
            at(x, owner, z_hi * 2 + (z_lo + lo) % 2, (c + other) % 2),
        )
        for lo in range(2)
        for other in range(2)
    ]
    for copy in outgoing[1:]:
        copy.start()

    @pl.when(jnp.logical_not(holds_own))
    def _():
        outgoing[0].start()

    @pl.when(holds_own)
    def _():
        stay = pltpu.make_async_copy(whole_out, out_place, local.at[12])
        stay.start()
        stay.wait()

    last += gather_sums(
        then_b, x_summed_b, y_summed_b, then_y_b, then_x_b, whole_b, sum_b, HEAD, 11
    )
    for copy in outgoing[1:]:
        copy.wait_send()

    @pl.when(jnp.logical_not(holds_own))
    def _():
        outgoing[0].wait_send()

    for source in range(RING):
        incoming = remote(
            whole_out,
            sum_out.at[:, lanes(source, WIDE)],
            send.at[final_at],
            recv.at[final_at + source],
            at(x, source, z_hi * 2 + y // 2, y % 2),
        )

        @pl.when(jnp.logical_not(holds_own & (y == source)))
        def _(incoming=incoming):
            incoming.wait_recv()

    wait_all(last)


def whole_layer(tokens, upstream, w_qkv, w_out, key_blocks, key_count):
    pair = (TOK_DEV, 2 * INNER)
    narrow = (TOK_DEV, INNER)
    full = (TOK_DEV, D)
    weight = (D, INNER)
    scratch = [
        (full, BF16),
        (full, BF16),
        (weight, BF16),
        (weight, BF16),
        (weight, BF16),
        (weight, BF16),
        ((TOK_DEV, 1), F32),
        (full, BF16),
        ((D, TOK_DEV), BF16),
        ((D, ALL_TOK), BF16),
        ((WIDE, ALL_TOK), BF16),
        ((ALL_TOK, INNER), BF16),
        (narrow, BF16),
        (pair, BF16),
        (pair, BF16),
        (pair, BF16),
        (narrow, BF16),
        ((LOCAL_HEADS, TOK_DEV, WINDOW), F32),
        (narrow, BF16),
        (narrow, BF16),
        (narrow, BF16),
        (narrow, BF16),
        (pair, F32),
        (pair, BF16),
        (pair, BF16),
        (pair, BF16),
        (pair, BF16),
        (full, F32),
        ((ALL_TOK, 2 * HEAD), BF16),
        ((ALL_TOK, HEAD), BF16),
        ((8, 4, ROWS, 2 * HEAD), BF16),
        ((8, 4, ROWS, HEAD), BF16),
        ((4, ROWS, INNER), BF16),
        ((3, 4, ROWS, 2 * HEAD), BF16),
        ((3, 4, ROWS, 2 * HEAD), BF16),
        ((3, 4, ROWS, HEAD), BF16),
        ((3, 4, ROWS, HEAD), BF16),
        ((3, 4, ROWS, WIDE), BF16),
        ((4, ROWS, 2 * HEAD), BF16),
        ((4, ROWS, 2 * HEAD), BF16),
        ((4, ROWS, HEAD), BF16),
        ((4, ROWS, HEAD), BF16),
        ((4, ROWS, WIDE), BF16),
        ((3, ROWS, 2 * HEAD), BF16),
        ((3, ROWS, 2 * HEAD), BF16),
        ((3, ROWS, HEAD), BF16),
        ((3, ROWS, HEAD), BF16),
        ((3, ROWS, WIDE), BF16),
        ((2, ROWS, 2 * HEAD), BF16),
        ((2, ROWS, HEAD), BF16),
        ((ROWS, WIDE), BF16),
    ]
    semaphores = 130
    anywhere = pl.BlockSpec(memory_space=pl.ANY)
    scalars = pl.BlockSpec(memory_space=pltpu.SMEM)
    vector = pl.BlockSpec(memory_space=pltpu.VMEM)
    return pl.pallas_call(
        layer_kernel,
        out_shape=(
            jax.ShapeDtypeStruct(full, BF16),
            jax.ShapeDtypeStruct(full, BF16),
            jax.ShapeDtypeStruct((ROWS, 2 * INNER), BF16),
            jax.ShapeDtypeStruct((ROWS, INNER), BF16),
            jax.ShapeDtypeStruct((ROWS, INNER), BF16),
        ),
        in_specs=[anywhere] * 4 + [scalars] * 2,
        out_specs=(vector,) * 5,
        scratch_shapes=[pltpu.VMEM(shape, dtype) for shape, dtype in scratch]
        + [
            pltpu.SemaphoreType.DMA((semaphores,)),
            pltpu.SemaphoreType.DMA((semaphores,)),
            pltpu.SemaphoreType.DMA((13,)),
        ],
        compiler_params=pltpu.CompilerParams(
            collective_id=0, has_side_effects=True, vmem_limit_bytes=VMEM_LIMIT
        ),
        name="whole_layer",
    )(tokens, upstream, w_qkv, w_out, key_blocks, key_count)


def finish_kernel(
    factor, layer_in, tokens_in, sum_a, sum_b, sum_out, layer_out, grad_tokens, grad_qkv, grad_out
):
    layer_out[...] = layer_in[...]
    grad_tokens[...] = tokens_in[...]
    for head in range(LOCAL_HEADS):
        cols = lanes(head)
        grad_qkv[:, cols] = sum_a[:, lanes(2 * head)].astype(F32) * factor
        grad_qkv[:, lanes(head + LOCAL_HEADS)] = sum_b[:, cols].astype(F32) * factor
        grad_qkv[:, lanes(head + 2 * LOCAL_HEADS)] = (
            sum_a[:, lanes(2 * head + 1)].astype(F32) * factor
        )
    grad_out[...] = sum_out[...].astype(F32) * factor


def finish(factor, *results):
    full = jax.ShapeDtypeStruct((TOK_DEV, D), BF16)
    vector = pl.BlockSpec(memory_space=pltpu.VMEM)
    return pl.pallas_call(
        functools.partial(finish_kernel, factor),
        out_shape=(
            full,
            full,
            jax.ShapeDtypeStruct((ROWS, 3 * INNER), F32),
            jax.ShapeDtypeStruct((ROWS, INNER), F32),
        ),
        in_specs=[vector] * 5,
        out_specs=(vector,) * 4,
        name="finish",
    )(*results)


def body(tokens, cotangent, w_qkv, w_out, key_blocks, key_count):
    factor = 1.0 / math.sqrt(lax.axis_size("dp") * lax.axis_size("seq") * TOK_DEV)
    results = whole_layer(
        tokens[0], cotangent[0], w_qkv, w_out, key_blocks.reshape(-1), key_count
    )
    layer_out, grad_tokens, grad_w_qkv, grad_w_out = finish(factor, *results)
    return (layer_out[None], grad_tokens[None], grad_w_qkv, grad_w_out)


def solution(mesh):
    return jax.shard_map(
        body,
        mesh=mesh,
        in_specs=(P("dp", "seq", None), P("dp", "seq", None), P(), P(), P(), P()),
        out_specs=(P("dp", "seq", None), P("dp", "seq", None), P("seq", None), P("seq", None)),
        check_vma=False,
    )
```

```python
import functools
import math

import jax
import jax.numpy as jnp
from jax import lax
from jax.experimental import pallas as pl
from jax.experimental.pallas import tpu as pltpu
from jax.sharding import PartitionSpec as P

LOCAL_HEADS = 8
HEAD = 128
INNER = LOCAL_HEADS * HEAD
D = 2048
TOK_DEV = 128
N_SEQ = 32
RING = 4
GROUP = 2 * RING
WINDOW = 3 * TOK_DEV
ALL_TOK = GROUP * TOK_DEV
ROWS = D // N_SEQ
HALF_ROWS = ROWS // 2
WIDE = 256
VMEM_LIMIT = 63 * 1024 * 1024

epsilon = 1e-06

BF16 = jnp.bfloat16
F32 = jnp.float32
CONTRACT_COLUMNS = (((1,), (1,)), ((), ()))
CONTRACT_ROWS = (((0,), (0,)), ((), ()))
STEPS = range(1, RING)
GROUP_STEPS = [(o, other) for o in range(RING) for other in range(2) if o + other]


def place():
    dp, seq = lax.axis_index("dp"), lax.axis_index("seq")
    return seq % 4, (seq // 4) % 4, (seq // 16) * 2 + dp // 2, dp % 2


def at(x, y, z, c):
    return {"dp": (z % 2) * 2 + c, "seq": (z // 2) * 16 + y * 4 + x}


def lanes(slot, width=HEAD):
    start = slot * width
    return pl.ds(start if isinstance(start, int) else pl.multiple_of(start, width), width)


def remote(src, dst, send, recv, device):
    return pltpu.make_async_remote_copy(
        src_ref=src,
        dst_ref=dst,
        send_sem=send,
        recv_sem=recv,
        device_id=device,
        device_id_type=pl.DeviceIdType.MESH,
    )


class Copies:
    def __init__(self, send, recv):
        self.send, self.recv, self.used = send, recv, 0

    def reserve(self, count):
        first = self.used
        self.used += count
        return first

    def start(self, src, dst, device):
        i = self.reserve(1)
        copy = remote(src, dst, self.send.at[i], self.recv.at[i], device)
        copy.start()
        return copy


def wait_all(copies):
    for copy in copies:
        copy.wait()


def signal_all(peers):
    barrier = pltpu.get_barrier_semaphore()
    for peer in peers:
        pl.semaphore_signal(
            barrier, inc=1, device_id=peer, device_id_type=pl.DeviceIdType.MESH
        )


class RingGather:
    def __init__(self, copies, slot, fast, slow, partner):
        self.copies, self.slot = copies, slot
        self.fast, self.slow, self.partner = fast, slow, partner
        self.waits, self.back = [], []

    def start(self, src, dst, device, part=None):
        return self.copies.start(self.slot(src, part), self.slot(dst, part), device)

    def begin(self):
        self.near = self.start(0, 2, self.fast)
        self.waits.append(self.start(0, 1, self.partner))

    def pass_on(self):
        self.near.wait()
        self.far = self.start(2, 4, self.fast)
        self.waits.append(self.start(2, 3, self.partner))

    def begin_slow(self, part):
        self.back.append(self.start(0, 6, self.slow, part))

    def share_far(self):
        self.far.wait()
        self.waits.append(self.start(4, 5, self.partner))

    def share_back(self):
        wait_all(self.back)
        self.waits.append(self.start(6, 7, self.partner))

    def end(self):
        wait_all(self.waits)


def added(first, *others):
    total = first.astype(F32)
    for other in others:
        total = total + other.astype(F32)
    return total.astype(BF16)


def layer_kernel(
    tokens_hbm,
    upstream_hbm,
    w_qkv_hbm,
    w_out_hbm,
    key_blocks,
    key_count,
    layer_out,
    grad_tokens,
    sum_a,
    sum_b,
    sum_out,
    tokens,
    upstream,
    w_query,
    w_keys,
    w_values,
    w_out,
    inv_rms,
    normed,
    upstream_t,
    all_normed,
    cot_rows,
    all_attended,
    query,
    kv,
    before,
    after,
    grad_att,
    probability,
    attended,
    grad_query,
    grad_keys,
    grad_values,
    own,
    to_before,
    to_after,
    from_after,
    from_before,
    grad_normed,
    grads_a,
    grads_b,
    part_a,
    part_b,
    part_out,
    x_first_a,
    z_first_a,
    x_first_b,
    z_first_b,
    y_first_out,
    x_summed_a,
    z_summed_a,
    x_summed_b,
    z_summed_b,
    y_summed_out,
    then_z_a,
    then_x_a,
    then_z_b,
    then_x_b,
    then_x_out,
    whole_a,
    whole_b,
    whole_out,
    send,
    recv,
    local,
):
    x, y, z, c = place()
    dp, seq = lax.axis_index("dp"), lax.axis_index("seq")
    z_hi, z_lo = z // 2, z % 2
    mine = y * 2 + c
    sign = jnp.where(x < 2, -1, 1)
    following = {"dp": dp, "seq": (seq + 1) % N_SEQ}
    preceding = {"dp": dp, "seq": (seq + N_SEQ - 1) % N_SEQ}
    has_after, has_before = seq < N_SEQ - 1, seq > 0
    scale = HEAD ** (-0.5)
    copies = Copies(send, recv)

    loads = {
        name: pltpu.make_async_copy(src, dst, local.at[i])
        for i, (name, src, dst) in enumerate(
            [
                ("tokens", tokens_hbm, tokens),
                ("keys", w_qkv_hbm.at[:, pl.ds(INNER, INNER)], w_keys),
                ("values", w_qkv_hbm.at[:, pl.ds(2 * INNER, INNER)], w_values),
                ("upstream", upstream_hbm, upstream),
                ("query", w_qkv_hbm.at[:, pl.ds(0, INNER)], w_query),
                ("out", w_out_hbm, w_out),
            ]
        )
    }
    loads["tokens"].start()
    loads["keys"].start()

    peers = [
        at(x, (y + o) % 4, z_hi * 2 + (z_lo + lo) % 2, (c + other) % 2)
        for o in range(RING)
        for lo in range(2)
        for other in range(2)
        if o + lo + other
    ]
    peers += [at(x, y, (1 - z_hi) * 2 + lo, core) for lo in range(2) for core in range(2)]
    peers += [at((x + o) % 4, y, z, c) for o in STEPS]
    peers += [following, preceding]
    signal_all(peers)

    zero_block = jnp.zeros((TOK_DEV, 2 * INNER), BF16)

    @pl.when(jnp.logical_not(has_before))
    def _():
        before[...] = zero_block
        from_before[...] = zero_block

    @pl.when(jnp.logical_not(has_after))
    def _():
        after[...] = zero_block
        from_after[...] = zero_block

    count = key_count[seq]
    listed = [key_blocks[seq, j] for j in range(3)]
    biases = []
    for shift in (-1, 0, 1):
        used = jnp.int32(0)
        for j in range(3):
            hit = jnp.where(listed[j] == seq + shift, 1, 0) * jnp.where(j < count, 1, 0)
            used = used + hit
        used = jnp.full((1, TOK_DEV), used, jnp.int32)
        biases.append(jnp.where(used > 0, 0.0, -jnp.inf).astype(F32))
    bias = jnp.concatenate(biases, axis=1)

    loads["tokens"].wait()
    loads["values"].start()
    wide_tokens = tokens[...].astype(F32)
    inv_rms[...] = lax.rsqrt(jnp.mean(wide_tokens * wide_tokens, axis=1, keepdims=True) + epsilon)
    normed[...] = (wide_tokens * inv_rms[...]).astype(BF16)

    def project(rows, weight, out, first):
        def chunk(i, carry):
            product = jnp.dot(rows[...], weight[:, lanes(i, WIDE)], preferred_element_type=F32)
            out[:, lanes(i + first, WIDE)] = product.astype(BF16)
            return carry

        lax.fori_loop(0, INNER // WIDE, chunk, 0)

    def halo(i, part):
        cols = pl.ds(part * INNER, INNER)
        return (
            remote(kv.at[:, cols], before.at[:, cols], send.at[i], recv.at[i], following),
            remote(kv.at[:, cols], after.at[:, cols], send.at[i + 1], recv.at[i + 1], preceding),
        )

    halo_at = [copies.reserve(2), copies.reserve(2)]

    def send_halo(part):
        forth, back = halo(halo_at[part], part)

        @pl.when(has_after)
        def _():
            forth.start()

        @pl.when(has_before)
        def _():
            back.start()

    def take_halo(part):
        forth, back = halo(halo_at[part], part)

        @pl.when(has_after)
        def _():
            forth.wait_send()
            back.wait_recv()

        @pl.when(has_before)
        def _():
            back.wait_send()
            forth.wait_recv()

    def turn(rows, out):
        def chunk(i, carry):
            out[pl.ds(pl.multiple_of(i * WIDE, WIDE), WIDE), pl.ds(0, TOK_DEV)] = jnp.transpose(
                rows[:, lanes(i, WIDE)]
            )
            return carry

        lax.fori_loop(0, D // WIDE, chunk, 0)

    def exchange_y(src_view, dst_view):
        sent = []
        for o, other in GROUP_STEPS:
            to, core = (y + sign * o + 4) % 4, (c + other) % 2
            sent.append(
                copies.start(src_view(to, core), dst_view(2 * o + other), at(x, to, z, core))
            )
        return sent

    def exchange_z(src_view, dst_view):
        sent = []
        for o, other in GROUP_STEPS:
            to, core = (z + o) % 4, (c + other) % 2
            sent.append(
                copies.start(src_view(to, core), dst_view(2 * o + other), at(x, y, to, core))
            )
        return sent

    partner = at(x, y, z, 1 - c)
    fast, slow = at(x, (y + sign + 4) % 4, z, c), at(x, (y - sign + 4) % 4, z, c)

    def normed_slot(slot, part):
        rows = pl.ds(0, D) if part is None else pl.ds(part * (D // 2), D // 2)
        return all_normed.at[rows, lanes(slot)]

    def attended_slot(slot, part):
        cols = pl.ds(0, INNER) if part is None else pl.ds(part * (INNER // 2), INNER // 2)
        return all_attended.at[lanes(slot), cols]

    normed_ring = RingGather(copies, normed_slot, fast, slow, partner)
    attended_ring = RingGather(
        copies,
        attended_slot,
        at(x, y, (z + 1) % 4, c),
        at(x, y, (z + 3) % 4, c),
        partner,
    )

    turn(normed, all_normed)
    pl.semaphore_wait(pltpu.get_barrier_semaphore(), len(peers))
    normed_ring.begin()
    normed_ring.begin_slow(0)
    loads["keys"].wait()
    loads["upstream"].start()
    loads["query"].start()
    project(normed, w_keys, kv, 0)
    send_halo(0)
    loads["values"].wait()
    loads["out"].start()
    project(normed, w_values, kv, INNER // WIDE)
    send_halo(1)
    loads["upstream"].wait()
    turn(upstream, upstream_t)

    def turned(to, core):
        return upstream_t.at[lanes(to * 2 + core, WIDE), :]

    loads["query"].wait()
    project(normed, w_query, query, 0)
    loads["out"].wait()
    project(upstream, w_out, grad_att, 0)

    def pairs(body):
        def step(i, carry):
            for head in (2 * i, 2 * i + 1):
                body(head)
            return carry

        return step

    def window(cols):
        return jnp.concatenate([before[:, cols], kv[:, cols], after[:, cols]], axis=0)

    def value_cols(head):
        return lanes(head + LOCAL_HEADS)

    def weigh(head):
        cols = lanes(head)
        scores = lax.dot_general(
            query[:, cols], window(cols), CONTRACT_COLUMNS, preferred_element_type=F32
        )
        scores = scores * scale + bias
        raised = jnp.exp(scores - jnp.max(scores, axis=1, keepdims=True))
        probability[head] = raised / jnp.sum(raised, axis=1, keepdims=True)

    def give_back(part, cols):
        to_before[:, cols] = part[:TOK_DEV].astype(BF16)
        own[:, cols] = part[TOK_DEV : 2 * TOK_DEV]
        to_after[:, cols] = part[2 * TOK_DEV :].astype(BF16)

    def attend(head):
        cols = lanes(head)
        weights = probability[head].astype(BF16)
        output = jnp.dot(weights, window(value_cols(head)), preferred_element_type=F32)
        attended[:, cols] = output.astype(BF16)
        part = lax.dot_general(
            weights, grad_att[:, cols], CONTRACT_ROWS, preferred_element_type=F32
        )
        give_back(part, value_cols(head))

    def attend_back(head):
        cols = lanes(head)
        grad = grad_att[:, cols]
        keys = window(cols)
        delta = jnp.sum(
            grad.astype(F32) * attended[:, cols].astype(F32), axis=1, keepdims=True
        )
        grad_prob = lax.dot_general(
            grad, window(value_cols(head)), CONTRACT_COLUMNS, preferred_element_type=F32
        )
        grad_score = (probability[head] * (grad_prob - delta) * scale).astype(BF16)
        grad_query[:, cols] = jnp.dot(grad_score, keys, preferred_element_type=F32).astype(BF16)
        part = lax.dot_general(
            grad_score, query[:, cols], CONTRACT_ROWS, preferred_element_type=F32
        )
        give_back(part, cols)

    pair_count = LOCAL_HEADS // 2
    back_at = copies.reserve(4 * pair_count)

    def returned(i):
        cols = lanes(i, 2 * HEAD)
        down, up = back_at + i, back_at + 2 * pair_count + i
        return (
            remote(
                to_before.at[:, cols], from_after.at[:, cols], send.at[down], recv.at[down], preceding
            ),
            remote(
                to_after.at[:, cols], from_before.at[:, cols], send.at[up], recv.at[up], following
            ),
        )

    def send_back(i):
        down, up = returned(i)

        @pl.when(has_before)
        def _():
            down.start()

        @pl.when(has_after)
        def _():
            up.start()

    def take_back(first):
        @pl.when(has_after)
        def _():
            for i in range(first, first + pair_count):
                down, up = returned(i)
                down.wait_recv()
                up.wait_send()

        @pl.when(has_before)
        def _():
            for i in range(first, first + pair_count):
                down, up = returned(i)
                down.wait_send()
                up.wait_recv()

    def settle(out, first):
        cols = pl.ds(first, INNER)
        out[...] = added(own[:, cols], from_after[:, cols], from_before[:, cols])

    take_halo(0)
    lax.fori_loop(0, pair_count, pairs(weigh), 0)
    normed_ring.pass_on()
    take_halo(1)
    normed_ring.begin_slow(1)

    def attend_pair(i, carry):
        pairs(attend)(i, carry)
        send_back(i + pair_count)
        return carry

    lax.fori_loop(0, pair_count, attend_pair, 0)
    all_attended[pl.ds(0, TOK_DEV), :] = attended[...]
    attended_ring.begin()
    attended_ring.begin_slow(None)

    def back_pair(i, carry):
        pairs(attend_back)(i, carry)
        send_back(i)
        return carry

    lax.fori_loop(0, pair_count, back_pair, 0)

    def swap_columns(src, dst, cols, i):
        stay = pltpu.make_async_copy(
            src.at[:, lanes(mine)], dst.at[pl.ds(0, TOK_DEV), cols], local.at[i]
        )
        stay.start()
        return [stay] + exchange_y(
            lambda to, core: src.at[:, lanes(to * 2 + core)],
            lambda slot: dst.at[lanes(slot), cols],
        )

    sent_query = swap_columns(grad_query, grads_a, pl.ds(0, HEAD), 7)

    def out_chunk(i, carry):
        cols = lanes(i, WIDE)
        rows = pl.ds(pl.multiple_of(i * WIDE, WIDE), WIDE)
        product = lax.dot_general(
            attended[...], w_out[rows, :], CONTRACT_COLUMNS, preferred_element_type=F32
        )
        layer_out[:, cols] = (tokens[:, cols].astype(F32) + product).astype(BF16)
        return carry

    lax.fori_loop(0, D // WIDE, out_chunk, 0)
    take_back(pair_count)
    settle(grad_values, INNER)
    sent_values = swap_columns(grad_values, grads_a, pl.ds(HEAD, HEAD), 8)
    attended_ring.pass_on()

    def grad_chunk_a(i, carry):
        rows = pl.ds(pl.multiple_of(i * WIDE, WIDE), WIDE)
        grad_normed[:, lanes(i, WIDE)] = lax.dot_general(
            grad_query[...], w_query[rows, :], CONTRACT_COLUMNS, preferred_element_type=F32
        ) + lax.dot_general(
            grad_values[...], w_values[rows, :], CONTRACT_COLUMNS, preferred_element_type=F32
        )
        return carry

    lax.fori_loop(0, D // WIDE, grad_chunk_a, 0)
    normed_ring.share_far()
    take_back(0)
    settle(grad_keys, 0)
    sent_keys = swap_columns(grad_keys, grads_b, pl.ds(0, HEAD), 9)
    keep = [pltpu.make_async_copy(turned(z, c), cot_rows.at[:, lanes(0)], local.at[6])]
    keep[0].start()
    sent_cot = exchange_z(turned, lambda slot: cot_rows.at[:, lanes(slot)])
    normed_ring.share_back()
    attended_ring.share_back()
    attended_ring.share_far()
    normed_ring.end()

    def multiply(grads, part, width):
        def chunk(i, carry):
            rows = pl.ds(pl.multiple_of(i * WIDE, WIDE), WIDE)
            product = jnp.dot(all_normed[rows, :], grads[...], preferred_element_type=F32)
            part[i // 4, i % 4] = product.astype(BF16).reshape(4, ROWS, width)
            return carry

        lax.fori_loop(0, D // WIDE, chunk, 0)

    def half(lo):
        return pl.ds(pl.multiple_of(lo * HALF_ROWS, HALF_ROWS), HALF_ROWS)

    first_y, last_y = pl.ds(0, 2), pl.ds(2, 2)

    def scatter(grads, part, width, x_first, z_first):
        multiply(grads, part, width)
        x_sent, z_sent = [], []
        for o in STEPS:
            to = (x + o) % 4
            x_sent.append(
                copies.start(part.at[:, first_y, to], x_first.at[o - 1], at(to, y, z, c))
            )
            to = (z + o) % 4
            z_sent.append(
                copies.start(
                    part.at[to // 2, last_y, :, half(to % 2)], z_first.at[o - 1], at(x, y, to, c)
                )
            )
        return x_sent, z_sent

    def scatter_on(sent, part, x_first, z_first, x_summed, z_summed, then_z, then_x):
        x_sent, z_sent = sent
        wait_all(x_sent)
        x_summed[...] = added(part[:, first_y, x], x_first[0], x_first[1], x_first[2])
        z_then = []
        for o in STEPS:
            to = (z + o) % 4
            z_then.append(
                copies.start(
                    x_summed.at[to // 2, :, half(to % 2)], then_z.at[o - 1], at(x, y, to, c)
                )
            )
        wait_all(z_sent)
        z_summed[...] = added(
            part[z_hi, last_y, :, half(z_lo)], z_first[0], z_first[1], z_first[2]
        )
        x_then = [
            copies.start(z_summed.at[:, (x + o) % 4], then_x.at[o - 1], at((x + o) % 4, y, z, c))
            for o in STEPS
        ]
        return z_then, x_then

    finals = [
        (o, lo, other)
        for o in range(RING)
        for lo in range(2)
        for other in range(2)
        if o + lo + other
    ]

    def gather_sums(sent, x_summed, z_summed, then_z, then_x, whole, out, width, i):
        z_then, x_then = sent
        wait_all(z_then)
        whole[first_y] = added(x_summed[z_hi, :, half(z_lo)], then_z[0], then_z[1], then_z[2])
        wait_all(x_then)
        whole[last_y] = added(z_summed[:, x], then_x[0], then_x[1], then_x[2])
        own_place = out.at[half(z_lo), lanes(mine, width)]
        stay = pltpu.make_async_copy(whole.at[y], own_place, local.at[i])
        stay.start()
        last = [stay]
        for o, lo, other in finals:
            to = (y + o) % 4
            device = at(x, to, z_hi * 2 + (z_lo + lo) % 2, (c + other) % 2)
            last.append(copies.start(whole.at[to], own_place, device))
        return last

    wait_all(sent_query + sent_values)
    sent_a = scatter(grads_a, part_a, 2 * HEAD, x_first_a, z_first_a)

    wait_all(sent_keys)
    sent_b = scatter(grads_b, part_b, HEAD, x_first_b, z_first_b)

    def grad_chunk_b(i, total):
        rows, cols = pl.ds(pl.multiple_of(i * WIDE, WIDE), WIDE), lanes(i, WIDE)
        product = grad_normed[:, cols] + lax.dot_general(
            grad_keys[...], w_keys[rows, :], CONTRACT_COLUMNS, preferred_element_type=F32
        )
        grad_normed[:, cols] = product
        along = product * (tokens[:, cols].astype(F32) * inv_rms[...])
        return total + jnp.sum(along, axis=1, keepdims=True)

    total = lax.fori_loop(0, D // WIDE, grad_chunk_b, jnp.zeros((TOK_DEV, 1), F32))
    mean = total * (1.0 / D)

    def tokens_chunk(i, carry):
        cols = lanes(i, WIDE)
        normed_wide = tokens[:, cols].astype(F32) * inv_rms[...]
        branch = inv_rms[...] * (grad_normed[:, cols] - normed_wide * mean)
        grad_tokens[:, cols] = (upstream[:, cols].astype(F32) + branch).astype(BF16)
        return carry

    wait_all(keep + sent_cot)
    attended_ring.end()

    def out_part(i, carry):
        cols = lanes(i, WIDE)
        product = jnp.dot(cot_rows[...], all_attended[:, cols], preferred_element_type=F32)
        part_out[:, :, cols] = product.astype(BF16).reshape(4, ROWS, WIDE)
        return carry

    lax.fori_loop(0, INNER // WIDE, out_part, 0)
    y_sent_out = [
        copies.start(
            part_out.at[:, :, lanes((y + o) % 4, WIDE)],
            y_first_out.at[o - 1],
            at(x, (y + o) % 4, z, c),
        )
        for o in STEPS
    ]
    then_a = scatter_on(
        sent_a, part_a, x_first_a, z_first_a, x_summed_a, z_summed_a, then_z_a, then_x_a
    )
    wait_all(y_sent_out)
    y_summed_out[...] = added(
        part_out[:, :, lanes(y, WIDE)], y_first_out[0], y_first_out[1], y_first_out[2]
    )
    x_then_out = [
        copies.start(
            y_summed_out.at[(x + o) % 4], then_x_out.at[o - 1], at((x + o) % 4, y, z, c)
        )
        for o in STEPS
    ]
    lax.fori_loop(0, D // WIDE, tokens_chunk, 0)
    then_b = scatter_on(
        sent_b, part_b, x_first_b, z_first_b, x_summed_b, z_summed_b, then_z_b, then_x_b
    )
    last = gather_sums(
        then_a, x_summed_a, z_summed_a, then_z_a, then_x_a, whole_a, sum_a, 2 * HEAD, 10
    )

    wait_all(x_then_out)
    whole_out[...] = added(y_summed_out[x], then_x_out[0], then_x_out[1], then_x_out[2])
    final_at = copies.reserve(4)
    owner = 2 * z_lo + c
    holds_own = y == owner
    out_place = sum_out.at[:, lanes(y, WIDE)]
    outgoing = [
        remote(
            whole_out,
            out_place,
            send.at[final_at + 2 * lo + other],
            recv.at[final_at + y],
            at(x, owner, z_hi * 2 + (z_lo + lo) % 2, (c + other) % 2),
        )
        for lo in range(2)
        for other in range(2)
    ]
    for copy in outgoing[1:]:
        copy.start()

    @pl.when(jnp.logical_not(holds_own))
    def _():
        outgoing[0].start()

    @pl.when(holds_own)
    def _():
        stay = pltpu.make_async_copy(whole_out, out_place, local.at[12])
        stay.start()
        stay.wait()

    last += gather_sums(
        then_b, x_summed_b, z_summed_b, then_z_b, then_x_b, whole_b, sum_b, HEAD, 11
    )
    for copy in outgoing[1:]:
        copy.wait_send()

    @pl.when(jnp.logical_not(holds_own))
    def _():
        outgoing[0].wait_send()

    for source in range(RING):
        incoming = remote(
            whole_out,
            sum_out.at[:, lanes(source, WIDE)],
            send.at[final_at],
            recv.at[final_at + source],
            at(x, source, z_hi * 2 + y // 2, y % 2),
        )

        @pl.when(jnp.logical_not(holds_own & (y == source)))
        def _(incoming=incoming):
            incoming.wait_recv()

    wait_all(last)


def whole_layer(tokens, upstream, w_qkv, w_out, key_blocks, key_count):
    pair = (TOK_DEV, 2 * INNER)
    narrow = (TOK_DEV, INNER)
    full = (TOK_DEV, D)
    weight = (D, INNER)
    scratch = [
        (full, BF16),
        (full, BF16),
        (weight, BF16),
        (weight, BF16),
        (weight, BF16),
        (weight, BF16),
        ((TOK_DEV, 1), F32),
        (full, BF16),
        ((D, TOK_DEV), BF16),
        ((D, ALL_TOK), BF16),
        ((WIDE, ALL_TOK), BF16),
        ((ALL_TOK, INNER), BF16),
        (narrow, BF16),
        (pair, BF16),
        (pair, BF16),
        (pair, BF16),
        (narrow, BF16),
        ((LOCAL_HEADS, TOK_DEV, WINDOW), F32),
        (narrow, BF16),
        (narrow, BF16),
        (narrow, BF16),
        (narrow, BF16),
        (pair, F32),
        (pair, BF16),
        (pair, BF16),
        (pair, BF16),
        (pair, BF16),
        (full, F32),
        ((ALL_TOK, 2 * HEAD), BF16),
        ((ALL_TOK, HEAD), BF16),
        ((2, 4, 4, ROWS, 2 * HEAD), BF16),
        ((2, 4, 4, ROWS, HEAD), BF16),
        ((4, ROWS, INNER), BF16),
        ((3, 2, 2, ROWS, 2 * HEAD), BF16),
        ((3, 2, 4, HALF_ROWS, 2 * HEAD), BF16),
        ((3, 2, 2, ROWS, HEAD), BF16),
        ((3, 2, 4, HALF_ROWS, HEAD), BF16),
        ((3, 4, ROWS, WIDE), BF16),
        ((2, 2, ROWS, 2 * HEAD), BF16),
        ((2, 4, HALF_ROWS, 2 * HEAD), BF16),
        ((2, 2, ROWS, HEAD), BF16),
        ((2, 4, HALF_ROWS, HEAD), BF16),
        ((4, ROWS, WIDE), BF16),
        ((3, 2, HALF_ROWS, 2 * HEAD), BF16),
        ((3, 2, HALF_ROWS, 2 * HEAD), BF16),
        ((3, 2, HALF_ROWS, HEAD), BF16),
        ((3, 2, HALF_ROWS, HEAD), BF16),
        ((3, ROWS, WIDE), BF16),
        ((4, HALF_ROWS, 2 * HEAD), BF16),
        ((4, HALF_ROWS, HEAD), BF16),
        ((ROWS, WIDE), BF16),
    ]
    semaphores = 140
    anywhere = pl.BlockSpec(memory_space=pl.ANY)
    scalars = pl.BlockSpec(memory_space=pltpu.SMEM)
    vector = pl.BlockSpec(memory_space=pltpu.VMEM)
    return pl.pallas_call(
        layer_kernel,
        out_shape=(
            jax.ShapeDtypeStruct(full, BF16),
            jax.ShapeDtypeStruct(full, BF16),
            jax.ShapeDtypeStruct((ROWS, 2 * INNER), BF16),
            jax.ShapeDtypeStruct((ROWS, INNER), BF16),
            jax.ShapeDtypeStruct((ROWS, INNER), BF16),
        ),
        in_specs=[anywhere] * 4 + [scalars] * 2,
        out_specs=(vector,) * 5,
        scratch_shapes=[pltpu.VMEM(shape, dtype) for shape, dtype in scratch]
        + [
            pltpu.SemaphoreType.DMA((semaphores,)),
            pltpu.SemaphoreType.DMA((semaphores,)),
            pltpu.SemaphoreType.DMA((13,)),
        ],
        compiler_params=pltpu.CompilerParams(
            collective_id=0, has_side_effects=True, vmem_limit_bytes=VMEM_LIMIT
        ),
        name="whole_layer",
    )(tokens, upstream, w_qkv, w_out, key_blocks, key_count)


def finish_kernel(
    factor, layer_in, tokens_in, sum_a, sum_b, sum_out, layer_out, grad_tokens, grad_qkv, grad_out
):
    layer_out[...] = layer_in[...]
    grad_tokens[...] = tokens_in[...]
    for head in range(LOCAL_HEADS):
        cols = lanes(head)
        grad_qkv[:, cols] = sum_a[:, lanes(2 * head)].astype(F32) * factor
        grad_qkv[:, lanes(head + LOCAL_HEADS)] = sum_b[:, cols].astype(F32) * factor
        grad_qkv[:, lanes(head + 2 * LOCAL_HEADS)] = (
            sum_a[:, lanes(2 * head + 1)].astype(F32) * factor
        )
    grad_out[...] = sum_out[...].astype(F32) * factor


def finish(factor, *results):
    full = jax.ShapeDtypeStruct((TOK_DEV, D), BF16)
    vector = pl.BlockSpec(memory_space=pltpu.VMEM)
    return pl.pallas_call(
        functools.partial(finish_kernel, factor),
        out_shape=(
            full,
            full,
            jax.ShapeDtypeStruct((ROWS, 3 * INNER), F32),
            jax.ShapeDtypeStruct((ROWS, INNER), F32),
        ),
        in_specs=[vector] * 5,
        out_specs=(vector,) * 4,
        name="finish",
    )(*results)


def body(tokens, cotangent, w_qkv, w_out, key_blocks, key_count):
    factor = 1.0 / math.sqrt(lax.axis_size("dp") * lax.axis_size("seq") * TOK_DEV)
    results = whole_layer(
        tokens[0], cotangent[0], w_qkv, w_out, key_blocks, key_count
    )
    layer_out, grad_tokens, grad_w_qkv, grad_w_out = finish(factor, *results)
    return (layer_out[None], grad_tokens[None], grad_w_qkv, grad_w_out)


def solution(mesh):
    return jax.shard_map(
        body,
        mesh=mesh,
        in_specs=(P("dp", "seq", None), P("dp", "seq", None), P(), P(), P(), P()),
        out_specs=(P("dp", "seq", None), P("dp", "seq", None), P("seq", None), P("seq", None)),
        check_vma=False,
    )
```

```python
import functools
import math

import jax
import jax.numpy as jnp
from jax import lax
from jax.experimental import pallas as pl
from jax.experimental.pallas import tpu as pltpu
from jax.sharding import PartitionSpec as P

LOCAL_HEADS = 8
HEAD = 128
INNER = LOCAL_HEADS * HEAD
D = 2048
TOK_DEV = 128
N_SEQ = 32
RING = 4
GROUP = 2 * RING
WINDOW = 3 * TOK_DEV
ALL_TOK = GROUP * TOK_DEV
ROWS = D // N_SEQ
HALF_ROWS = ROWS // 2
WIDE = 256
VMEM_LIMIT = 63 * 1024 * 1024

epsilon = 1e-06

BF16 = jnp.bfloat16
F32 = jnp.float32
CONTRACT_COLUMNS = (((1,), (1,)), ((), ()))
CONTRACT_ROWS = (((0,), (0,)), ((), ()))
STEPS = range(1, RING)
GROUP_STEPS = [(o, other) for o in range(RING) for other in range(2) if o + other]


def place():
    dp, seq = lax.axis_index("dp"), lax.axis_index("seq")
    return seq % 4, (seq // 4) % 4, (seq // 16) * 2 + dp // 2, dp % 2


def at(x, y, z, c):
    return {"dp": (z % 2) * 2 + c, "seq": (z // 2) * 16 + y * 4 + x}


def lanes(slot, width=HEAD):
    start = slot * width
    return pl.ds(start if isinstance(start, int) else pl.multiple_of(start, width), width)


def remote(src, dst, send, recv, device):
    return pltpu.make_async_remote_copy(
        src_ref=src,
        dst_ref=dst,
        send_sem=send,
        recv_sem=recv,
        device_id=device,
        device_id_type=pl.DeviceIdType.MESH,
    )


class Copies:
    def __init__(self, send, recv):
        self.send, self.recv, self.used = send, recv, 0

    def reserve(self, count):
        first = self.used
        self.used += count
        return first

    def start(self, src, dst, device):
        i = self.reserve(1)
        copy = remote(src, dst, self.send.at[i], self.recv.at[i], device)
        copy.start()
        return copy


def wait_all(copies):
    for copy in copies:
        copy.wait()


def signal_all(peers):
    barrier = pltpu.get_barrier_semaphore()
    for peer in peers:
        pl.semaphore_signal(
            barrier, inc=1, device_id=peer, device_id_type=pl.DeviceIdType.MESH
        )


class RingGather:
    def __init__(self, copies, slot, fast, slow, partner):
        self.copies, self.slot = copies, slot
        self.fast, self.slow, self.partner = fast, slow, partner
        self.waits, self.back = [], []

    def start(self, src, dst, device, part=None):
        return self.copies.start(self.slot(src, part), self.slot(dst, part), device)

    def begin(self):
        self.near = self.start(0, 2, self.fast)
        self.waits.append(self.start(0, 1, self.partner))

    def pass_on(self):
        self.near.wait()
        self.far = self.start(2, 4, self.fast)
        self.waits.append(self.start(2, 3, self.partner))

    def begin_slow(self, part):
        self.back.append(self.start(0, 6, self.slow, part))

    def share_far(self):
        self.far.wait()
        self.waits.append(self.start(4, 5, self.partner))

    def share_back(self):
        wait_all(self.back)
        self.waits.append(self.start(6, 7, self.partner))

    def end(self):
        wait_all(self.waits)


def added(first, *others):
    total = first.astype(F32)
    for other in others:
        total = total + other.astype(F32)
    return total.astype(BF16)


def layer_kernel(
    tokens_hbm,
    upstream_hbm,
    w_qkv_hbm,
    w_out_hbm,
    key_blocks,
    key_count,
    layer_out,
    grad_tokens,
    sum_a,
    sum_b,
    sum_out,
    tokens,
    upstream,
    w_query,
    w_keys,
    w_values,
    w_out,
    inv_rms,
    normed,
    upstream_t,
    all_normed,
    cot_rows,
    all_attended,
    query,
    kv,
    before,
    after,
    grad_att,
    probability,
    attended,
    grad_query,
    grad_keys,
    grad_values,
    own,
    to_before,
    to_after,
    from_after,
    from_before,
    grad_normed,
    grads_a,
    grads_b,
    part_a,
    part_b,
    part_out,
    x_first_a,
    z_first_a,
    x_first_b,
    z_first_b,
    y_first_out,
    x_summed_a,
    z_summed_a,
    x_summed_b,
    z_summed_b,
    y_summed_out,
    then_z_a,
    then_x_a,
    then_z_b,
    then_x_b,
    then_x_out,
    whole_a,
    whole_b,
    whole_out,
    send,
    recv,
    local,
):
    x, y, z, c = place()
    dp, seq = lax.axis_index("dp"), lax.axis_index("seq")
    z_hi, z_lo = z // 2, z % 2
    mine = y * 2 + c
    sign = jnp.where(x < 2, -1, 1)
    following = {"dp": dp, "seq": (seq + 1) % N_SEQ}
    preceding = {"dp": dp, "seq": (seq + N_SEQ - 1) % N_SEQ}
    has_after, has_before = seq < N_SEQ - 1, seq > 0
    scale = HEAD ** (-0.5)
    copies = Copies(send, recv)

    loads = {
        name: pltpu.make_async_copy(src, dst, local.at[i])
        for i, (name, src, dst) in enumerate(
            [
                ("tokens", tokens_hbm, tokens),
                ("keys", w_qkv_hbm.at[:, pl.ds(INNER, INNER)], w_keys),
                ("values", w_qkv_hbm.at[:, pl.ds(2 * INNER, INNER)], w_values),
                ("upstream", upstream_hbm, upstream),
                ("query", w_qkv_hbm.at[:, pl.ds(0, INNER)], w_query),
                ("out", w_out_hbm, w_out),
            ]
        )
    }
    loads["tokens"].start()
    loads["keys"].start()

    peers = [
        at(x, (y + o) % 4, z_hi * 2 + (z_lo + lo) % 2, (c + other) % 2)
        for o in range(RING)
        for lo in range(2)
        for other in range(2)
        if o + lo + other
    ]
    peers += [at(x, y, (1 - z_hi) * 2 + lo, core) for lo in range(2) for core in range(2)]
    peers += [at((x + o) % 4, y, z, c) for o in STEPS]
    peers += [following, preceding]
    signal_all(peers)

    zero_block = jnp.zeros((TOK_DEV, 2 * INNER), BF16)

    @pl.when(jnp.logical_not(has_before))
    def _():
        before[...] = zero_block
        from_before[...] = zero_block

    @pl.when(jnp.logical_not(has_after))
    def _():
        after[...] = zero_block
        from_after[...] = zero_block

    count = key_count[seq]
    listed = [key_blocks[j, seq] for j in range(3)]
    biases = []
    for shift in (-1, 0, 1):
        used = jnp.int32(0)
        for j in range(3):
            hit = jnp.where(listed[j] == seq + shift, 1, 0) * jnp.where(j < count, 1, 0)
            used = used + hit
        used = jnp.full((1, TOK_DEV), used, jnp.int32)
        biases.append(jnp.where(used > 0, 0.0, -jnp.inf).astype(F32))
    bias = jnp.concatenate(biases, axis=1)

    loads["tokens"].wait()
    loads["values"].start()
    wide_tokens = tokens[...].astype(F32)
    inv_rms[...] = lax.rsqrt(jnp.mean(wide_tokens * wide_tokens, axis=1, keepdims=True) + epsilon)
    normed[...] = (wide_tokens * inv_rms[...]).astype(BF16)

    def project(rows, weight, out, first):
        def chunk(i, carry):
            product = jnp.dot(rows[...], weight[:, lanes(i, WIDE)], preferred_element_type=F32)
            out[:, lanes(i + first, WIDE)] = product.astype(BF16)
            return carry

        lax.fori_loop(0, INNER // WIDE, chunk, 0)

    def halo(i, part):
        cols = pl.ds(part * INNER, INNER)
        return (
            remote(kv.at[:, cols], before.at[:, cols], send.at[i], recv.at[i], following),
            remote(kv.at[:, cols], after.at[:, cols], send.at[i + 1], recv.at[i + 1], preceding),
        )

    halo_at = [copies.reserve(2), copies.reserve(2)]

    def send_halo(part):
        forth, back = halo(halo_at[part], part)

        @pl.when(has_after)
        def _():
            forth.start()

        @pl.when(has_before)
        def _():
            back.start()

    def take_halo(part):
        forth, back = halo(halo_at[part], part)

        @pl.when(has_after)
        def _():
            forth.wait_send()
            back.wait_recv()

        @pl.when(has_before)
        def _():
            back.wait_send()
            forth.wait_recv()

    def turn(rows, out):
        def chunk(i, carry):
            out[pl.ds(pl.multiple_of(i * WIDE, WIDE), WIDE), pl.ds(0, TOK_DEV)] = jnp.transpose(
                rows[:, lanes(i, WIDE)]
            )
            return carry

        lax.fori_loop(0, D // WIDE, chunk, 0)

    def exchange_y(src_view, dst_view):
        sent = []
        for o, other in GROUP_STEPS:
            to, core = (y + sign * o + 4) % 4, (c + other) % 2
            sent.append(
                copies.start(src_view(to, core), dst_view(2 * o + other), at(x, to, z, core))
            )
        return sent

    def exchange_z(src_view, dst_view):
        sent = []
        for o, other in GROUP_STEPS:
            to, core = (z + o) % 4, (c + other) % 2
            sent.append(
                copies.start(src_view(to, core), dst_view(2 * o + other), at(x, y, to, core))
            )
        return sent

    partner = at(x, y, z, 1 - c)
    fast, slow = at(x, (y + sign + 4) % 4, z, c), at(x, (y - sign + 4) % 4, z, c)

    def normed_slot(slot, part):
        rows = pl.ds(0, D) if part is None else pl.ds(part * (D // 2), D // 2)
        return all_normed.at[rows, lanes(slot)]

    def attended_slot(slot, part):
        cols = pl.ds(0, INNER) if part is None else pl.ds(part * (INNER // 2), INNER // 2)
        return all_attended.at[lanes(slot), cols]

    normed_ring = RingGather(copies, normed_slot, fast, slow, partner)
    attended_ring = RingGather(
        copies,
        attended_slot,
        at(x, y, (z + 1) % 4, c),
        at(x, y, (z + 3) % 4, c),
        partner,
    )

    turn(normed, all_normed)
    pl.semaphore_wait(pltpu.get_barrier_semaphore(), len(peers))
    normed_ring.begin()
    normed_ring.begin_slow(0)
    loads["keys"].wait()
    loads["upstream"].start()
    loads["query"].start()
    project(normed, w_keys, kv, 0)
    send_halo(0)
    loads["values"].wait()
    loads["out"].start()
    project(normed, w_values, kv, INNER // WIDE)
    send_halo(1)
    loads["upstream"].wait()
    turn(upstream, upstream_t)

    def turned(to, core):
        return upstream_t.at[lanes(to * 2 + core, WIDE), :]

    loads["query"].wait()
    project(normed, w_query, query, 0)
    loads["out"].wait()
    project(upstream, w_out, grad_att, 0)

    def pairs(body):
        def step(i, carry):
            for head in (2 * i, 2 * i + 1):
                body(head)
            return carry

        return step

    def window(cols):
        return jnp.concatenate([before[:, cols], kv[:, cols], after[:, cols]], axis=0)

    def value_cols(head):
        return lanes(head + LOCAL_HEADS)

    def weigh(head):
        cols = lanes(head)
        scores = lax.dot_general(
            query[:, cols], window(cols), CONTRACT_COLUMNS, preferred_element_type=F32
        )
        scores = scores * scale + bias
        raised = jnp.exp(scores - jnp.max(scores, axis=1, keepdims=True))
        probability[head] = raised / jnp.sum(raised, axis=1, keepdims=True)

    def give_back(part, cols):
        to_before[:, cols] = part[:TOK_DEV].astype(BF16)
        own[:, cols] = part[TOK_DEV : 2 * TOK_DEV]
        to_after[:, cols] = part[2 * TOK_DEV :].astype(BF16)

    def attend(head):
        cols = lanes(head)
        weights = probability[head].astype(BF16)
        output = jnp.dot(weights, window(value_cols(head)), preferred_element_type=F32)
        attended[:, cols] = output.astype(BF16)
        part = lax.dot_general(
            weights, grad_att[:, cols], CONTRACT_ROWS, preferred_element_type=F32
        )
        give_back(part, value_cols(head))

    def attend_back(head):
        cols = lanes(head)
        grad = grad_att[:, cols]
        keys = window(cols)
        delta = jnp.sum(
            grad.astype(F32) * attended[:, cols].astype(F32), axis=1, keepdims=True
        )
        grad_prob = lax.dot_general(
            grad, window(value_cols(head)), CONTRACT_COLUMNS, preferred_element_type=F32
        )
        grad_score = (probability[head] * (grad_prob - delta) * scale).astype(BF16)
        grad_query[:, cols] = jnp.dot(grad_score, keys, preferred_element_type=F32).astype(BF16)
        part = lax.dot_general(
            grad_score, query[:, cols], CONTRACT_ROWS, preferred_element_type=F32
        )
        give_back(part, cols)

    pair_count = LOCAL_HEADS // 2
    back_at = copies.reserve(4 * pair_count)

    def returned(i):
        cols = lanes(i, 2 * HEAD)
        down, up = back_at + i, back_at + 2 * pair_count + i
        return (
            remote(
                to_before.at[:, cols], from_after.at[:, cols], send.at[down], recv.at[down], preceding
            ),
            remote(
                to_after.at[:, cols], from_before.at[:, cols], send.at[up], recv.at[up], following
            ),
        )

    def send_back(i):
        down, up = returned(i)

        @pl.when(has_before)
        def _():
            down.start()

        @pl.when(has_after)
        def _():
            up.start()

    def take_back(first):
        @pl.when(has_after)
        def _():
            for i in range(first, first + pair_count):
                down, up = returned(i)
                down.wait_recv()
                up.wait_send()

        @pl.when(has_before)
        def _():
            for i in range(first, first + pair_count):
                down, up = returned(i)
                down.wait_send()
                up.wait_recv()

    def settle(out, first):
        cols = pl.ds(first, INNER)
        out[...] = added(own[:, cols], from_after[:, cols], from_before[:, cols])

    take_halo(0)
    lax.fori_loop(0, pair_count, pairs(weigh), 0)
    normed_ring.pass_on()
    take_halo(1)
    normed_ring.begin_slow(1)

    def attend_pair(i, carry):
        pairs(attend)(i, carry)
        send_back(i + pair_count)
        return carry

    lax.fori_loop(0, pair_count, attend_pair, 0)
    all_attended[pl.ds(0, TOK_DEV), :] = attended[...]
    attended_ring.begin()
    attended_ring.begin_slow(None)

    def back_pair(i, carry):
        pairs(attend_back)(i, carry)
        send_back(i)
        return carry

    lax.fori_loop(0, pair_count, back_pair, 0)

    def swap_columns(src, dst, cols, i):
        stay = pltpu.make_async_copy(
            src.at[:, lanes(mine)], dst.at[pl.ds(0, TOK_DEV), cols], local.at[i]
        )
        stay.start()
        return [stay] + exchange_y(
            lambda to, core: src.at[:, lanes(to * 2 + core)],
            lambda slot: dst.at[lanes(slot), cols],
        )

    sent_query = swap_columns(grad_query, grads_a, pl.ds(0, HEAD), 7)

    def out_chunk(i, carry):
        cols = lanes(i, WIDE)
        rows = pl.ds(pl.multiple_of(i * WIDE, WIDE), WIDE)
        product = lax.dot_general(
            attended[...], w_out[rows, :], CONTRACT_COLUMNS, preferred_element_type=F32
        )
        layer_out[:, cols] = (tokens[:, cols].astype(F32) + product).astype(BF16)
        return carry

    lax.fori_loop(0, D // WIDE, out_chunk, 0)
    take_back(pair_count)
    settle(grad_values, INNER)
    sent_values = swap_columns(grad_values, grads_a, pl.ds(HEAD, HEAD), 8)
    attended_ring.pass_on()

    def grad_chunk_a(i, carry):
        rows = pl.ds(pl.multiple_of(i * WIDE, WIDE), WIDE)
        grad_normed[:, lanes(i, WIDE)] = lax.dot_general(
            grad_query[...], w_query[rows, :], CONTRACT_COLUMNS, preferred_element_type=F32
        ) + lax.dot_general(
            grad_values[...], w_values[rows, :], CONTRACT_COLUMNS, preferred_element_type=F32
        )
        return carry

    lax.fori_loop(0, D // WIDE, grad_chunk_a, 0)
    normed_ring.share_far()
    take_back(0)
    settle(grad_keys, 0)
    sent_keys = swap_columns(grad_keys, grads_b, pl.ds(0, HEAD), 9)
    keep = [pltpu.make_async_copy(turned(z, c), cot_rows.at[:, lanes(0)], local.at[6])]
    keep[0].start()
    sent_cot = exchange_z(turned, lambda slot: cot_rows.at[:, lanes(slot)])
    normed_ring.share_back()
    attended_ring.share_back()
    attended_ring.share_far()
    normed_ring.end()

    def multiply(grads, part, width):
        def chunk(i, carry):
            rows = pl.ds(pl.multiple_of(i * WIDE, WIDE), WIDE)
            product = jnp.dot(all_normed[rows, :], grads[...], preferred_element_type=F32)
            part[i // 4, i % 4] = product.astype(BF16).reshape(4, ROWS, width)
            return carry

        lax.fori_loop(0, D // WIDE, chunk, 0)

    def half(lo):
        return pl.ds(pl.multiple_of(lo * HALF_ROWS, HALF_ROWS), HALF_ROWS)

    first_y, last_y = pl.ds(0, 2), pl.ds(2, 2)

    def scatter(grads, part, width, x_first, z_first):
        multiply(grads, part, width)
        x_sent, z_sent = [], []
        for o in STEPS:
            to = (x + o) % 4
            x_sent.append(
                copies.start(part.at[:, first_y, to], x_first.at[o - 1], at(to, y, z, c))
            )
            to = (z + o) % 4
            z_sent.append(
                copies.start(
                    part.at[to // 2, last_y, :, half(to % 2)], z_first.at[o - 1], at(x, y, to, c)
                )
            )
        return x_sent, z_sent

    def scatter_on(sent, part, x_first, z_first, x_summed, z_summed, then_z, then_x):
        x_sent, z_sent = sent
        wait_all(x_sent)
        x_summed[...] = added(part[:, first_y, x], x_first[0], x_first[1], x_first[2])
        z_then = []
        for o in STEPS:
            to = (z + o) % 4
            z_then.append(
                copies.start(
                    x_summed.at[to // 2, :, half(to % 2)], then_z.at[o - 1], at(x, y, to, c)
                )
            )
        wait_all(z_sent)
        z_summed[...] = added(
            part[z_hi, last_y, :, half(z_lo)], z_first[0], z_first[1], z_first[2]
        )
        x_then = [
            copies.start(z_summed.at[:, (x + o) % 4], then_x.at[o - 1], at((x + o) % 4, y, z, c))
            for o in STEPS
        ]
        return z_then, x_then

    finals = [
        (o, lo, other)
        for o in range(RING)
        for lo in range(2)
        for other in range(2)
        if o + lo + other
    ]

    def gather_sums(sent, x_summed, z_summed, then_z, then_x, whole, out, width, i):
        z_then, x_then = sent
        wait_all(z_then)
        whole[first_y] = added(x_summed[z_hi, :, half(z_lo)], then_z[0], then_z[1], then_z[2])
        wait_all(x_then)
        whole[last_y] = added(z_summed[:, x], then_x[0], then_x[1], then_x[2])
        own_place = out.at[half(z_lo), lanes(mine, width)]
        stay = pltpu.make_async_copy(whole.at[y], own_place, local.at[i])
        stay.start()
        last = [stay]
        for o, lo, other in finals:
            to = (y + o) % 4
            device = at(x, to, z_hi * 2 + (z_lo + lo) % 2, (c + other) % 2)
            last.append(copies.start(whole.at[to], own_place, device))
        return last

    wait_all(sent_query + sent_values)
    sent_a = scatter(grads_a, part_a, 2 * HEAD, x_first_a, z_first_a)

    wait_all(sent_keys)
    sent_b = scatter(grads_b, part_b, HEAD, x_first_b, z_first_b)

    def grad_chunk_b(i, total):
        rows, cols = pl.ds(pl.multiple_of(i * WIDE, WIDE), WIDE), lanes(i, WIDE)
        product = grad_normed[:, cols] + lax.dot_general(
            grad_keys[...], w_keys[rows, :], CONTRACT_COLUMNS, preferred_element_type=F32
        )
        grad_normed[:, cols] = product
        along = product * (tokens[:, cols].astype(F32) * inv_rms[...])
        return total + jnp.sum(along, axis=1, keepdims=True)

    total = lax.fori_loop(0, D // WIDE, grad_chunk_b, jnp.zeros((TOK_DEV, 1), F32))
    mean = total * (1.0 / D)

    def tokens_chunk(i, carry):
        cols = lanes(i, WIDE)
        normed_wide = tokens[:, cols].astype(F32) * inv_rms[...]
        branch = inv_rms[...] * (grad_normed[:, cols] - normed_wide * mean)
        grad_tokens[:, cols] = (upstream[:, cols].astype(F32) + branch).astype(BF16)
        return carry

    wait_all(keep + sent_cot)
    attended_ring.end()

    def out_part(i, carry):
        cols = lanes(i, WIDE)
        product = jnp.dot(cot_rows[...], all_attended[:, cols], preferred_element_type=F32)
        part_out[:, :, cols] = product.astype(BF16).reshape(4, ROWS, WIDE)
        return carry

    lax.fori_loop(0, INNER // WIDE, out_part, 0)
    y_sent_out = [
        copies.start(
            part_out.at[:, :, lanes((y + o) % 4, WIDE)],
            y_first_out.at[o - 1],
            at(x, (y + o) % 4, z, c),
        )
        for o in STEPS
    ]
    then_a = scatter_on(
        sent_a, part_a, x_first_a, z_first_a, x_summed_a, z_summed_a, then_z_a, then_x_a
    )
    wait_all(y_sent_out)
    y_summed_out[...] = added(
        part_out[:, :, lanes(y, WIDE)], y_first_out[0], y_first_out[1], y_first_out[2]
    )
    x_then_out = [
        copies.start(
            y_summed_out.at[(x + o) % 4], then_x_out.at[o - 1], at((x + o) % 4, y, z, c)
        )
        for o in STEPS
    ]
    lax.fori_loop(0, D // WIDE, tokens_chunk, 0)
    then_b = scatter_on(
        sent_b, part_b, x_first_b, z_first_b, x_summed_b, z_summed_b, then_z_b, then_x_b
    )
    last = gather_sums(
        then_a, x_summed_a, z_summed_a, then_z_a, then_x_a, whole_a, sum_a, 2 * HEAD, 10
    )

    wait_all(x_then_out)
    whole_out[...] = added(y_summed_out[x], then_x_out[0], then_x_out[1], then_x_out[2])
    final_at = copies.reserve(4)
    owner = 2 * z_lo + c
    holds_own = y == owner
    out_place = sum_out.at[:, lanes(y, WIDE)]
    outgoing = [
        remote(
            whole_out,
            out_place,
            send.at[final_at + 2 * lo + other],
            recv.at[final_at + y],
            at(x, owner, z_hi * 2 + (z_lo + lo) % 2, (c + other) % 2),
        )
        for lo in range(2)
        for other in range(2)
    ]
    for copy in outgoing[1:]:
        copy.start()

    @pl.when(jnp.logical_not(holds_own))
    def _():
        outgoing[0].start()

    @pl.when(holds_own)
    def _():
        stay = pltpu.make_async_copy(whole_out, out_place, local.at[12])
        stay.start()
        stay.wait()

    last += gather_sums(
        then_b, x_summed_b, z_summed_b, then_z_b, then_x_b, whole_b, sum_b, HEAD, 11
    )
    for copy in outgoing[1:]:
        copy.wait_send()

    @pl.when(jnp.logical_not(holds_own))
    def _():
        outgoing[0].wait_send()

    for source in range(RING):
        incoming = remote(
            whole_out,
            sum_out.at[:, lanes(source, WIDE)],
            send.at[final_at],
            recv.at[final_at + source],
            at(x, source, z_hi * 2 + y // 2, y % 2),
        )

        @pl.when(jnp.logical_not(holds_own & (y == source)))
        def _(incoming=incoming):
            incoming.wait_recv()

    wait_all(last)


def whole_layer(tokens, upstream, w_qkv, w_out, key_blocks, key_count):
    pair = (TOK_DEV, 2 * INNER)
    narrow = (TOK_DEV, INNER)
    full = (TOK_DEV, D)
    weight = (D, INNER)
    scratch = [
        (full, BF16),
        (full, BF16),
        (weight, BF16),
        (weight, BF16),
        (weight, BF16),
        (weight, BF16),
        ((TOK_DEV, 1), F32),
        (full, BF16),
        ((D, TOK_DEV), BF16),
        ((D, ALL_TOK), BF16),
        ((WIDE, ALL_TOK), BF16),
        ((ALL_TOK, INNER), BF16),
        (narrow, BF16),
        (pair, BF16),
        (pair, BF16),
        (pair, BF16),
        (narrow, BF16),
        ((LOCAL_HEADS, TOK_DEV, WINDOW), F32),
        (narrow, BF16),
        (narrow, BF16),
        (narrow, BF16),
        (narrow, BF16),
        (pair, F32),
        (pair, BF16),
        (pair, BF16),
        (pair, BF16),
        (pair, BF16),
        (full, F32),
        ((ALL_TOK, 2 * HEAD), BF16),
        ((ALL_TOK, HEAD), BF16),
        ((2, 4, 4, ROWS, 2 * HEAD), BF16),
        ((2, 4, 4, ROWS, HEAD), BF16),
        ((4, ROWS, INNER), BF16),
        ((3, 2, 2, ROWS, 2 * HEAD), BF16),
        ((3, 2, 4, HALF_ROWS, 2 * HEAD), BF16),
        ((3, 2, 2, ROWS, HEAD), BF16),
        ((3, 2, 4, HALF_ROWS, HEAD), BF16),
        ((3, 4, ROWS, WIDE), BF16),
        ((2, 2, ROWS, 2 * HEAD), BF16),
        ((2, 4, HALF_ROWS, 2 * HEAD), BF16),
        ((2, 2, ROWS, HEAD), BF16),
        ((2, 4, HALF_ROWS, HEAD), BF16),
        ((4, ROWS, WIDE), BF16),
        ((3, 2, HALF_ROWS, 2 * HEAD), BF16),
        ((3, 2, HALF_ROWS, 2 * HEAD), BF16),
        ((3, 2, HALF_ROWS, HEAD), BF16),
        ((3, 2, HALF_ROWS, HEAD), BF16),
        ((3, ROWS, WIDE), BF16),
        ((4, HALF_ROWS, 2 * HEAD), BF16),
        ((4, HALF_ROWS, HEAD), BF16),
        ((ROWS, WIDE), BF16),
    ]
    semaphores = 140
    anywhere = pl.BlockSpec(memory_space=pl.ANY)
    scalars = pl.BlockSpec(memory_space=pltpu.SMEM)
    vector = pl.BlockSpec(memory_space=pltpu.VMEM)
    return pl.pallas_call(
        layer_kernel,
        out_shape=(
            jax.ShapeDtypeStruct(full, BF16),
            jax.ShapeDtypeStruct(full, BF16),
            jax.ShapeDtypeStruct((ROWS, 2 * INNER), BF16),
            jax.ShapeDtypeStruct((ROWS, INNER), BF16),
            jax.ShapeDtypeStruct((ROWS, INNER), BF16),
        ),
        in_specs=[anywhere] * 4 + [scalars] * 2,
        out_specs=(vector,) * 5,
        scratch_shapes=[pltpu.VMEM(shape, dtype) for shape, dtype in scratch]
        + [
            pltpu.SemaphoreType.DMA((semaphores,)),
            pltpu.SemaphoreType.DMA((semaphores,)),
            pltpu.SemaphoreType.DMA((13,)),
        ],
        compiler_params=pltpu.CompilerParams(
            collective_id=0, has_side_effects=True, vmem_limit_bytes=VMEM_LIMIT
        ),
        name="whole_layer",
    )(tokens, upstream, w_qkv, w_out, key_blocks, key_count)


def finish_kernel(
    factor, layer_in, tokens_in, sum_a, sum_b, sum_out, layer_out, grad_tokens, grad_qkv, grad_out
):
    layer_out[...] = layer_in[...]
    grad_tokens[...] = tokens_in[...]
    for head in range(LOCAL_HEADS):
        cols = lanes(head)
        grad_qkv[:, cols] = sum_a[:, lanes(2 * head)].astype(F32) * factor
        grad_qkv[:, lanes(head + LOCAL_HEADS)] = sum_b[:, cols].astype(F32) * factor
        grad_qkv[:, lanes(head + 2 * LOCAL_HEADS)] = (
            sum_a[:, lanes(2 * head + 1)].astype(F32) * factor
        )
    grad_out[...] = sum_out[...].astype(F32) * factor


def finish(factor, *results):
    full = jax.ShapeDtypeStruct((TOK_DEV, D), BF16)
    outs = (
        full,
        full,
        jax.ShapeDtypeStruct((ROWS, 3 * INNER), F32),
        jax.ShapeDtypeStruct((ROWS, INNER), F32),
    )
    steps = 2

    def blocks(arrays):
        return tuple(
            pl.BlockSpec((a.shape[0] // steps, a.shape[1]), lambda i: (i, 0)) for a in arrays
        )

    return pl.pallas_call(
        functools.partial(finish_kernel, factor),
        grid=(steps,),
        out_shape=outs,
        in_specs=blocks(results),
        out_specs=blocks(outs),
        name="finish",
    )(*results)


def body(tokens, cotangent, w_qkv, w_out, key_blocks, key_count):
    factor = 1.0 / math.sqrt(lax.axis_size("dp") * lax.axis_size("seq") * TOK_DEV)
    results = whole_layer(
        tokens[0], cotangent[0], w_qkv, w_out, key_blocks.T, key_count
    )
    layer_out, grad_tokens, grad_w_qkv, grad_w_out = finish(factor, *results)
    return (layer_out[None], grad_tokens[None], grad_w_qkv, grad_w_out)


def solution(mesh):
    return jax.shard_map(
        body,
        mesh=mesh,
        in_specs=(P("dp", "seq", None), P("dp", "seq", None), P(), P(), P(), P()),
        out_specs=(P("dp", "seq", None), P("dp", "seq", None), P("seq", None), P("seq", None)),
        check_vma=False,
    )
```

```python
import functools
import math

import jax
import jax.numpy as jnp
from jax import lax
from jax.experimental import pallas as pl
from jax.experimental.pallas import tpu as pltpu
from jax.sharding import PartitionSpec as P

LOCAL_HEADS = 8
HEAD = 128
INNER = LOCAL_HEADS * HEAD
D = 2048
TOK_DEV = 128
N_SEQ = 32
RING = 4
GROUP = 2 * RING
WINDOW = 3 * TOK_DEV
ALL_TOK = GROUP * TOK_DEV
ROWS = D // N_SEQ
HALF_ROWS = ROWS // 2
WIDE = 256
VMEM_LIMIT = 63 * 1024 * 1024

epsilon = 1e-06

BF16 = jnp.bfloat16
F32 = jnp.float32
CONTRACT_COLUMNS = (((1,), (1,)), ((), ()))
CONTRACT_ROWS = (((0,), (0,)), ((), ()))
STEPS = range(1, RING)
GROUP_STEPS = [(o, other) for o in range(RING) for other in range(2) if o + other]


def place():
    dp, seq = lax.axis_index("dp"), lax.axis_index("seq")
    return seq % 4, (seq // 4) % 4, (seq // 16) * 2 + dp // 2, dp % 2


def at(x, y, z, c):
    return {"dp": (z % 2) * 2 + c, "seq": (z // 2) * 16 + y * 4 + x}


def lanes(slot, width=HEAD):
    start = slot * width
    return pl.ds(start if isinstance(start, int) else pl.multiple_of(start, width), width)


def remote(src, dst, send, recv, device):
    return pltpu.make_async_remote_copy(
        src_ref=src,
        dst_ref=dst,
        send_sem=send,
        recv_sem=recv,
        device_id=device,
        device_id_type=pl.DeviceIdType.MESH,
    )


class Copies:
    def __init__(self, send, recv):
        self.send, self.recv, self.used = send, recv, 0

    def reserve(self, count):
        first = self.used
        self.used += count
        return first

    def start(self, src, dst, device):
        i = self.reserve(1)
        copy = remote(src, dst, self.send.at[i], self.recv.at[i], device)
        copy.start()
        return copy


def wait_all(copies):
    for copy in copies:
        copy.wait()


def signal_all(peers):
    barrier = pltpu.get_barrier_semaphore()
    for peer in peers:
        pl.semaphore_signal(
            barrier, inc=1, device_id=peer, device_id_type=pl.DeviceIdType.MESH
        )


class RingGather:
    def __init__(self, copies, slot, fast, slow, partner):
        self.copies, self.slot = copies, slot
        self.fast, self.slow, self.partner = fast, slow, partner
        self.waits, self.back = [], []

    def start(self, src, dst, device, part=None):
        return self.copies.start(self.slot(src, part), self.slot(dst, part), device)

    def begin(self):
        self.near = self.start(0, 2, self.fast)
        self.waits.append(self.start(0, 1, self.partner))

    def pass_on(self):
        self.near.wait()
        self.far = self.start(2, 4, self.fast)
        self.waits.append(self.start(2, 3, self.partner))

    def begin_slow(self, part):
        self.back.append(self.start(0, 6, self.slow, part))

    def share_far(self):
        self.far.wait()
        self.waits.append(self.start(4, 5, self.partner))

    def share_back(self):
        wait_all(self.back)
        self.waits.append(self.start(6, 7, self.partner))

    def end(self):
        wait_all(self.waits)


def added(first, *others):
    total = first.astype(F32)
    for other in others:
        total = total + other.astype(F32)
    return total.astype(BF16)


def layer_kernel(
    tokens_hbm,
    upstream_hbm,
    w_qkv_hbm,
    w_out_hbm,
    key_blocks,
    key_count,
    layer_out,
    grad_tokens,
    sum_a,
    sum_b,
    sum_out,
    tokens,
    upstream,
    w_query,
    w_keys,
    w_values,
    w_out,
    inv_rms,
    normed,
    upstream_t,
    all_normed,
    cot_rows,
    all_attended,
    query,
    kv,
    before,
    after,
    grad_att,
    probability,
    attended,
    grad_query,
    grad_keys,
    grad_values,
    own,
    to_before,
    to_after,
    from_after,
    from_before,
    grad_normed,
    grads_a,
    grads_b,
    part_a,
    part_b,
    part_out,
    x_first_a,
    z_first_a,
    x_first_b,
    z_first_b,
    y_first_out,
    x_summed_a,
    z_summed_a,
    x_summed_b,
    z_summed_b,
    y_summed_out,
    then_z_a,
    then_x_a,
    then_z_b,
    then_x_b,
    then_x_out,
    whole_a,
    whole_b,
    whole_out,
    send,
    recv,
    local,
):
    x, y, z, c = place()
    dp, seq = lax.axis_index("dp"), lax.axis_index("seq")
    z_hi, z_lo = z // 2, z % 2
    mine = y * 2 + c
    sign = jnp.where(x < 2, -1, 1)
    following = {"dp": dp, "seq": (seq + 1) % N_SEQ}
    preceding = {"dp": dp, "seq": (seq + N_SEQ - 1) % N_SEQ}
    has_after, has_before = seq < N_SEQ - 1, seq > 0
    scale = HEAD ** (-0.5)
    copies = Copies(send, recv)

    loads = {
        name: pltpu.make_async_copy(src, dst, local.at[i])
        for i, (name, src, dst) in enumerate(
            [
                ("tokens", tokens_hbm, tokens),
                ("keys", w_qkv_hbm.at[:, pl.ds(INNER, INNER)], w_keys),
                ("values", w_qkv_hbm.at[:, pl.ds(2 * INNER, INNER)], w_values),
                ("upstream", upstream_hbm, upstream),
                ("query", w_qkv_hbm.at[:, pl.ds(0, INNER)], w_query),
                ("out", w_out_hbm, w_out),
            ]
        )
    }
    loads["tokens"].start()
    loads["keys"].start()

    peers = [
        at(x, (y + o) % 4, z_hi * 2 + (z_lo + lo) % 2, (c + other) % 2)
        for o in range(RING)
        for lo in range(2)
        for other in range(2)
        if o + lo + other
    ]
    peers += [at(x, y, (1 - z_hi) * 2 + lo, core) for lo in range(2) for core in range(2)]
    peers += [at((x + o) % 4, y, z, c) for o in STEPS]
    peers += [following, preceding]
    signal_all(peers)

    zero_block = jnp.zeros((TOK_DEV, 2 * INNER), BF16)

    @pl.when(jnp.logical_not(has_before))
    def _():
        before[...] = zero_block
        from_before[...] = zero_block

    @pl.when(jnp.logical_not(has_after))
    def _():
        after[...] = zero_block
        from_after[...] = zero_block

    count = key_count[seq]
    listed = [key_blocks[j, seq] for j in range(3)]
    biases = []
    for shift in (-1, 0, 1):
        used = jnp.int32(0)
        for j in range(3):
            hit = jnp.where(listed[j] == seq + shift, 1, 0) * jnp.where(j < count, 1, 0)
            used = used + hit
        used = jnp.full((1, TOK_DEV), used, jnp.int32)
        biases.append(jnp.where(used > 0, 0.0, -jnp.inf).astype(F32))
    bias = jnp.concatenate(biases, axis=1)

    loads["tokens"].wait()
    wide_tokens = tokens[...].astype(F32)
    inv_rms[...] = lax.rsqrt(jnp.mean(wide_tokens * wide_tokens, axis=1, keepdims=True) + epsilon)
    normed[...] = (wide_tokens * inv_rms[...]).astype(BF16)

    def project(rows, weight, out, first):
        def chunk(i, carry):
            product = jnp.dot(rows[...], weight[:, lanes(i, WIDE)], preferred_element_type=F32)
            out[:, lanes(i + first, WIDE)] = product.astype(BF16)
            return carry

        lax.fori_loop(0, INNER // WIDE, chunk, 0)

    def halo(i, part):
        cols = pl.ds(part * INNER, INNER)
        return (
            remote(kv.at[:, cols], before.at[:, cols], send.at[i], recv.at[i], following),
            remote(kv.at[:, cols], after.at[:, cols], send.at[i + 1], recv.at[i + 1], preceding),
        )

    halo_at = [copies.reserve(2), copies.reserve(2)]

    def send_halo(part):
        forth, back = halo(halo_at[part], part)

        @pl.when(has_after)
        def _():
            forth.start()

        @pl.when(has_before)
        def _():
            back.start()

    def take_halo(part):
        forth, back = halo(halo_at[part], part)

        @pl.when(has_after)
        def _():
            forth.wait_send()
            back.wait_recv()

        @pl.when(has_before)
        def _():
            back.wait_send()
            forth.wait_recv()

    def turn(rows, out):
        def chunk(i, carry):
            out[pl.ds(pl.multiple_of(i * WIDE, WIDE), WIDE), pl.ds(0, TOK_DEV)] = jnp.transpose(
                rows[:, lanes(i, WIDE)]
            )
            return carry

        lax.fori_loop(0, D // WIDE, chunk, 0)

    def exchange_y(src_view, dst_view):
        sent = []
        for o, other in GROUP_STEPS:
            to, core = (y + sign * o + 4) % 4, (c + other) % 2
            sent.append(
                copies.start(src_view(to, core), dst_view(2 * o + other), at(x, to, z, core))
            )
        return sent

    def exchange_z(src_view, dst_view):
        sent = []
        for o, other in GROUP_STEPS:
            to, core = (z + o) % 4, (c + other) % 2
            sent.append(
                copies.start(src_view(to, core), dst_view(2 * o + other), at(x, y, to, core))
            )
        return sent

    partner = at(x, y, z, 1 - c)
    fast, slow = at(x, (y + sign + 4) % 4, z, c), at(x, (y - sign + 4) % 4, z, c)

    def normed_slot(slot, part):
        rows = pl.ds(0, D) if part is None else pl.ds(part * (D // 2), D // 2)
        return all_normed.at[rows, lanes(slot)]

    def attended_slot(slot, part):
        cols = pl.ds(0, INNER) if part is None else pl.ds(part * (INNER // 2), INNER // 2)
        return all_attended.at[lanes(slot), cols]

    normed_ring = RingGather(copies, normed_slot, fast, slow, partner)
    attended_ring = RingGather(
        copies,
        attended_slot,
        at(x, y, (z + 1) % 4, c),
        at(x, y, (z + 3) % 4, c),
        partner,
    )

    turn(normed, all_normed)
    pl.semaphore_wait(pltpu.get_barrier_semaphore(), len(peers))
    normed_ring.begin()
    normed_ring.begin_slow(0)
    loads["keys"].wait()
    loads["values"].start()
    loads["upstream"].start()
    project(normed, w_keys, kv, 0)
    send_halo(0)
    loads["values"].wait()
    loads["query"].start()
    loads["out"].start()
    project(normed, w_values, kv, INNER // WIDE)
    send_halo(1)
    loads["upstream"].wait()
    turn(upstream, upstream_t)

    def turned(to, core):
        return upstream_t.at[lanes(to * 2 + core, WIDE), :]

    loads["query"].wait()
    project(normed, w_query, query, 0)
    loads["out"].wait()
    project(upstream, w_out, grad_att, 0)

    def pairs(body):
        def step(i, carry):
            for head in (2 * i, 2 * i + 1):
                body(head)
            return carry

        return step

    def window(cols):
        return jnp.concatenate([before[:, cols], kv[:, cols], after[:, cols]], axis=0)

    def value_cols(head):
        return lanes(head + LOCAL_HEADS)

    def weigh(head):
        cols = lanes(head)
        scores = lax.dot_general(
            query[:, cols], window(cols), CONTRACT_COLUMNS, preferred_element_type=F32
        )
        scores = scores * scale + bias
        raised = jnp.exp(scores - jnp.max(scores, axis=1, keepdims=True))
        probability[head] = raised / jnp.sum(raised, axis=1, keepdims=True)

    def give_back(part, cols):
        to_before[:, cols] = part[:TOK_DEV].astype(BF16)
        own[:, cols] = part[TOK_DEV : 2 * TOK_DEV]
        to_after[:, cols] = part[2 * TOK_DEV :].astype(BF16)

    def attend(head):
        cols = lanes(head)
        weights = probability[head].astype(BF16)
        output = jnp.dot(weights, window(value_cols(head)), preferred_element_type=F32)
        attended[:, cols] = output.astype(BF16)
        part = lax.dot_general(
            weights, grad_att[:, cols], CONTRACT_ROWS, preferred_element_type=F32
        )
        give_back(part, value_cols(head))

    def attend_back(head):
        cols = lanes(head)
        grad = grad_att[:, cols]
        keys = window(cols)
        delta = jnp.sum(
            grad.astype(F32) * attended[:, cols].astype(F32), axis=1, keepdims=True
        )
        grad_prob = lax.dot_general(
            grad, window(value_cols(head)), CONTRACT_COLUMNS, preferred_element_type=F32
        )
        grad_score = (probability[head] * (grad_prob - delta) * scale).astype(BF16)
        grad_query[:, cols] = jnp.dot(grad_score, keys, preferred_element_type=F32).astype(BF16)
        part = lax.dot_general(
            grad_score, query[:, cols], CONTRACT_ROWS, preferred_element_type=F32
        )
        give_back(part, cols)

    pair_count = LOCAL_HEADS // 2
    back_at = copies.reserve(4 * pair_count)

    def returned(i):
        cols = lanes(i, 2 * HEAD)
        down, up = back_at + i, back_at + 2 * pair_count + i
        return (
            remote(
                to_before.at[:, cols], from_after.at[:, cols], send.at[down], recv.at[down], preceding
            ),
            remote(
                to_after.at[:, cols], from_before.at[:, cols], send.at[up], recv.at[up], following
            ),
        )

    def send_back(i):
        down, up = returned(i)

        @pl.when(has_before)
        def _():
            down.start()

        @pl.when(has_after)
        def _():
            up.start()

    def take_back(first):
        @pl.when(has_after)
        def _():
            for i in range(first, first + pair_count):
                down, up = returned(i)
                down.wait_recv()
                up.wait_send()

        @pl.when(has_before)
        def _():
            for i in range(first, first + pair_count):
                down, up = returned(i)
                down.wait_send()
                up.wait_recv()

    def settle(out, first):
        cols = pl.ds(first, INNER)
        out[...] = added(own[:, cols], from_after[:, cols], from_before[:, cols])

    take_halo(0)
    lax.fori_loop(0, pair_count, pairs(weigh), 0)
    normed_ring.pass_on()
    take_halo(1)
    normed_ring.begin_slow(1)

    def attend_pair(i, carry):
        pairs(attend)(i, carry)
        send_back(i + pair_count)
        return carry

    lax.fori_loop(0, pair_count, attend_pair, 0)
    all_attended[pl.ds(0, TOK_DEV), :] = attended[...]
    attended_ring.begin()
    attended_ring.begin_slow(None)

    def back_pair(i, carry):
        pairs(attend_back)(i, carry)
        send_back(i)
        return carry

    lax.fori_loop(0, pair_count, back_pair, 0)

    def swap_columns(src, dst, cols, i):
        stay = pltpu.make_async_copy(
            src.at[:, lanes(mine)], dst.at[pl.ds(0, TOK_DEV), cols], local.at[i]
        )
        stay.start()
        return [stay] + exchange_y(
            lambda to, core: src.at[:, lanes(to * 2 + core)],
            lambda slot: dst.at[lanes(slot), cols],
        )

    sent_query = swap_columns(grad_query, grads_a, pl.ds(0, HEAD), 7)

    def out_chunk(i, carry):
        cols = lanes(i, WIDE)
        rows = pl.ds(pl.multiple_of(i * WIDE, WIDE), WIDE)
        product = lax.dot_general(
            attended[...], w_out[rows, :], CONTRACT_COLUMNS, preferred_element_type=F32
        )
        layer_out[:, cols] = (tokens[:, cols].astype(F32) + product).astype(BF16)
        return carry

    lax.fori_loop(0, D // WIDE, out_chunk, 0)
    take_back(pair_count)
    settle(grad_values, INNER)
    sent_values = swap_columns(grad_values, grads_a, pl.ds(HEAD, HEAD), 8)
    attended_ring.pass_on()

    def grad_chunk_a(i, carry):
        rows = pl.ds(pl.multiple_of(i * WIDE, WIDE), WIDE)
        grad_normed[:, lanes(i, WIDE)] = lax.dot_general(
            grad_query[...], w_query[rows, :], CONTRACT_COLUMNS, preferred_element_type=F32
        ) + lax.dot_general(
            grad_values[...], w_values[rows, :], CONTRACT_COLUMNS, preferred_element_type=F32
        )
        return carry

    lax.fori_loop(0, D // WIDE, grad_chunk_a, 0)
    normed_ring.share_far()
    take_back(0)
    settle(grad_keys, 0)
    sent_keys = swap_columns(grad_keys, grads_b, pl.ds(0, HEAD), 9)
    keep = [pltpu.make_async_copy(turned(z, c), cot_rows.at[:, lanes(0)], local.at[6])]
    keep[0].start()
    sent_cot = exchange_z(turned, lambda slot: cot_rows.at[:, lanes(slot)])
    normed_ring.share_back()
    attended_ring.share_back()
    attended_ring.share_far()
    normed_ring.end()

    def multiply(grads, part, width):
        def chunk(i, carry):
            rows = pl.ds(pl.multiple_of(i * WIDE, WIDE), WIDE)
            product = jnp.dot(all_normed[rows, :], grads[...], preferred_element_type=F32)
            part[i // 4, i % 4] = product.astype(BF16).reshape(4, ROWS, width)
            return carry

        lax.fori_loop(0, D // WIDE, chunk, 0)

    def half(lo):
        return pl.ds(pl.multiple_of(lo * HALF_ROWS, HALF_ROWS), HALF_ROWS)

    first_y, last_y = pl.ds(0, 2), pl.ds(2, 2)

    def scatter(grads, part, width, x_first, z_first):
        multiply(grads, part, width)
        x_sent, z_sent = [], []
        for o in STEPS:
            to = (x + o) % 4
            x_sent.append(
                copies.start(part.at[:, first_y, to], x_first.at[o - 1], at(to, y, z, c))
            )
            to = (z + o) % 4
            z_sent.append(
                copies.start(
                    part.at[to // 2, last_y, :, half(to % 2)], z_first.at[o - 1], at(x, y, to, c)
                )
            )
        return x_sent, z_sent

    def scatter_on(sent, part, x_first, z_first, x_summed, z_summed, then_z, then_x):
        x_sent, z_sent = sent
        wait_all(x_sent)
        x_summed[...] = added(part[:, first_y, x], x_first[0], x_first[1], x_first[2])
        z_then = []
        for o in STEPS:
            to = (z + o) % 4
            z_then.append(
                copies.start(
                    x_summed.at[to // 2, :, half(to % 2)], then_z.at[o - 1], at(x, y, to, c)
                )
            )
        wait_all(z_sent)
        z_summed[...] = added(
            part[z_hi, last_y, :, half(z_lo)], z_first[0], z_first[1], z_first[2]
        )
        x_then = [
            copies.start(z_summed.at[:, (x + o) % 4], then_x.at[o - 1], at((x + o) % 4, y, z, c))
            for o in STEPS
        ]
        return z_then, x_then

    finals = [
        (o, lo, other)
        for o in range(RING)
        for lo in range(2)
        for other in range(2)
        if o + lo + other
    ]

    def gather_sums(sent, x_summed, z_summed, then_z, then_x, whole, out, width, i):
        z_then, x_then = sent
        wait_all(z_then)
        whole[first_y] = added(x_summed[z_hi, :, half(z_lo)], then_z[0], then_z[1], then_z[2])
        wait_all(x_then)
        whole[last_y] = added(z_summed[:, x], then_x[0], then_x[1], then_x[2])
        own_place = out.at[half(z_lo), lanes(mine, width)]
        stay = pltpu.make_async_copy(whole.at[y], own_place, local.at[i])
        stay.start()
        last = [stay]
        for o, lo, other in finals:
            to = (y + o) % 4
            device = at(x, to, z_hi * 2 + (z_lo + lo) % 2, (c + other) % 2)
            last.append(copies.start(whole.at[to], own_place, device))
        return last

    wait_all(sent_query + sent_values)
    sent_a = scatter(grads_a, part_a, 2 * HEAD, x_first_a, z_first_a)

    wait_all(sent_keys)
    sent_b = scatter(grads_b, part_b, HEAD, x_first_b, z_first_b)

    def grad_chunk_b(i, total):
        rows, cols = pl.ds(pl.multiple_of(i * WIDE, WIDE), WIDE), lanes(i, WIDE)
        product = grad_normed[:, cols] + lax.dot_general(
            grad_keys[...], w_keys[rows, :], CONTRACT_COLUMNS, preferred_element_type=F32
        )
        grad_normed[:, cols] = product
        along = product * (tokens[:, cols].astype(F32) * inv_rms[...])
        return total + jnp.sum(along, axis=1, keepdims=True)

    total = lax.fori_loop(0, D // WIDE, grad_chunk_b, jnp.zeros((TOK_DEV, 1), F32))
    mean = total * (1.0 / D)

    def tokens_chunk(i, carry):
        cols = lanes(i, WIDE)
        normed_wide = tokens[:, cols].astype(F32) * inv_rms[...]
        branch = inv_rms[...] * (grad_normed[:, cols] - normed_wide * mean)
        grad_tokens[:, cols] = (upstream[:, cols].astype(F32) + branch).astype(BF16)
        return carry

    wait_all(keep + sent_cot)
    attended_ring.end()

    def out_part(i, carry):
        cols = lanes(i, WIDE)
        product = jnp.dot(cot_rows[...], all_attended[:, cols], preferred_element_type=F32)
        part_out[:, :, cols] = product.astype(BF16).reshape(4, ROWS, WIDE)
        return carry

    lax.fori_loop(0, INNER // WIDE, out_part, 0)
    y_sent_out = [
        copies.start(
            part_out.at[:, :, lanes((y + o) % 4, WIDE)],
            y_first_out.at[o - 1],
            at(x, (y + o) % 4, z, c),
        )
        for o in STEPS
    ]
    then_a = scatter_on(
        sent_a, part_a, x_first_a, z_first_a, x_summed_a, z_summed_a, then_z_a, then_x_a
    )
    wait_all(y_sent_out)
    y_summed_out[...] = added(
        part_out[:, :, lanes(y, WIDE)], y_first_out[0], y_first_out[1], y_first_out[2]
    )
    x_then_out = [
        copies.start(
            y_summed_out.at[(x + o) % 4], then_x_out.at[o - 1], at((x + o) % 4, y, z, c)
        )
        for o in STEPS
    ]
    lax.fori_loop(0, D // WIDE, tokens_chunk, 0)
    then_b = scatter_on(
        sent_b, part_b, x_first_b, z_first_b, x_summed_b, z_summed_b, then_z_b, then_x_b
    )
    last = gather_sums(
        then_a, x_summed_a, z_summed_a, then_z_a, then_x_a, whole_a, sum_a, 2 * HEAD, 10
    )

    wait_all(x_then_out)
    whole_out[...] = added(y_summed_out[x], then_x_out[0], then_x_out[1], then_x_out[2])
    final_at = copies.reserve(4)
    owner = 2 * z_lo + c
    holds_own = y == owner
    out_place = sum_out.at[:, lanes(y, WIDE)]
    outgoing = [
        remote(
            whole_out,
            out_place,
            send.at[final_at + 2 * lo + other],
            recv.at[final_at + y],
            at(x, owner, z_hi * 2 + (z_lo + lo) % 2, (c + other) % 2),
        )
        for lo in range(2)
        for other in range(2)
    ]
    for copy in outgoing[1:]:
        copy.start()

    @pl.when(jnp.logical_not(holds_own))
    def _():
        outgoing[0].start()

    @pl.when(holds_own)
    def _():
        stay = pltpu.make_async_copy(whole_out, out_place, local.at[12])
        stay.start()
        stay.wait()

    last += gather_sums(
        then_b, x_summed_b, z_summed_b, then_z_b, then_x_b, whole_b, sum_b, HEAD, 11
    )
    for copy in outgoing[1:]:
        copy.wait_send()

    @pl.when(jnp.logical_not(holds_own))
    def _():
        outgoing[0].wait_send()

    for source in range(RING):
        incoming = remote(
            whole_out,
            sum_out.at[:, lanes(source, WIDE)],
            send.at[final_at],
            recv.at[final_at + source],
            at(x, source, z_hi * 2 + y // 2, y % 2),
        )

        @pl.when(jnp.logical_not(holds_own & (y == source)))
        def _(incoming=incoming):
            incoming.wait_recv()

    wait_all(last)


def whole_layer(tokens, upstream, w_qkv, w_out, key_blocks, key_count):
    pair = (TOK_DEV, 2 * INNER)
    narrow = (TOK_DEV, INNER)
    full = (TOK_DEV, D)
    weight = (D, INNER)
    scratch = [
        (full, BF16),
        (full, BF16),
        (weight, BF16),
        (weight, BF16),
        (weight, BF16),
        (weight, BF16),
        ((TOK_DEV, 1), F32),
        (full, BF16),
        ((D, TOK_DEV), BF16),
        ((D, ALL_TOK), BF16),
        ((WIDE, ALL_TOK), BF16),
        ((ALL_TOK, INNER), BF16),
        (narrow, BF16),
        (pair, BF16),
        (pair, BF16),
        (pair, BF16),
        (narrow, BF16),
        ((LOCAL_HEADS, TOK_DEV, WINDOW), F32),
        (narrow, BF16),
        (narrow, BF16),
        (narrow, BF16),
        (narrow, BF16),
        (pair, F32),
        (pair, BF16),
        (pair, BF16),
        (pair, BF16),
        (pair, BF16),
        (full, F32),
        ((ALL_TOK, 2 * HEAD), BF16),
        ((ALL_TOK, HEAD), BF16),
        ((2, 4, 4, ROWS, 2 * HEAD), BF16),
        ((2, 4, 4, ROWS, HEAD), BF16),
        ((4, ROWS, INNER), BF16),
        ((3, 2, 2, ROWS, 2 * HEAD), BF16),
        ((3, 2, 4, HALF_ROWS, 2 * HEAD), BF16),
        ((3, 2, 2, ROWS, HEAD), BF16),
        ((3, 2, 4, HALF_ROWS, HEAD), BF16),
        ((3, 4, ROWS, WIDE), BF16),
        ((2, 2, ROWS, 2 * HEAD), BF16),
        ((2, 4, HALF_ROWS, 2 * HEAD), BF16),
        ((2, 2, ROWS, HEAD), BF16),
        ((2, 4, HALF_ROWS, HEAD), BF16),
        ((4, ROWS, WIDE), BF16),
        ((3, 2, HALF_ROWS, 2 * HEAD), BF16),
        ((3, 2, HALF_ROWS, 2 * HEAD), BF16),
        ((3, 2, HALF_ROWS, HEAD), BF16),
        ((3, 2, HALF_ROWS, HEAD), BF16),
        ((3, ROWS, WIDE), BF16),
        ((4, HALF_ROWS, 2 * HEAD), BF16),
        ((4, HALF_ROWS, HEAD), BF16),
        ((ROWS, WIDE), BF16),
    ]
    semaphores = 140
    anywhere = pl.BlockSpec(memory_space=pl.ANY)
    scalars = pl.BlockSpec(memory_space=pltpu.SMEM)
    vector = pl.BlockSpec(memory_space=pltpu.VMEM)
    return pl.pallas_call(
        layer_kernel,
        out_shape=(
            jax.ShapeDtypeStruct(full, BF16),
            jax.ShapeDtypeStruct(full, BF16),
            jax.ShapeDtypeStruct((ROWS, 2 * INNER), BF16),
            jax.ShapeDtypeStruct((ROWS, INNER), BF16),
            jax.ShapeDtypeStruct((ROWS, INNER), BF16),
        ),
        in_specs=[anywhere] * 4 + [scalars] * 2,
        out_specs=(vector,) * 5,
        scratch_shapes=[pltpu.VMEM(shape, dtype) for shape, dtype in scratch]
        + [
            pltpu.SemaphoreType.DMA((semaphores,)),
            pltpu.SemaphoreType.DMA((semaphores,)),
            pltpu.SemaphoreType.DMA((13,)),
        ],
        compiler_params=pltpu.CompilerParams(
            collective_id=0, has_side_effects=True, vmem_limit_bytes=VMEM_LIMIT
        ),
        name="whole_layer",
    )(tokens, upstream, w_qkv, w_out, key_blocks, key_count)


def finish_kernel(
    factor, layer_in, tokens_in, sum_a, sum_b, sum_out, layer_out, grad_tokens, grad_qkv, grad_out
):
    layer_out[...] = layer_in[...]
    grad_tokens[...] = tokens_in[...]
    for head in range(LOCAL_HEADS):
        cols = lanes(head)
        grad_qkv[:, cols] = sum_a[:, lanes(2 * head)].astype(F32) * factor
        grad_qkv[:, lanes(head + LOCAL_HEADS)] = sum_b[:, cols].astype(F32) * factor
        grad_qkv[:, lanes(head + 2 * LOCAL_HEADS)] = (
            sum_a[:, lanes(2 * head + 1)].astype(F32) * factor
        )
    grad_out[...] = sum_out[...].astype(F32) * factor


def finish(factor, *results):
    full = jax.ShapeDtypeStruct((TOK_DEV, D), BF16)
    outs = (
        full,
        full,
        jax.ShapeDtypeStruct((ROWS, 3 * INNER), F32),
        jax.ShapeDtypeStruct((ROWS, INNER), F32),
    )
    steps = 2

    def blocks(arrays):
        return tuple(
            pl.BlockSpec((a.shape[0] // steps, a.shape[1]), lambda i: (i, 0)) for a in arrays
        )

    return pl.pallas_call(
        functools.partial(finish_kernel, factor),
        grid=(steps,),
        out_shape=outs,
        in_specs=blocks(results),
        out_specs=blocks(outs),
        name="finish",
    )(*results)


def body(tokens, cotangent, w_qkv, w_out, key_blocks, key_count):
    factor = 1.0 / math.sqrt(lax.axis_size("dp") * lax.axis_size("seq") * TOK_DEV)
    results = whole_layer(
        tokens[0], cotangent[0], w_qkv, w_out, key_blocks.T, key_count
    )
    layer_out, grad_tokens, grad_w_qkv, grad_w_out = finish(factor, *results)
    return (layer_out[None], grad_tokens[None], grad_w_qkv, grad_w_out)


def solution(mesh):
    return jax.shard_map(
        body,
        mesh=mesh,
        in_specs=(P("dp", "seq", None), P("dp", "seq", None), P(), P(), P(), P()),
        out_specs=(P("dp", "seq", None), P("dp", "seq", None), P("seq", None), P("seq", None)),
        check_vma=False,
    )
```

```python
import functools
import math

import jax
import jax.numpy as jnp
from jax import lax
from jax.experimental import pallas as pl
from jax.experimental.pallas import tpu as pltpu
from jax.sharding import PartitionSpec as P

LOCAL_HEADS = 8
HEAD = 128
INNER = LOCAL_HEADS * HEAD
D = 2048
TOK_DEV = 128
N_SEQ = 32
RING = 4
GROUP = 2 * RING
WINDOW = 3 * TOK_DEV
ALL_TOK = GROUP * TOK_DEV
ROWS = D // N_SEQ
HALF_ROWS = ROWS // 2
WIDE = 256
VMEM_LIMIT = 63 * 1024 * 1024

epsilon = 1e-06

BF16 = jnp.bfloat16
F32 = jnp.float32
CONTRACT_COLUMNS = (((1,), (1,)), ((), ()))
CONTRACT_ROWS = (((0,), (0,)), ((), ()))
STEPS = range(1, RING)
GROUP_STEPS = [(o, other) for o in range(RING) for other in range(2) if o + other]


def place():
    dp, seq = lax.axis_index("dp"), lax.axis_index("seq")
    return seq % 4, (seq // 4) % 4, (seq // 16) * 2 + dp // 2, dp % 2


def at(x, y, z, c):
    return {"dp": (z % 2) * 2 + c, "seq": (z // 2) * 16 + y * 4 + x}


def lanes(slot, width=HEAD):
    start = slot * width
    return pl.ds(start if isinstance(start, int) else pl.multiple_of(start, width), width)


def remote(src, dst, send, recv, device):
    return pltpu.make_async_remote_copy(
        src_ref=src,
        dst_ref=dst,
        send_sem=send,
        recv_sem=recv,
        device_id=device,
        device_id_type=pl.DeviceIdType.MESH,
    )


class Copies:
    def __init__(self, send, recv):
        self.send, self.recv, self.used = send, recv, 0

    def reserve(self, count):
        first = self.used
        self.used += count
        return first

    def start(self, src, dst, device):
        i = self.reserve(1)
        copy = remote(src, dst, self.send.at[i], self.recv.at[i], device)
        copy.start()
        return copy


def wait_all(copies):
    for copy in copies:
        copy.wait()


def signal_all(peers):
    barrier = pltpu.get_barrier_semaphore()
    for peer in peers:
        pl.semaphore_signal(
            barrier, inc=1, device_id=peer, device_id_type=pl.DeviceIdType.MESH
        )


class RingGather:
    def __init__(self, copies, slot, fast, slow, partner):
        self.copies, self.slot = copies, slot
        self.fast, self.slow, self.partner = fast, slow, partner
        self.waits, self.back = [], []

    def start(self, src, dst, device, part=None):
        return self.copies.start(self.slot(src, part), self.slot(dst, part), device)

    def begin(self):
        self.near = self.start(0, 2, self.fast)
        self.waits.append(self.start(0, 1, self.partner))

    def pass_on(self):
        self.near.wait()
        self.far = self.start(2, 4, self.fast)
        self.waits.append(self.start(2, 3, self.partner))

    def begin_slow(self, part):
        self.back.append(self.start(0, 6, self.slow, part))

    def share_far(self):
        self.far.wait()
        self.waits.append(self.start(4, 5, self.partner))

    def share_back(self):
        wait_all(self.back)
        self.waits.append(self.start(6, 7, self.partner))

    def end(self):
        wait_all(self.waits)


def added(first, *others):
    total = first.astype(F32)
    for other in others:
        total = total + other.astype(F32)
    return total.astype(BF16)


def layer_kernel(
    tokens_hbm,
    upstream_hbm,
    w_qkv_hbm,
    w_out_hbm,
    key_blocks,
    key_count,
    layer_out,
    grad_tokens,
    sum_a,
    sum_b,
    sum_out,
    tokens,
    upstream,
    w_query,
    w_keys,
    w_values,
    w_out,
    inv_rms,
    normed,
    upstream_t,
    all_normed,
    cot_rows,
    all_attended,
    query,
    kv,
    before,
    after,
    grad_att,
    probability,
    attended,
    grad_query,
    grad_keys,
    grad_values,
    own,
    to_before,
    to_after,
    from_after,
    from_before,
    grad_normed,
    grads_a,
    grads_b,
    part_a,
    part_b,
    part_out,
    x_first_a,
    z_first_a,
    x_first_b,
    z_first_b,
    y_first_out,
    x_summed_a,
    z_summed_a,
    x_summed_b,
    z_summed_b,
    y_summed_out,
    then_z_a,
    then_x_a,
    then_z_b,
    then_x_b,
    then_x_out,
    whole_a,
    whole_b,
    whole_out,
    send,
    recv,
    local,
):
    x, y, z, c = place()
    dp, seq = lax.axis_index("dp"), lax.axis_index("seq")
    z_hi, z_lo = z // 2, z % 2
    mine = y * 2 + c
    sign = jnp.where(x < 2, -1, 1)
    following = {"dp": dp, "seq": (seq + 1) % N_SEQ}
    preceding = {"dp": dp, "seq": (seq + N_SEQ - 1) % N_SEQ}
    has_after, has_before = seq < N_SEQ - 1, seq > 0
    scale = HEAD ** (-0.5)
    copies = Copies(send, recv)

    loads = {
        name: pltpu.make_async_copy(src, dst, local.at[i])
        for i, (name, src, dst) in enumerate(
            [
                ("tokens", tokens_hbm, tokens),
                ("keys", w_qkv_hbm.at[:, pl.ds(INNER, INNER)], w_keys),
                ("values", w_qkv_hbm.at[:, pl.ds(2 * INNER, INNER)], w_values),
                ("upstream", upstream_hbm, upstream),
                ("query", w_qkv_hbm.at[:, pl.ds(0, INNER)], w_query),
                ("out", w_out_hbm, w_out),
            ]
        )
    }
    loads["tokens"].start()
    loads["keys"].start()

    peers = [
        at(x, (y + o) % 4, z_hi * 2 + (z_lo + lo) % 2, (c + other) % 2)
        for o in range(RING)
        for lo in range(2)
        for other in range(2)
        if o + lo + other
    ]
    peers += [at(x, y, (1 - z_hi) * 2 + lo, core) for lo in range(2) for core in range(2)]
    peers += [at((x + o) % 4, y, z, c) for o in STEPS]
    peers += [following, preceding]
    signal_all(peers)

    zero_block = jnp.zeros((TOK_DEV, 2 * INNER), BF16)

    @pl.when(jnp.logical_not(has_before))
    def _():
        before[...] = zero_block
        from_before[...] = zero_block

    @pl.when(jnp.logical_not(has_after))
    def _():
        after[...] = zero_block
        from_after[...] = zero_block

    count = key_count[seq]
    listed = [key_blocks[j, seq] for j in range(3)]
    biases = []
    for shift in (-1, 0, 1):
        used = jnp.int32(0)
        for j in range(3):
            hit = jnp.where(listed[j] == seq + shift, 1, 0) * jnp.where(j < count, 1, 0)
            used = used + hit
        used = jnp.full((1, TOK_DEV), used, jnp.int32)
        biases.append(jnp.where(used > 0, 0.0, -jnp.inf).astype(F32))
    bias = jnp.concatenate(biases, axis=1)

    loads["tokens"].wait()
    wide_tokens = tokens[...].astype(F32)
    inv_rms[...] = lax.rsqrt(jnp.mean(wide_tokens * wide_tokens, axis=1, keepdims=True) + epsilon)
    normed[...] = (wide_tokens * inv_rms[...]).astype(BF16)

    def project(rows, weight, out, first):
        def chunk(i, carry):
            product = jnp.dot(rows[...], weight[:, lanes(i, WIDE)], preferred_element_type=F32)
            out[:, lanes(i + first, WIDE)] = product.astype(BF16)
            return carry

        lax.fori_loop(0, INNER // WIDE, chunk, 0)

    def halo(i, part):
        cols = pl.ds(part * INNER, INNER)
        return (
            remote(kv.at[:, cols], before.at[:, cols], send.at[i], recv.at[i], following),
            remote(kv.at[:, cols], after.at[:, cols], send.at[i + 1], recv.at[i + 1], preceding),
        )

    halo_at = [copies.reserve(2), copies.reserve(2)]

    def send_halo(part):
        forth, back = halo(halo_at[part], part)

        @pl.when(has_after)
        def _():
            forth.start()

        @pl.when(has_before)
        def _():
            back.start()

    def take_halo(part):
        forth, back = halo(halo_at[part], part)

        @pl.when(has_after)
        def _():
            forth.wait_send()
            back.wait_recv()

        @pl.when(has_before)
        def _():
            back.wait_send()
            forth.wait_recv()

    def turn(rows, out):
        def chunk(i, carry):
            out[pl.ds(pl.multiple_of(i * WIDE, WIDE), WIDE), pl.ds(0, TOK_DEV)] = jnp.transpose(
                rows[:, lanes(i, WIDE)]
            )
            return carry

        lax.fori_loop(0, D // WIDE, chunk, 0)

    def exchange_y(src_view, dst_view):
        sent = []
        for o, other in GROUP_STEPS:
            to, core = (y + sign * o + 4) % 4, (c + other) % 2
            sent.append(
                copies.start(src_view(to, core), dst_view(2 * o + other), at(x, to, z, core))
            )
        return sent

    def exchange_z(src_view, dst_view):
        sent = []
        for o, other in GROUP_STEPS:
            to, core = (z + o) % 4, (c + other) % 2
            sent.append(
                copies.start(src_view(to, core), dst_view(2 * o + other), at(x, y, to, core))
            )
        return sent

    partner = at(x, y, z, 1 - c)
    fast, slow = at(x, (y + sign + 4) % 4, z, c), at(x, (y - sign + 4) % 4, z, c)

    def normed_slot(slot, part):
        rows = pl.ds(0, D) if part is None else pl.ds(part * (D // 2), D // 2)
        return all_normed.at[rows, lanes(slot)]

    def attended_slot(slot, part):
        cols = pl.ds(0, INNER) if part is None else pl.ds(part * (INNER // 2), INNER // 2)
        return all_attended.at[lanes(slot), cols]

    normed_ring = RingGather(copies, normed_slot, fast, slow, partner)
    attended_ring = RingGather(
        copies,
        attended_slot,
        at(x, y, (z + 1) % 4, c),
        at(x, y, (z + 3) % 4, c),
        partner,
    )

    turn(normed, all_normed)
    pl.semaphore_wait(pltpu.get_barrier_semaphore(), len(peers))
    normed_ring.begin()
    normed_ring.begin_slow(0)
    loads["keys"].wait()
    loads["values"].start()
    loads["upstream"].start()
    project(normed, w_keys, kv, 0)
    send_halo(0)
    loads["values"].wait()
    loads["query"].start()
    loads["out"].start()
    project(normed, w_values, kv, INNER // WIDE)
    send_halo(1)
    loads["upstream"].wait()
    turn(upstream, upstream_t)

    def turned(to, core):
        return upstream_t.at[lanes(to * 2 + core, WIDE), :]

    loads["query"].wait()
    project(normed, w_query, query, 0)
    loads["out"].wait()
    project(upstream, w_out, grad_att, 0)

    def pairs(body):
        def step(i, carry):
            for head in (2 * i, 2 * i + 1):
                body(head)
            return carry

        return step

    def window(cols):
        return jnp.concatenate([before[:, cols], kv[:, cols], after[:, cols]], axis=0)

    def value_cols(head):
        return lanes(head + LOCAL_HEADS)

    def weigh(head):
        cols = lanes(head)
        scores = lax.dot_general(
            query[:, cols], window(cols), CONTRACT_COLUMNS, preferred_element_type=F32
        )
        scores = scores * scale + bias
        raised = jnp.exp(scores - jnp.max(scores, axis=1, keepdims=True))
        probability[head] = raised / jnp.sum(raised, axis=1, keepdims=True)

    def give_back(part, cols):
        to_before[:, cols] = part[:TOK_DEV].astype(BF16)
        own[:, cols] = part[TOK_DEV : 2 * TOK_DEV]
        to_after[:, cols] = part[2 * TOK_DEV :].astype(BF16)

    def attend(head):
        cols = lanes(head)
        weights = probability[head].astype(BF16)
        output = jnp.dot(weights, window(value_cols(head)), preferred_element_type=F32)
        attended[:, cols] = output.astype(BF16)
        part = lax.dot_general(
            weights, grad_att[:, cols], CONTRACT_ROWS, preferred_element_type=F32
        )
        give_back(part, value_cols(head))

    def attend_back(head):
        cols = lanes(head)
        grad = grad_att[:, cols]
        keys = window(cols)
        delta = jnp.sum(
            grad.astype(F32) * attended[:, cols].astype(F32), axis=1, keepdims=True
        )
        grad_prob = lax.dot_general(
            grad, window(value_cols(head)), CONTRACT_COLUMNS, preferred_element_type=F32
        )
        grad_score = (probability[head] * (grad_prob - delta) * scale).astype(BF16)
        grad_query[:, cols] = jnp.dot(grad_score, keys, preferred_element_type=F32).astype(BF16)
        part = lax.dot_general(
            grad_score, query[:, cols], CONTRACT_ROWS, preferred_element_type=F32
        )
        give_back(part, cols)

    pair_count = LOCAL_HEADS // 2
    back_at = copies.reserve(4 * pair_count)

    def returned(i):
        cols = lanes(i, 2 * HEAD)
        down, up = back_at + i, back_at + 2 * pair_count + i
        return (
            remote(
                to_before.at[:, cols], from_after.at[:, cols], send.at[down], recv.at[down], preceding
            ),
            remote(
                to_after.at[:, cols], from_before.at[:, cols], send.at[up], recv.at[up], following
            ),
        )

    def send_back(i):
        down, up = returned(i)

        @pl.when(has_before)
        def _():
            down.start()

        @pl.when(has_after)
        def _():
            up.start()

    def take_back(first):
        @pl.when(has_after)
        def _():
            for i in range(first, first + pair_count):
                down, up = returned(i)
                down.wait_recv()
                up.wait_send()

        @pl.when(has_before)
        def _():
            for i in range(first, first + pair_count):
                down, up = returned(i)
                down.wait_send()
                up.wait_recv()

    def settle(out, first):
        cols = pl.ds(first, INNER)
        out[...] = added(own[:, cols], from_after[:, cols], from_before[:, cols])

    take_halo(0)
    lax.fori_loop(0, pair_count, pairs(weigh), 0)
    normed_ring.pass_on()
    take_halo(1)
    normed_ring.begin_slow(1)

    def attend_pair(i, carry):
        pairs(attend)(i, carry)
        send_back(i + pair_count)
        return carry

    lax.fori_loop(0, pair_count, attend_pair, 0)
    all_attended[pl.ds(0, TOK_DEV), :] = attended[...]
    attended_ring.begin()
    attended_ring.begin_slow(None)

    def back_pair(i, carry):
        pairs(attend_back)(i, carry)
        send_back(i)
        return carry

    lax.fori_loop(0, pair_count, back_pair, 0)

    def swap_columns(src, dst, cols, i):
        stay = pltpu.make_async_copy(
            src.at[:, lanes(mine)], dst.at[pl.ds(0, TOK_DEV), cols], local.at[i]
        )
        stay.start()
        return [stay] + exchange_y(
            lambda to, core: src.at[:, lanes(to * 2 + core)],
            lambda slot: dst.at[lanes(slot), cols],
        )

    sent_query = swap_columns(grad_query, grads_a, pl.ds(0, HEAD), 7)

    def out_chunk(i, carry):
        cols = lanes(i, WIDE)
        rows = pl.ds(pl.multiple_of(i * WIDE, WIDE), WIDE)
        product = lax.dot_general(
            attended[...], w_out[rows, :], CONTRACT_COLUMNS, preferred_element_type=F32
        )
        layer_out[:, cols] = (tokens[:, cols].astype(F32) + product).astype(BF16)
        return carry

    lax.fori_loop(0, D // WIDE, out_chunk, 0)
    take_back(pair_count)
    settle(grad_values, INNER)
    sent_values = swap_columns(grad_values, grads_a, pl.ds(HEAD, HEAD), 8)
    attended_ring.pass_on()

    def grad_chunk_a(i, carry):
        rows = pl.ds(pl.multiple_of(i * WIDE, WIDE), WIDE)
        grad_normed[:, lanes(i, WIDE)] = lax.dot_general(
            grad_query[...], w_query[rows, :], CONTRACT_COLUMNS, preferred_element_type=F32
        ) + lax.dot_general(
            grad_values[...], w_values[rows, :], CONTRACT_COLUMNS, preferred_element_type=F32
        )
        return carry

    lax.fori_loop(0, D // WIDE, grad_chunk_a, 0)
    normed_ring.share_far()
    take_back(0)
    settle(grad_keys, 0)
    sent_keys = swap_columns(grad_keys, grads_b, pl.ds(0, HEAD), 9)
    keep = [pltpu.make_async_copy(turned(z, c), cot_rows.at[:, lanes(0)], local.at[6])]
    keep[0].start()
    sent_cot = exchange_z(turned, lambda slot: cot_rows.at[:, lanes(slot)])
    normed_ring.share_back()
    normed_ring.end()

    def multiply(grads, part, width):
        def chunk(i, carry):
            rows = pl.ds(pl.multiple_of(i * WIDE, WIDE), WIDE)
            product = jnp.dot(all_normed[rows, :], grads[...], preferred_element_type=F32)
            part[i // 4, i % 4] = product.astype(BF16).reshape(4, ROWS, width)
            return carry

        lax.fori_loop(0, D // WIDE, chunk, 0)

    def half(lo):
        return pl.ds(pl.multiple_of(lo * HALF_ROWS, HALF_ROWS), HALF_ROWS)

    first_y, last_y = pl.ds(0, 2), pl.ds(2, 2)

    def scatter(grads, part, width, x_first, z_first):
        multiply(grads, part, width)
        x_sent, z_sent = [], []
        for o in STEPS:
            to = (x + o) % 4
            x_sent.append(
                copies.start(part.at[:, first_y, to], x_first.at[o - 1], at(to, y, z, c))
            )
            to = (z + o) % 4
            z_sent.append(
                copies.start(
                    part.at[to // 2, last_y, :, half(to % 2)], z_first.at[o - 1], at(x, y, to, c)
                )
            )
        return x_sent, z_sent

    def scatter_on(sent, part, x_first, z_first, x_summed, z_summed, then_z, then_x):
        x_sent, z_sent = sent
        wait_all(x_sent)
        x_summed[...] = added(part[:, first_y, x], x_first[0], x_first[1], x_first[2])
        z_then = []
        for o in STEPS:
            to = (z + o) % 4
            z_then.append(
                copies.start(
                    x_summed.at[to // 2, :, half(to % 2)], then_z.at[o - 1], at(x, y, to, c)
                )
            )
        wait_all(z_sent)
        z_summed[...] = added(
            part[z_hi, last_y, :, half(z_lo)], z_first[0], z_first[1], z_first[2]
        )
        x_then = [
            copies.start(z_summed.at[:, (x + o) % 4], then_x.at[o - 1], at((x + o) % 4, y, z, c))
            for o in STEPS
        ]
        return z_then, x_then

    finals = [
        (o, lo, other)
        for o in range(RING)
        for lo in range(2)
        for other in range(2)
        if o + lo + other
    ]

    def gather_sums(sent, x_summed, z_summed, then_z, then_x, whole, out, width, i):
        z_then, x_then = sent
        wait_all(z_then)
        whole[first_y] = added(x_summed[z_hi, :, half(z_lo)], then_z[0], then_z[1], then_z[2])
        wait_all(x_then)
        whole[last_y] = added(z_summed[:, x], then_x[0], then_x[1], then_x[2])
        own_place = out.at[half(z_lo), lanes(mine, width)]
        stay = pltpu.make_async_copy(whole.at[y], own_place, local.at[i])
        stay.start()
        last = [stay]
        for o, lo, other in finals:
            to = (y + o) % 4
            device = at(x, to, z_hi * 2 + (z_lo + lo) % 2, (c + other) % 2)
            last.append(copies.start(whole.at[to], own_place, device))
        return last

    wait_all(sent_query + sent_values)
    sent_a = scatter(grads_a, part_a, 2 * HEAD, x_first_a, z_first_a)
    attended_ring.share_back()
    attended_ring.share_far()

    wait_all(sent_keys)
    sent_b = scatter(grads_b, part_b, HEAD, x_first_b, z_first_b)

    def grad_chunk_b(i, total):
        rows, cols = pl.ds(pl.multiple_of(i * WIDE, WIDE), WIDE), lanes(i, WIDE)
        product = grad_normed[:, cols] + lax.dot_general(
            grad_keys[...], w_keys[rows, :], CONTRACT_COLUMNS, preferred_element_type=F32
        )
        grad_normed[:, cols] = product
        along = product * (tokens[:, cols].astype(F32) * inv_rms[...])
        return total + jnp.sum(along, axis=1, keepdims=True)

    total = lax.fori_loop(0, D // WIDE, grad_chunk_b, jnp.zeros((TOK_DEV, 1), F32))
    mean = total * (1.0 / D)

    def tokens_chunk(i, carry):
        cols = lanes(i, WIDE)
        normed_wide = tokens[:, cols].astype(F32) * inv_rms[...]
        branch = inv_rms[...] * (grad_normed[:, cols] - normed_wide * mean)
        grad_tokens[:, cols] = (upstream[:, cols].astype(F32) + branch).astype(BF16)
        return carry

    wait_all(keep + sent_cot)
    attended_ring.end()

    def out_part(i, carry):
        cols = lanes(i, WIDE)
        product = jnp.dot(cot_rows[...], all_attended[:, cols], preferred_element_type=F32)
        part_out[:, :, cols] = product.astype(BF16).reshape(4, ROWS, WIDE)
        return carry

    lax.fori_loop(0, INNER // WIDE, out_part, 0)
    y_sent_out = [
        copies.start(
            part_out.at[:, :, lanes((y + o) % 4, WIDE)],
            y_first_out.at[o - 1],
            at(x, (y + o) % 4, z, c),
        )
        for o in STEPS
    ]
    then_a = scatter_on(
        sent_a, part_a, x_first_a, z_first_a, x_summed_a, z_summed_a, then_z_a, then_x_a
    )
    wait_all(y_sent_out)
    y_summed_out[...] = added(
        part_out[:, :, lanes(y, WIDE)], y_first_out[0], y_first_out[1], y_first_out[2]
    )
    x_then_out = [
        copies.start(
            y_summed_out.at[(x + o) % 4], then_x_out.at[o - 1], at((x + o) % 4, y, z, c)
        )
        for o in STEPS
    ]
    lax.fori_loop(0, D // WIDE, tokens_chunk, 0)
    then_b = scatter_on(
        sent_b, part_b, x_first_b, z_first_b, x_summed_b, z_summed_b, then_z_b, then_x_b
    )
    last = gather_sums(
        then_a, x_summed_a, z_summed_a, then_z_a, then_x_a, whole_a, sum_a, 2 * HEAD, 10
    )

    wait_all(x_then_out)
    whole_out[...] = added(y_summed_out[x], then_x_out[0], then_x_out[1], then_x_out[2])
    final_at = copies.reserve(4)
    owner = 2 * z_lo + c
    holds_own = y == owner
    out_place = sum_out.at[:, lanes(y, WIDE)]
    outgoing = [
        remote(
            whole_out,
            out_place,
            send.at[final_at + 2 * lo + other],
            recv.at[final_at + y],
            at(x, owner, z_hi * 2 + (z_lo + lo) % 2, (c + other) % 2),
        )
        for lo in range(2)
        for other in range(2)
    ]
    for copy in outgoing[1:]:
        copy.start()

    @pl.when(jnp.logical_not(holds_own))
    def _():
        outgoing[0].start()

    @pl.when(holds_own)
    def _():
        stay = pltpu.make_async_copy(whole_out, out_place, local.at[12])
        stay.start()
        stay.wait()

    last += gather_sums(
        then_b, x_summed_b, z_summed_b, then_z_b, then_x_b, whole_b, sum_b, HEAD, 11
    )
    for copy in outgoing[1:]:
        copy.wait_send()

    @pl.when(jnp.logical_not(holds_own))
    def _():
        outgoing[0].wait_send()

    for source in range(RING):
        incoming = remote(
            whole_out,
            sum_out.at[:, lanes(source, WIDE)],
            send.at[final_at],
            recv.at[final_at + source],
            at(x, source, z_hi * 2 + y // 2, y % 2),
        )

        @pl.when(jnp.logical_not(holds_own & (y == source)))
        def _(incoming=incoming):
            incoming.wait_recv()

    wait_all(last)


def whole_layer(tokens, upstream, w_qkv, w_out, key_blocks, key_count):
    pair = (TOK_DEV, 2 * INNER)
    narrow = (TOK_DEV, INNER)
    full = (TOK_DEV, D)
    weight = (D, INNER)
    scratch = [
        (full, BF16),
        (full, BF16),
        (weight, BF16),
        (weight, BF16),
        (weight, BF16),
        (weight, BF16),
        ((TOK_DEV, 1), F32),
        (full, BF16),
        ((D, TOK_DEV), BF16),
        ((D, ALL_TOK), BF16),
        ((WIDE, ALL_TOK), BF16),
        ((ALL_TOK, INNER), BF16),
        (narrow, BF16),
        (pair, BF16),
        (pair, BF16),
        (pair, BF16),
        (narrow, BF16),
        ((LOCAL_HEADS, TOK_DEV, WINDOW), F32),
        (narrow, BF16),
        (narrow, BF16),
        (narrow, BF16),
        (narrow, BF16),
        (pair, F32),
        (pair, BF16),
        (pair, BF16),
        (pair, BF16),
        (pair, BF16),
        (full, F32),
        ((ALL_TOK, 2 * HEAD), BF16),
        ((ALL_TOK, HEAD), BF16),
        ((2, 4, 4, ROWS, 2 * HEAD), BF16),
        ((2, 4, 4, ROWS, HEAD), BF16),
        ((4, ROWS, INNER), BF16),
        ((3, 2, 2, ROWS, 2 * HEAD), BF16),
        ((3, 2, 4, HALF_ROWS, 2 * HEAD), BF16),
        ((3, 2, 2, ROWS, HEAD), BF16),
        ((3, 2, 4, HALF_ROWS, HEAD), BF16),
        ((3, 4, ROWS, WIDE), BF16),
        ((2, 2, ROWS, 2 * HEAD), BF16),
        ((2, 4, HALF_ROWS, 2 * HEAD), BF16),
        ((2, 2, ROWS, HEAD), BF16),
        ((2, 4, HALF_ROWS, HEAD), BF16),
        ((4, ROWS, WIDE), BF16),
        ((3, 2, HALF_ROWS, 2 * HEAD), BF16),
        ((3, 2, HALF_ROWS, 2 * HEAD), BF16),
        ((3, 2, HALF_ROWS, HEAD), BF16),
        ((3, 2, HALF_ROWS, HEAD), BF16),
        ((3, ROWS, WIDE), BF16),
        ((4, HALF_ROWS, 2 * HEAD), BF16),
        ((4, HALF_ROWS, HEAD), BF16),
        ((ROWS, WIDE), BF16),
    ]
    semaphores = 140
    anywhere = pl.BlockSpec(memory_space=pl.ANY)
    scalars = pl.BlockSpec(memory_space=pltpu.SMEM)
    vector = pl.BlockSpec(memory_space=pltpu.VMEM)
    return pl.pallas_call(
        layer_kernel,
        out_shape=(
            jax.ShapeDtypeStruct(full, BF16),
            jax.ShapeDtypeStruct(full, BF16),
            jax.ShapeDtypeStruct((ROWS, 2 * INNER), BF16),
            jax.ShapeDtypeStruct((ROWS, INNER), BF16),
            jax.ShapeDtypeStruct((ROWS, INNER), BF16),
        ),
        in_specs=[anywhere] * 4 + [scalars] * 2,
        out_specs=(vector,) * 5,
        scratch_shapes=[pltpu.VMEM(shape, dtype) for shape, dtype in scratch]
        + [
            pltpu.SemaphoreType.DMA((semaphores,)),
            pltpu.SemaphoreType.DMA((semaphores,)),
            pltpu.SemaphoreType.DMA((13,)),
        ],
        compiler_params=pltpu.CompilerParams(
            collective_id=0, has_side_effects=True, vmem_limit_bytes=VMEM_LIMIT
        ),
        name="whole_layer",
    )(tokens, upstream, w_qkv, w_out, key_blocks, key_count)


def finish_kernel(
    factor, layer_in, tokens_in, sum_a, sum_b, sum_out, layer_out, grad_tokens, grad_qkv, grad_out
):
    layer_out[...] = layer_in[...]
    grad_tokens[...] = tokens_in[...]
    for head in range(LOCAL_HEADS):
        cols = lanes(head)
        grad_qkv[:, cols] = sum_a[:, lanes(2 * head)].astype(F32) * factor
        grad_qkv[:, lanes(head + LOCAL_HEADS)] = sum_b[:, cols].astype(F32) * factor
        grad_qkv[:, lanes(head + 2 * LOCAL_HEADS)] = (
            sum_a[:, lanes(2 * head + 1)].astype(F32) * factor
        )
    grad_out[...] = sum_out[...].astype(F32) * factor


def finish(factor, *results):
    full = jax.ShapeDtypeStruct((TOK_DEV, D), BF16)
    outs = (
        full,
        full,
        jax.ShapeDtypeStruct((ROWS, 3 * INNER), F32),
        jax.ShapeDtypeStruct((ROWS, INNER), F32),
    )
    steps = 2

    def blocks(arrays):
        return tuple(
            pl.BlockSpec((a.shape[0] // steps, a.shape[1]), lambda i: (i, 0)) for a in arrays
        )

    return pl.pallas_call(
        functools.partial(finish_kernel, factor),
        grid=(steps,),
        out_shape=outs,
        in_specs=blocks(results),
        out_specs=blocks(outs),
        name="finish",
    )(*results)


def body(tokens, cotangent, w_qkv, w_out, key_blocks, key_count):
    factor = 1.0 / math.sqrt(lax.axis_size("dp") * lax.axis_size("seq") * TOK_DEV)
    results = whole_layer(
        tokens[0], cotangent[0], w_qkv, w_out, key_blocks.T, key_count
    )
    layer_out, grad_tokens, grad_w_qkv, grad_w_out = finish(factor, *results)
    return (layer_out[None], grad_tokens[None], grad_w_qkv, grad_w_out)


def solution(mesh):
    return jax.shard_map(
        body,
        mesh=mesh,
        in_specs=(P("dp", "seq", None), P("dp", "seq", None), P(), P(), P(), P()),
        out_specs=(P("dp", "seq", None), P("dp", "seq", None), P("seq", None), P("seq", None)),
        check_vma=False,
    )
```

```python
import functools
import math

import jax
import jax.numpy as jnp
from jax import lax
from jax.experimental import pallas as pl
from jax.experimental.pallas import tpu as pltpu
from jax.sharding import PartitionSpec as P

LOCAL_HEADS = 8
HEAD = 128
INNER = LOCAL_HEADS * HEAD
D = 2048
TOK_DEV = 128
N_SEQ = 32
RING = 4
GROUP = 2 * RING
WINDOW = 3 * TOK_DEV
ALL_TOK = GROUP * TOK_DEV
ROWS = D // N_SEQ
HALF_ROWS = ROWS // 2
WIDE = 256
VMEM_LIMIT = 63 * 1024 * 1024

epsilon = 1e-06

BF16 = jnp.bfloat16
F32 = jnp.float32
CONTRACT_COLUMNS = (((1,), (1,)), ((), ()))
CONTRACT_ROWS = (((0,), (0,)), ((), ()))
STEPS = range(1, RING)
GROUP_STEPS = [(o, other) for o in range(RING) for other in range(2) if o + other]


def place():
    dp, seq = lax.axis_index("dp"), lax.axis_index("seq")
    return seq % 4, (seq // 4) % 4, (seq // 16) * 2 + dp // 2, dp % 2


def at(x, y, z, c):
    return {"dp": (z % 2) * 2 + c, "seq": (z // 2) * 16 + y * 4 + x}


def lanes(slot, width=HEAD):
    start = slot * width
    return pl.ds(start if isinstance(start, int) else pl.multiple_of(start, width), width)


def remote(src, dst, send, recv, device):
    return pltpu.make_async_remote_copy(
        src_ref=src,
        dst_ref=dst,
        send_sem=send,
        recv_sem=recv,
        device_id=device,
        device_id_type=pl.DeviceIdType.MESH,
    )


class Copies:
    def __init__(self, send, recv):
        self.send, self.recv, self.used = send, recv, 0

    def reserve(self, count):
        first = self.used
        self.used += count
        return first

    def start(self, src, dst, device):
        i = self.reserve(1)
        copy = remote(src, dst, self.send.at[i], self.recv.at[i], device)
        copy.start()
        return copy


def wait_all(copies):
    for copy in copies:
        copy.wait()


def signal_all(peers):
    barrier = pltpu.get_barrier_semaphore()
    for peer in peers:
        pl.semaphore_signal(
            barrier, inc=1, device_id=peer, device_id_type=pl.DeviceIdType.MESH
        )


class RingGather:
    def __init__(self, copies, slot, fast, slow, partner):
        self.copies, self.slot = copies, slot
        self.fast, self.slow, self.partner = fast, slow, partner
        self.waits, self.back = [], []

    def start(self, src, dst, device, part=None):
        return self.copies.start(self.slot(src, part), self.slot(dst, part), device)

    def begin(self):
        self.near = self.start(0, 2, self.fast)
        self.waits.append(self.start(0, 1, self.partner))

    def pass_on(self):
        self.near.wait()
        self.far = self.start(2, 4, self.fast)
        self.waits.append(self.start(2, 3, self.partner))

    def begin_slow(self, part):
        self.back.append(self.start(0, 6, self.slow, part))

    def share_far(self):
        self.far.wait()
        self.waits.append(self.start(4, 5, self.partner))

    def share_back(self):
        wait_all(self.back)
        self.waits.append(self.start(6, 7, self.partner))

    def end(self):
        wait_all(self.waits)


def added(first, *others):
    total = first.astype(F32)
    for other in others:
        total = total + other.astype(F32)
    return total.astype(BF16)


def layer_kernel(
    tokens_hbm,
    upstream_hbm,
    w_qkv_hbm,
    w_out_hbm,
    key_blocks,
    key_count,
    layer_out_hbm,
    grad_tokens_hbm,
    sum_a,
    sum_b,
    sum_out,
    layer_out,
    grad_tokens,
    tokens,
    upstream,
    w_query,
    w_keys,
    w_values,
    w_out,
    inv_rms,
    normed,
    upstream_t,
    all_normed,
    cot_rows,
    all_attended,
    query,
    kv,
    before,
    after,
    grad_att,
    probability,
    attended,
    grad_query,
    grad_keys,
    grad_values,
    own,
    to_before,
    to_after,
    from_after,
    from_before,
    grad_normed,
    grads_a,
    grads_b,
    part_a,
    part_b,
    part_out,
    x_first_a,
    z_first_a,
    x_first_b,
    z_first_b,
    y_first_out,
    x_summed_a,
    z_summed_a,
    x_summed_b,
    z_summed_b,
    y_summed_out,
    then_z_a,
    then_x_a,
    then_z_b,
    then_x_b,
    then_x_out,
    whole_a,
    whole_b,
    whole_out,
    send,
    recv,
    local,
):
    x, y, z, c = place()
    dp, seq = lax.axis_index("dp"), lax.axis_index("seq")
    z_hi, z_lo = z // 2, z % 2
    mine = y * 2 + c
    sign = jnp.where(x < 2, -1, 1)
    following = {"dp": dp, "seq": (seq + 1) % N_SEQ}
    preceding = {"dp": dp, "seq": (seq + N_SEQ - 1) % N_SEQ}
    has_after, has_before = seq < N_SEQ - 1, seq > 0
    scale = HEAD ** (-0.5)
    copies = Copies(send, recv)

    loads = {
        name: pltpu.make_async_copy(src, dst, local.at[i])
        for i, (name, src, dst) in enumerate(
            [
                ("tokens", tokens_hbm, tokens),
                ("keys", w_qkv_hbm.at[:, pl.ds(INNER, INNER)], w_keys),
                ("values", w_qkv_hbm.at[:, pl.ds(2 * INNER, INNER)], w_values),
                ("upstream", upstream_hbm, upstream),
                ("query", w_qkv_hbm.at[:, pl.ds(0, INNER)], w_query),
                ("out", w_out_hbm, w_out),
            ]
        )
    }
    loads["tokens"].start()
    loads["keys"].start()

    peers = [
        at(x, (y + o) % 4, z_hi * 2 + (z_lo + lo) % 2, (c + other) % 2)
        for o in range(RING)
        for lo in range(2)
        for other in range(2)
        if o + lo + other
    ]
    peers += [at(x, y, (1 - z_hi) * 2 + lo, core) for lo in range(2) for core in range(2)]
    peers += [at((x + o) % 4, y, z, c) for o in STEPS]
    peers += [following, preceding]
    signal_all(peers)

    zero_block = jnp.zeros((TOK_DEV, 2 * INNER), BF16)

    @pl.when(jnp.logical_not(has_before))
    def _():
        before[...] = zero_block
        from_before[...] = zero_block

    @pl.when(jnp.logical_not(has_after))
    def _():
        after[...] = zero_block
        from_after[...] = zero_block

    count = key_count[seq]
    listed = [key_blocks[j, seq] for j in range(3)]
    biases = []
    for shift in (-1, 0, 1):
        used = jnp.int32(0)
        for j in range(3):
            hit = jnp.where(listed[j] == seq + shift, 1, 0) * jnp.where(j < count, 1, 0)
            used = used + hit
        used = jnp.full((1, TOK_DEV), used, jnp.int32)
        biases.append(jnp.where(used > 0, 0.0, -jnp.inf).astype(F32))
    bias = jnp.concatenate(biases, axis=1)

    loads["tokens"].wait()
    loads["values"].start()
    wide_tokens = tokens[...].astype(F32)
    inv_rms[...] = lax.rsqrt(jnp.mean(wide_tokens * wide_tokens, axis=1, keepdims=True) + epsilon)
    normed[...] = (wide_tokens * inv_rms[...]).astype(BF16)

    def project(rows, weight, out, first):
        def chunk(i, carry):
            product = jnp.dot(rows[...], weight[:, lanes(i, WIDE)], preferred_element_type=F32)
            out[:, lanes(i + first, WIDE)] = product.astype(BF16)
            return carry

        lax.fori_loop(0, INNER // WIDE, chunk, 0)

    def halo(i, part):
        cols = pl.ds(part * INNER, INNER)
        return (
            remote(kv.at[:, cols], before.at[:, cols], send.at[i], recv.at[i], following),
            remote(kv.at[:, cols], after.at[:, cols], send.at[i + 1], recv.at[i + 1], preceding),
        )

    halo_at = [copies.reserve(2), copies.reserve(2)]

    def send_halo(part):
        forth, back = halo(halo_at[part], part)

        @pl.when(has_after)
        def _():
            forth.start()

        @pl.when(has_before)
        def _():
            back.start()

    def take_halo(part):
        forth, back = halo(halo_at[part], part)

        @pl.when(has_after)
        def _():
            forth.wait_send()
            back.wait_recv()

        @pl.when(has_before)
        def _():
            back.wait_send()
            forth.wait_recv()

    def turn(rows, out):
        def chunk(i, carry):
            out[pl.ds(pl.multiple_of(i * WIDE, WIDE), WIDE), pl.ds(0, TOK_DEV)] = jnp.transpose(
                rows[:, lanes(i, WIDE)]
            )
            return carry

        lax.fori_loop(0, D // WIDE, chunk, 0)

    def exchange_y(src_view, dst_view):
        sent = []
        for o, other in GROUP_STEPS:
            to, core = (y + sign * o + 4) % 4, (c + other) % 2
            sent.append(
                copies.start(src_view(to, core), dst_view(2 * o + other), at(x, to, z, core))
            )
        return sent

    def exchange_z(src_view, dst_view):
        sent = []
        for o, other in GROUP_STEPS:
            to, core = (z + o) % 4, (c + other) % 2
            sent.append(
                copies.start(src_view(to, core), dst_view(2 * o + other), at(x, y, to, core))
            )
        return sent

    partner = at(x, y, z, 1 - c)
    fast, slow = at(x, (y + sign + 4) % 4, z, c), at(x, (y - sign + 4) % 4, z, c)

    def normed_slot(slot, part):
        rows = pl.ds(0, D) if part is None else pl.ds(part * (D // 2), D // 2)
        return all_normed.at[rows, lanes(slot)]

    def attended_slot(slot, part):
        cols = pl.ds(0, INNER) if part is None else pl.ds(part * (INNER // 2), INNER // 2)
        return all_attended.at[lanes(slot), cols]

    normed_ring = RingGather(copies, normed_slot, fast, slow, partner)
    attended_ring = RingGather(
        copies,
        attended_slot,
        at(x, y, (z + 1) % 4, c),
        at(x, y, (z + 3) % 4, c),
        partner,
    )

    turn(normed, all_normed)
    pl.semaphore_wait(pltpu.get_barrier_semaphore(), len(peers))
    normed_ring.begin()
    normed_ring.begin_slow(0)
    loads["keys"].wait()
    loads["upstream"].start()
    loads["query"].start()
    project(normed, w_keys, kv, 0)
    send_halo(0)
    loads["values"].wait()
    loads["out"].start()
    project(normed, w_values, kv, INNER // WIDE)
    send_halo(1)
    loads["upstream"].wait()
    turn(upstream, upstream_t)

    def turned(to, core):
        return upstream_t.at[lanes(to * 2 + core, WIDE), :]

    loads["query"].wait()
    project(normed, w_query, query, 0)
    loads["out"].wait()
    project(upstream, w_out, grad_att, 0)

    def pairs(body):
        def step(i, carry):
            for head in (2 * i, 2 * i + 1):
                body(head)
            return carry

        return step

    def window(cols):
        return jnp.concatenate([before[:, cols], kv[:, cols], after[:, cols]], axis=0)

    def value_cols(head):
        return lanes(head + LOCAL_HEADS)

    def weigh(head):
        cols = lanes(head)
        scores = lax.dot_general(
            query[:, cols], window(cols), CONTRACT_COLUMNS, preferred_element_type=F32
        )
        scores = scores * scale + bias
        raised = jnp.exp(scores - jnp.max(scores, axis=1, keepdims=True))
        probability[head] = raised / jnp.sum(raised, axis=1, keepdims=True)

    def give_back(part, cols):
        to_before[:, cols] = part[:TOK_DEV].astype(BF16)
        own[:, cols] = part[TOK_DEV : 2 * TOK_DEV]
        to_after[:, cols] = part[2 * TOK_DEV :].astype(BF16)

    def attend(head):
        cols = lanes(head)
        weights = probability[head].astype(BF16)
        output = jnp.dot(weights, window(value_cols(head)), preferred_element_type=F32)
        attended[:, cols] = output.astype(BF16)
        part = lax.dot_general(
            weights, grad_att[:, cols], CONTRACT_ROWS, preferred_element_type=F32
        )
        give_back(part, value_cols(head))

    def attend_back(head):
        cols = lanes(head)
        grad = grad_att[:, cols]
        keys = window(cols)
        delta = jnp.sum(
            grad.astype(F32) * attended[:, cols].astype(F32), axis=1, keepdims=True
        )
        grad_prob = lax.dot_general(
            grad, window(value_cols(head)), CONTRACT_COLUMNS, preferred_element_type=F32
        )
        grad_score = (probability[head] * (grad_prob - delta) * scale).astype(BF16)
        grad_query[:, cols] = jnp.dot(grad_score, keys, preferred_element_type=F32).astype(BF16)
        part = lax.dot_general(
            grad_score, query[:, cols], CONTRACT_ROWS, preferred_element_type=F32
        )
        give_back(part, cols)

    pair_count = LOCAL_HEADS // 2
    back_at = copies.reserve(4 * pair_count)

    def returned(i):
        cols = lanes(i, 2 * HEAD)
        down, up = back_at + i, back_at + 2 * pair_count + i
        return (
            remote(
                to_before.at[:, cols], from_after.at[:, cols], send.at[down], recv.at[down], preceding
            ),
            remote(
                to_after.at[:, cols], from_before.at[:, cols], send.at[up], recv.at[up], following
            ),
        )

    def send_back(i):
        down, up = returned(i)

        @pl.when(has_before)
        def _():
            down.start()

        @pl.when(has_after)
        def _():
            up.start()

    def take_back(first):
        @pl.when(has_after)
        def _():
            for i in range(first, first + pair_count):
                down, up = returned(i)
                down.wait_recv()
                up.wait_send()

        @pl.when(has_before)
        def _():
            for i in range(first, first + pair_count):
                down, up = returned(i)
                down.wait_send()
                up.wait_recv()

    def settle(out, first):
        cols = pl.ds(first, INNER)
        out[...] = added(own[:, cols], from_after[:, cols], from_before[:, cols])

    take_halo(0)
    lax.fori_loop(0, pair_count, pairs(weigh), 0)
    normed_ring.pass_on()
    take_halo(1)
    normed_ring.begin_slow(1)

    def attend_pair(i, carry):
        pairs(attend)(i, carry)
        send_back(i + pair_count)
        return carry

    lax.fori_loop(0, pair_count, attend_pair, 0)
    all_attended[pl.ds(0, TOK_DEV), :] = attended[...]
    attended_ring.begin()
    attended_ring.begin_slow(None)

    def back_pair(i, carry):
        pairs(attend_back)(i, carry)
        send_back(i)
        return carry

    lax.fori_loop(0, pair_count, back_pair, 0)

    def swap_columns(src, dst, cols, i):
        stay = pltpu.make_async_copy(
            src.at[:, lanes(mine)], dst.at[pl.ds(0, TOK_DEV), cols], local.at[i]
        )
        stay.start()
        return [stay] + exchange_y(
            lambda to, core: src.at[:, lanes(to * 2 + core)],
            lambda slot: dst.at[lanes(slot), cols],
        )

    sent_query = swap_columns(grad_query, grads_a, pl.ds(0, HEAD), 7)

    def out_chunk(i, carry):
        cols = lanes(i, WIDE)
        rows = pl.ds(pl.multiple_of(i * WIDE, WIDE), WIDE)
        product = lax.dot_general(
            attended[...], w_out[rows, :], CONTRACT_COLUMNS, preferred_element_type=F32
        )
        layer_out[:, cols] = (tokens[:, cols].astype(F32) + product).astype(BF16)
        return carry

    lax.fori_loop(0, D // WIDE, out_chunk, 0)
    stored = [
        pltpu.make_async_copy(layer_out, layer_out_hbm, local.at[13]),
        pltpu.make_async_copy(grad_tokens, grad_tokens_hbm, local.at[14]),
    ]
    stored[0].start()
    take_back(pair_count)
    settle(grad_values, INNER)
    sent_values = swap_columns(grad_values, grads_a, pl.ds(HEAD, HEAD), 8)
    attended_ring.pass_on()

    def grad_chunk_a(i, carry):
        rows = pl.ds(pl.multiple_of(i * WIDE, WIDE), WIDE)
        grad_normed[:, lanes(i, WIDE)] = lax.dot_general(
            grad_query[...], w_query[rows, :], CONTRACT_COLUMNS, preferred_element_type=F32
        ) + lax.dot_general(
            grad_values[...], w_values[rows, :], CONTRACT_COLUMNS, preferred_element_type=F32
        )
        return carry

    lax.fori_loop(0, D // WIDE, grad_chunk_a, 0)
    normed_ring.share_far()
    take_back(0)
    settle(grad_keys, 0)
    sent_keys = swap_columns(grad_keys, grads_b, pl.ds(0, HEAD), 9)
    keep = [pltpu.make_async_copy(turned(z, c), cot_rows.at[:, lanes(0)], local.at[6])]
    keep[0].start()
    sent_cot = exchange_z(turned, lambda slot: cot_rows.at[:, lanes(slot)])
    normed_ring.share_back()
    attended_ring.share_back()
    attended_ring.share_far()
    normed_ring.end()

    def multiply(grads, part, width):
        def chunk(i, carry):
            rows = pl.ds(pl.multiple_of(i * WIDE, WIDE), WIDE)
            product = jnp.dot(all_normed[rows, :], grads[...], preferred_element_type=F32)
            part[i // 4, i % 4] = product.astype(BF16).reshape(4, ROWS, width)
            return carry

        lax.fori_loop(0, D // WIDE, chunk, 0)

    def half(lo):
        return pl.ds(pl.multiple_of(lo * HALF_ROWS, HALF_ROWS), HALF_ROWS)

    first_y, last_y = pl.ds(0, 2), pl.ds(2, 2)

    def scatter(grads, part, width, x_first, z_first):
        multiply(grads, part, width)
        x_sent, z_sent = [], []
        for o in STEPS:
            to = (x + o) % 4
            x_sent.append(
                copies.start(part.at[:, first_y, to], x_first.at[o - 1], at(to, y, z, c))
            )
            to = (z + o) % 4
            z_sent.append(
                copies.start(
                    part.at[to // 2, last_y, :, half(to % 2)], z_first.at[o - 1], at(x, y, to, c)
                )
            )
        return x_sent, z_sent

    def scatter_on(sent, part, x_first, z_first, x_summed, z_summed, then_z, then_x):
        x_sent, z_sent = sent
        wait_all(x_sent)
        x_summed[...] = added(part[:, first_y, x], x_first[0], x_first[1], x_first[2])
        z_then = []
        for o in STEPS:
            to = (z + o) % 4
            z_then.append(
                copies.start(
                    x_summed.at[to // 2, :, half(to % 2)], then_z.at[o - 1], at(x, y, to, c)
                )
            )
        wait_all(z_sent)
        z_summed[...] = added(
            part[z_hi, last_y, :, half(z_lo)], z_first[0], z_first[1], z_first[2]
        )
        x_then = [
            copies.start(z_summed.at[:, (x + o) % 4], then_x.at[o - 1], at((x + o) % 4, y, z, c))
            for o in STEPS
        ]
        return z_then, x_then

    finals = [
        (o, lo, other)
        for o in range(RING)
        for lo in range(2)
        for other in range(2)
        if o + lo + other
    ]

    def gather_sums(sent, x_summed, z_summed, then_z, then_x, whole, out, width, i):
        z_then, x_then = sent
        wait_all(z_then)
        whole[first_y] = added(x_summed[z_hi, :, half(z_lo)], then_z[0], then_z[1], then_z[2])
        wait_all(x_then)
        whole[last_y] = added(z_summed[:, x], then_x[0], then_x[1], then_x[2])
        own_place = out.at[half(z_lo), lanes(mine, width)]
        stay = pltpu.make_async_copy(whole.at[y], own_place, local.at[i])
        stay.start()
        last = [stay]
        for o, lo, other in finals:
            to = (y + o) % 4
            device = at(x, to, z_hi * 2 + (z_lo + lo) % 2, (c + other) % 2)
            last.append(copies.start(whole.at[to], own_place, device))
        return last

    wait_all(sent_query + sent_values)
    sent_a = scatter(grads_a, part_a, 2 * HEAD, x_first_a, z_first_a)

    wait_all(sent_keys)
    sent_b = scatter(grads_b, part_b, HEAD, x_first_b, z_first_b)

    def grad_chunk_b(i, total):
        rows, cols = pl.ds(pl.multiple_of(i * WIDE, WIDE), WIDE), lanes(i, WIDE)
        product = grad_normed[:, cols] + lax.dot_general(
            grad_keys[...], w_keys[rows, :], CONTRACT_COLUMNS, preferred_element_type=F32
        )
        grad_normed[:, cols] = product
        along = product * (tokens[:, cols].astype(F32) * inv_rms[...])
        return total + jnp.sum(along, axis=1, keepdims=True)

    total = lax.fori_loop(0, D // WIDE, grad_chunk_b, jnp.zeros((TOK_DEV, 1), F32))
    mean = total * (1.0 / D)

    def tokens_chunk(i, carry):
        cols = lanes(i, WIDE)
        normed_wide = tokens[:, cols].astype(F32) * inv_rms[...]
        branch = inv_rms[...] * (grad_normed[:, cols] - normed_wide * mean)
        grad_tokens[:, cols] = (upstream[:, cols].astype(F32) + branch).astype(BF16)
        return carry

    wait_all(keep + sent_cot)
    attended_ring.end()

    def out_part(i, carry):
        cols = lanes(i, WIDE)
        product = jnp.dot(cot_rows[...], all_attended[:, cols], preferred_element_type=F32)
        part_out[:, :, cols] = product.astype(BF16).reshape(4, ROWS, WIDE)
        return carry

    lax.fori_loop(0, INNER // WIDE, out_part, 0)
    y_sent_out = [
        copies.start(
            part_out.at[:, :, lanes((y + o) % 4, WIDE)],
            y_first_out.at[o - 1],
            at(x, (y + o) % 4, z, c),
        )
        for o in STEPS
    ]
    then_a = scatter_on(
        sent_a, part_a, x_first_a, z_first_a, x_summed_a, z_summed_a, then_z_a, then_x_a
    )
    wait_all(y_sent_out)
    y_summed_out[...] = added(
        part_out[:, :, lanes(y, WIDE)], y_first_out[0], y_first_out[1], y_first_out[2]
    )
    x_then_out = [
        copies.start(
            y_summed_out.at[(x + o) % 4], then_x_out.at[o - 1], at((x + o) % 4, y, z, c)
        )
        for o in STEPS
    ]
    lax.fori_loop(0, D // WIDE, tokens_chunk, 0)
    stored[1].start()
    then_b = scatter_on(
        sent_b, part_b, x_first_b, z_first_b, x_summed_b, z_summed_b, then_z_b, then_x_b
    )
    last = gather_sums(
        then_a, x_summed_a, z_summed_a, then_z_a, then_x_a, whole_a, sum_a, 2 * HEAD, 10
    )

    wait_all(x_then_out)
    whole_out[...] = added(y_summed_out[x], then_x_out[0], then_x_out[1], then_x_out[2])
    final_at = copies.reserve(4)
    owner = 2 * z_lo + c
    holds_own = y == owner
    out_place = sum_out.at[:, lanes(y, WIDE)]
    outgoing = [
        remote(
            whole_out,
            out_place,
            send.at[final_at + 2 * lo + other],
            recv.at[final_at + y],
            at(x, owner, z_hi * 2 + (z_lo + lo) % 2, (c + other) % 2),
        )
        for lo in range(2)
        for other in range(2)
    ]
    for copy in outgoing[1:]:
        copy.start()

    @pl.when(jnp.logical_not(holds_own))
    def _():
        outgoing[0].start()

    @pl.when(holds_own)
    def _():
        stay = pltpu.make_async_copy(whole_out, out_place, local.at[12])
        stay.start()
        stay.wait()

    last += gather_sums(
        then_b, x_summed_b, z_summed_b, then_z_b, then_x_b, whole_b, sum_b, HEAD, 11
    )
    for copy in outgoing[1:]:
        copy.wait_send()

    @pl.when(jnp.logical_not(holds_own))
    def _():
        outgoing[0].wait_send()

    for source in range(RING):
        incoming = remote(
            whole_out,
            sum_out.at[:, lanes(source, WIDE)],
            send.at[final_at],
            recv.at[final_at + source],
            at(x, source, z_hi * 2 + y // 2, y % 2),
        )

        @pl.when(jnp.logical_not(holds_own & (y == source)))
        def _(incoming=incoming):
            incoming.wait_recv()

    wait_all(last + stored)


def whole_layer(tokens, upstream, w_qkv, w_out, key_blocks, key_count):
    pair = (TOK_DEV, 2 * INNER)
    narrow = (TOK_DEV, INNER)
    full = (TOK_DEV, D)
    weight = (D, INNER)
    scratch = [
        (full, BF16),
        (full, BF16),
        (full, BF16),
        (full, BF16),
        (weight, BF16),
        (weight, BF16),
        (weight, BF16),
        (weight, BF16),
        ((TOK_DEV, 1), F32),
        (full, BF16),
        ((D, TOK_DEV), BF16),
        ((D, ALL_TOK), BF16),
        ((WIDE, ALL_TOK), BF16),
        ((ALL_TOK, INNER), BF16),
        (narrow, BF16),
        (pair, BF16),
        (pair, BF16),
        (pair, BF16),
        (narrow, BF16),
        ((LOCAL_HEADS, TOK_DEV, WINDOW), F32),
        (narrow, BF16),
        (narrow, BF16),
        (narrow, BF16),
        (narrow, BF16),
        (pair, F32),
        (pair, BF16),
        (pair, BF16),
        (pair, BF16),
        (pair, BF16),
        (full, F32),
        ((ALL_TOK, 2 * HEAD), BF16),
        ((ALL_TOK, HEAD), BF16),
        ((2, 4, 4, ROWS, 2 * HEAD), BF16),
        ((2, 4, 4, ROWS, HEAD), BF16),
        ((4, ROWS, INNER), BF16),
        ((3, 2, 2, ROWS, 2 * HEAD), BF16),
        ((3, 2, 4, HALF_ROWS, 2 * HEAD), BF16),
        ((3, 2, 2, ROWS, HEAD), BF16),
        ((3, 2, 4, HALF_ROWS, HEAD), BF16),
        ((3, 4, ROWS, WIDE), BF16),
        ((2, 2, ROWS, 2 * HEAD), BF16),
        ((2, 4, HALF_ROWS, 2 * HEAD), BF16),
        ((2, 2, ROWS, HEAD), BF16),
        ((2, 4, HALF_ROWS, HEAD), BF16),
        ((4, ROWS, WIDE), BF16),
        ((3, 2, HALF_ROWS, 2 * HEAD), BF16),
        ((3, 2, HALF_ROWS, 2 * HEAD), BF16),
        ((3, 2, HALF_ROWS, HEAD), BF16),
        ((3, 2, HALF_ROWS, HEAD), BF16),
        ((3, ROWS, WIDE), BF16),
        ((4, HALF_ROWS, 2 * HEAD), BF16),
        ((4, HALF_ROWS, HEAD), BF16),
        ((ROWS, WIDE), BF16),
    ]
    semaphores = 140
    anywhere = pl.BlockSpec(memory_space=pl.ANY)
    scalars = pl.BlockSpec(memory_space=pltpu.SMEM)
    vector = pl.BlockSpec(memory_space=pltpu.VMEM)
    return pl.pallas_call(
        layer_kernel,
        out_shape=(
            jax.ShapeDtypeStruct(full, BF16),
            jax.ShapeDtypeStruct(full, BF16),
            jax.ShapeDtypeStruct((ROWS, 2 * INNER), BF16),
            jax.ShapeDtypeStruct((ROWS, INNER), BF16),
            jax.ShapeDtypeStruct((ROWS, INNER), BF16),
        ),
        in_specs=[anywhere] * 4 + [scalars] * 2,
        out_specs=(anywhere,) * 2 + (vector,) * 3,
        scratch_shapes=[pltpu.VMEM(shape, dtype) for shape, dtype in scratch]
        + [
            pltpu.SemaphoreType.DMA((semaphores,)),
            pltpu.SemaphoreType.DMA((semaphores,)),
            pltpu.SemaphoreType.DMA((15,)),
        ],
        compiler_params=pltpu.CompilerParams(
            collective_id=0, has_side_effects=True, vmem_limit_bytes=VMEM_LIMIT
        ),
        name="whole_layer",
    )(tokens, upstream, w_qkv, w_out, key_blocks, key_count)


def finish_kernel(
    factor, layer_in, tokens_in, sum_a, sum_b, sum_out, layer_out, grad_tokens, grad_qkv, grad_out
):
    layer_out[...] = layer_in[...]
    grad_tokens[...] = tokens_in[...]
    for head in range(LOCAL_HEADS):
        cols = lanes(head)
        grad_qkv[:, cols] = sum_a[:, lanes(2 * head)].astype(F32) * factor
        grad_qkv[:, lanes(head + LOCAL_HEADS)] = sum_b[:, cols].astype(F32) * factor
        grad_qkv[:, lanes(head + 2 * LOCAL_HEADS)] = (
            sum_a[:, lanes(2 * head + 1)].astype(F32) * factor
        )
    grad_out[...] = sum_out[...].astype(F32) * factor


def finish(factor, *results):
    full = jax.ShapeDtypeStruct((TOK_DEV, D), BF16)
    outs = (
        full,
        full,
        jax.ShapeDtypeStruct((ROWS, 3 * INNER), F32),
        jax.ShapeDtypeStruct((ROWS, INNER), F32),
    )
    steps = 2

    def blocks(arrays):
        return tuple(
            pl.BlockSpec((a.shape[0] // steps, a.shape[1]), lambda i: (i, 0)) for a in arrays
        )

    return pl.pallas_call(
        functools.partial(finish_kernel, factor),
        grid=(steps,),
        out_shape=outs,
        in_specs=blocks(results),
        out_specs=blocks(outs),
        name="finish",
    )(*results)


def body(tokens, cotangent, w_qkv, w_out, key_blocks, key_count):
    factor = 1.0 / math.sqrt(lax.axis_size("dp") * lax.axis_size("seq") * TOK_DEV)
    results = whole_layer(
        tokens[0], cotangent[0], w_qkv, w_out, key_blocks.T, key_count
    )
    layer_out, grad_tokens, grad_w_qkv, grad_w_out = finish(factor, *results)
    return (layer_out[None], grad_tokens[None], grad_w_qkv, grad_w_out)


def solution(mesh):
    return jax.shard_map(
        body,
        mesh=mesh,
        in_specs=(P("dp", "seq", None), P("dp", "seq", None), P(), P(), P(), P()),
        out_specs=(P("dp", "seq", None), P("dp", "seq", None), P("seq", None), P("seq", None)),
        check_vma=False,
    )
```

```python
import functools
import math

import jax
import jax.numpy as jnp
from jax import lax
from jax.experimental import pallas as pl
from jax.experimental.pallas import tpu as pltpu
from jax.sharding import PartitionSpec as P

LOCAL_HEADS = 8
HEAD = 128
INNER = LOCAL_HEADS * HEAD
D = 2048
TOK_DEV = 128
N_SEQ = 32
RING = 4
GROUP = 2 * RING
WINDOW = 3 * TOK_DEV
ALL_TOK = GROUP * TOK_DEV
ROWS = D // N_SEQ
HALF_ROWS = ROWS // 2
WIDE = 256
VMEM_LIMIT = 63 * 1024 * 1024

epsilon = 1e-06

BF16 = jnp.bfloat16
F32 = jnp.float32
CONTRACT_COLUMNS = (((1,), (1,)), ((), ()))
CONTRACT_ROWS = (((0,), (0,)), ((), ()))
STEPS = range(1, RING)
GROUP_STEPS = [(o, other) for o in range(RING) for other in range(2) if o + other]


def place():
    dp, seq = lax.axis_index("dp"), lax.axis_index("seq")
    return seq % 4, (seq // 4) % 4, (seq // 16) * 2 + dp // 2, dp % 2


def at(x, y, z, c):
    return {"dp": (z % 2) * 2 + c, "seq": (z // 2) * 16 + y * 4 + x}


def lanes(slot, width=HEAD):
    start = slot * width
    return pl.ds(start if isinstance(start, int) else pl.multiple_of(start, width), width)


def remote(src, dst, send, recv, device):
    return pltpu.make_async_remote_copy(
        src_ref=src,
        dst_ref=dst,
        send_sem=send,
        recv_sem=recv,
        device_id=device,
        device_id_type=pl.DeviceIdType.MESH,
    )


class Copies:
    def __init__(self, send, recv):
        self.send, self.recv, self.used = send, recv, 0

    def reserve(self, count):
        first = self.used
        self.used += count
        return first

    def start(self, src, dst, device):
        i = self.reserve(1)
        copy = remote(src, dst, self.send.at[i], self.recv.at[i], device)
        copy.start()
        return copy


def wait_all(copies):
    for copy in copies:
        copy.wait()


def signal_all(peers):
    barrier = pltpu.get_barrier_semaphore()
    for peer in peers:
        pl.semaphore_signal(
            barrier, inc=1, device_id=peer, device_id_type=pl.DeviceIdType.MESH
        )


class RingGather:
    def __init__(self, copies, slot, fast, slow, partner):
        self.copies, self.slot = copies, slot
        self.fast, self.slow, self.partner = fast, slow, partner
        self.waits, self.back = [], []

    def start(self, src, dst, device, part=None):
        return self.copies.start(self.slot(src, part), self.slot(dst, part), device)

    def begin(self):
        self.near = self.start(0, 2, self.fast)
        self.waits.append(self.start(0, 1, self.partner))

    def pass_on(self):
        self.near.wait()
        self.far = self.start(2, 4, self.fast)
        self.waits.append(self.start(2, 3, self.partner))

    def begin_slow(self, part):
        self.back.append(self.start(0, 6, self.slow, part))

    def share_far(self):
        self.far.wait()
        self.waits.append(self.start(4, 5, self.partner))

    def share_back(self):
        wait_all(self.back)
        self.waits.append(self.start(6, 7, self.partner))

    def end(self):
        wait_all(self.waits)


def added(first, *others):
    total = first.astype(F32)
    for other in others:
        total = total + other.astype(F32)
    return total.astype(BF16)


def layer_kernel(
    tokens_hbm,
    upstream_hbm,
    w_qkv_hbm,
    w_out_hbm,
    key_blocks,
    key_count,
    layer_out,
    grad_tokens,
    sum_a,
    sum_b,
    sum_out,
    tokens,
    upstream,
    w_query,
    w_keys,
    w_values,
    w_out,
    inv_rms,
    normed,
    upstream_t,
    all_normed,
    cot_rows,
    all_attended,
    query,
    kv,
    before,
    after,
    grad_att,
    probability,
    attended,
    grad_query,
    grad_keys,
    grad_values,
    own,
    to_before,
    to_after,
    from_after,
    from_before,
    grad_normed,
    grads_a,
    grads_b,
    part_a,
    part_b,
    part_out,
    x_first_a,
    z_first_a,
    x_first_b,
    z_first_b,
    y_first_out,
    x_summed_a,
    z_summed_a,
    x_summed_b,
    z_summed_b,
    y_summed_out,
    then_z_a,
    then_x_a,
    then_z_b,
    then_x_b,
    then_x_out,
    whole_a,
    whole_b,
    whole_out,
    send,
    recv,
    local,
):
    x, y, z, c = place()
    dp, seq = lax.axis_index("dp"), lax.axis_index("seq")
    z_hi, z_lo = z // 2, z % 2
    mine = y * 2 + c
    sign = jnp.where(x < 2, -1, 1)
    following = {"dp": dp, "seq": (seq + 1) % N_SEQ}
    preceding = {"dp": dp, "seq": (seq + N_SEQ - 1) % N_SEQ}
    has_after, has_before = seq < N_SEQ - 1, seq > 0
    scale = HEAD ** (-0.5)
    copies = Copies(send, recv)

    loads = {
        name: pltpu.make_async_copy(src, dst, local.at[i])
        for i, (name, src, dst) in enumerate(
            [
                ("tokens", tokens_hbm, tokens),
                ("keys", w_qkv_hbm.at[:, pl.ds(INNER, INNER)], w_keys),
                ("values", w_qkv_hbm.at[:, pl.ds(2 * INNER, INNER)], w_values),
                ("upstream", upstream_hbm, upstream),
                ("query", w_qkv_hbm.at[:, pl.ds(0, INNER)], w_query),
                ("out", w_out_hbm, w_out),
            ]
        )
    }
    loads["tokens"].start()
    loads["keys"].start()

    peers = [
        at(x, (y + o) % 4, z_hi * 2 + (z_lo + lo) % 2, (c + other) % 2)
        for o in range(RING)
        for lo in range(2)
        for other in range(2)
        if o + lo + other
    ]
    peers += [at(x, y, (1 - z_hi) * 2 + lo, core) for lo in range(2) for core in range(2)]
    peers += [at((x + o) % 4, y, z, c) for o in STEPS]
    peers += [following, preceding]
    signal_all(peers)

    zero_block = jnp.zeros((TOK_DEV, 2 * INNER), BF16)

    @pl.when(jnp.logical_not(has_before))
    def _():
        before[...] = zero_block
        from_before[...] = zero_block

    @pl.when(jnp.logical_not(has_after))
    def _():
        after[...] = zero_block
        from_after[...] = zero_block

    count = key_count[seq]
    listed = [key_blocks[j, seq] for j in range(3)]
    biases = []
    for shift in (-1, 0, 1):
        used = jnp.int32(0)
        for j in range(3):
            hit = jnp.where(listed[j] == seq + shift, 1, 0) * jnp.where(j < count, 1, 0)
            used = used + hit
        used = jnp.full((1, TOK_DEV), used, jnp.int32)
        biases.append(jnp.where(used > 0, 0.0, -jnp.inf).astype(F32))
    bias = jnp.concatenate(biases, axis=1)

    loads["tokens"].wait()
    loads["values"].start()
    wide_tokens = tokens[...].astype(F32)
    inv_rms[...] = lax.rsqrt(jnp.mean(wide_tokens * wide_tokens, axis=1, keepdims=True) + epsilon)
    normed[...] = (wide_tokens * inv_rms[...]).astype(BF16)

    def project(rows, weight, out, first):
        def chunk(i, carry):
            product = jnp.dot(rows[...], weight[:, lanes(i, WIDE)], preferred_element_type=F32)
            out[:, lanes(i + first, WIDE)] = product.astype(BF16)
            return carry

        lax.fori_loop(0, INNER // WIDE, chunk, 0)

    def halo(i, part):
        cols = pl.ds(part * INNER, INNER)
        return (
            remote(kv.at[:, cols], before.at[:, cols], send.at[i], recv.at[i], following),
            remote(kv.at[:, cols], after.at[:, cols], send.at[i + 1], recv.at[i + 1], preceding),
        )

    halo_at = [copies.reserve(2), copies.reserve(2)]

    def send_halo(part):
        forth, back = halo(halo_at[part], part)

        @pl.when(has_after)
        def _():
            forth.start()

        @pl.when(has_before)
        def _():
            back.start()

    def take_halo(part):
        forth, back = halo(halo_at[part], part)

        @pl.when(has_after)
        def _():
            forth.wait_send()
            back.wait_recv()

        @pl.when(has_before)
        def _():
            back.wait_send()
            forth.wait_recv()

    def turn(rows, out):
        def chunk(i, carry):
            out[pl.ds(pl.multiple_of(i * WIDE, WIDE), WIDE), pl.ds(0, TOK_DEV)] = jnp.transpose(
                rows[:, lanes(i, WIDE)]
            )
            return carry

        lax.fori_loop(0, D // WIDE, chunk, 0)

    def exchange_y(src_view, dst_view):
        sent = []
        for o, other in GROUP_STEPS:
            to, core = (y + sign * o + 4) % 4, (c + other) % 2
            sent.append(
                copies.start(src_view(to, core), dst_view(2 * o + other), at(x, to, z, core))
            )
        return sent

    def exchange_z(src_view, dst_view):
        sent = []
        for o, other in GROUP_STEPS:
            to, core = (z + o) % 4, (c + other) % 2
            sent.append(
                copies.start(src_view(to, core), dst_view(2 * o + other), at(x, y, to, core))
            )
        return sent

    partner = at(x, y, z, 1 - c)
    fast, slow = at(x, (y + sign + 4) % 4, z, c), at(x, (y - sign + 4) % 4, z, c)

    def normed_slot(slot, part):
        rows = pl.ds(0, D) if part is None else pl.ds(part * (D // 2), D // 2)
        return all_normed.at[rows, lanes(slot)]

    def attended_slot(slot, part):
        cols = pl.ds(0, INNER) if part is None else pl.ds(part * (INNER // 2), INNER // 2)
        return all_attended.at[lanes(slot), cols]

    normed_ring = RingGather(copies, normed_slot, fast, slow, partner)
    attended_ring = RingGather(
        copies,
        attended_slot,
        at(x, y, (z + 1) % 4, c),
        at(x, y, (z + 3) % 4, c),
        partner,
    )

    turn(normed, all_normed)
    pl.semaphore_wait(pltpu.get_barrier_semaphore(), len(peers))
    normed_ring.begin()
    normed_ring.begin_slow(0)
    loads["keys"].wait()
    loads["upstream"].start()
    loads["query"].start()
    project(normed, w_keys, kv, 0)
    send_halo(0)
    loads["values"].wait()
    loads["out"].start()
    project(normed, w_values, kv, INNER // WIDE)
    send_halo(1)
    loads["upstream"].wait()
    turn(upstream, upstream_t)

    def turned(to, core):
        return upstream_t.at[lanes(to * 2 + core, WIDE), :]

    loads["query"].wait()
    project(normed, w_query, query, 0)
    loads["out"].wait()
    project(upstream, w_out, grad_att, 0)

    def pairs(body):
        def step(i, carry):
            for head in (2 * i, 2 * i + 1):
                body(head)
            return carry

        return step

    def window(cols):
        return jnp.concatenate([before[:, cols], kv[:, cols], after[:, cols]], axis=0)

    def value_cols(head):
        return lanes(head + LOCAL_HEADS)

    def weigh(head):
        cols = lanes(head)
        scores = lax.dot_general(
            query[:, cols], window(cols), CONTRACT_COLUMNS, preferred_element_type=F32
        )
        scores = scores * scale + bias
        raised = jnp.exp(scores - jnp.max(scores, axis=1, keepdims=True))
        probability[head] = raised / jnp.sum(raised, axis=1, keepdims=True)

    def give_back(part, cols):
        to_before[:, cols] = part[:TOK_DEV].astype(BF16)
        own[:, cols] = part[TOK_DEV : 2 * TOK_DEV]
        to_after[:, cols] = part[2 * TOK_DEV :].astype(BF16)

    def attend(head):
        cols = lanes(head)
        weights = probability[head].astype(BF16)
        output = jnp.dot(weights, window(value_cols(head)), preferred_element_type=F32)
        attended[:, cols] = output.astype(BF16)
        part = lax.dot_general(
            weights, grad_att[:, cols], CONTRACT_ROWS, preferred_element_type=F32
        )
        give_back(part, value_cols(head))

    def attend_back(head):
        cols = lanes(head)
        grad = grad_att[:, cols]
        keys = window(cols)
        delta = jnp.sum(
            grad.astype(F32) * attended[:, cols].astype(F32), axis=1, keepdims=True
        )
        grad_prob = lax.dot_general(
            grad, window(value_cols(head)), CONTRACT_COLUMNS, preferred_element_type=F32
        )
        grad_score = (probability[head] * (grad_prob - delta) * scale).astype(BF16)
        grad_query[:, cols] = jnp.dot(grad_score, keys, preferred_element_type=F32).astype(BF16)
        part = lax.dot_general(
            grad_score, query[:, cols], CONTRACT_ROWS, preferred_element_type=F32
        )
        give_back(part, cols)

    pair_count = LOCAL_HEADS // 2
    back_at = copies.reserve(4 * pair_count)

    def returned(i):
        cols = lanes(i, 2 * HEAD)
        down, up = back_at + i, back_at + 2 * pair_count + i
        return (
            remote(
                to_before.at[:, cols], from_after.at[:, cols], send.at[down], recv.at[down], preceding
            ),
            remote(
                to_after.at[:, cols], from_before.at[:, cols], send.at[up], recv.at[up], following
            ),
        )

    def send_back(i):
        down, up = returned(i)

        @pl.when(has_before)
        def _():
            down.start()

        @pl.when(has_after)
        def _():
            up.start()

    def take_back(first):
        @pl.when(has_after)
        def _():
            for i in range(first, first + pair_count):
                down, up = returned(i)
                down.wait_recv()
                up.wait_send()

        @pl.when(has_before)
        def _():
            for i in range(first, first + pair_count):
                down, up = returned(i)
                down.wait_send()
                up.wait_recv()

    def settle(out, first):
        cols = pl.ds(first, INNER)
        out[...] = added(own[:, cols], from_after[:, cols], from_before[:, cols])

    take_halo(0)
    lax.fori_loop(0, pair_count, pairs(weigh), 0)
    normed_ring.pass_on()
    take_halo(1)

    def attend_pair(i, carry):
        pairs(attend)(i, carry)
        send_back(i + pair_count)
        return carry

    lax.fori_loop(0, pair_count, attend_pair, 0)
    all_attended[pl.ds(0, TOK_DEV), :] = attended[...]
    attended_ring.begin()
    attended_ring.begin_slow(None)

    def back_pair(i, carry):
        pairs(attend_back)(i, carry)
        send_back(i)
        return carry

    lax.fori_loop(0, pair_count, back_pair, 0)

    def swap_columns(src, dst, cols, i):
        stay = pltpu.make_async_copy(
            src.at[:, lanes(mine)], dst.at[pl.ds(0, TOK_DEV), cols], local.at[i]
        )
        stay.start()
        return [stay] + exchange_y(
            lambda to, core: src.at[:, lanes(to * 2 + core)],
            lambda slot: dst.at[lanes(slot), cols],
        )

    sent_query = swap_columns(grad_query, grads_a, pl.ds(0, HEAD), 7)

    def out_chunk(i, carry):
        cols = lanes(i, WIDE)
        rows = pl.ds(pl.multiple_of(i * WIDE, WIDE), WIDE)
        product = lax.dot_general(
            attended[...], w_out[rows, :], CONTRACT_COLUMNS, preferred_element_type=F32
        )
        layer_out[:, cols] = (tokens[:, cols].astype(F32) + product).astype(BF16)
        return carry

    lax.fori_loop(0, D // WIDE, out_chunk, 0)
    take_back(pair_count)
    normed_ring.begin_slow(1)
    settle(grad_values, INNER)
    sent_values = swap_columns(grad_values, grads_a, pl.ds(HEAD, HEAD), 8)
    attended_ring.pass_on()

    def grad_chunk_a(i, carry):
        rows = pl.ds(pl.multiple_of(i * WIDE, WIDE), WIDE)
        grad_normed[:, lanes(i, WIDE)] = lax.dot_general(
            grad_query[...], w_query[rows, :], CONTRACT_COLUMNS, preferred_element_type=F32
        ) + lax.dot_general(
            grad_values[...], w_values[rows, :], CONTRACT_COLUMNS, preferred_element_type=F32
        )
        return carry

    lax.fori_loop(0, D // WIDE, grad_chunk_a, 0)
    normed_ring.share_far()
    take_back(0)
    settle(grad_keys, 0)
    sent_keys = swap_columns(grad_keys, grads_b, pl.ds(0, HEAD), 9)
    keep = [pltpu.make_async_copy(turned(z, c), cot_rows.at[:, lanes(0)], local.at[6])]
    keep[0].start()
    sent_cot = exchange_z(turned, lambda slot: cot_rows.at[:, lanes(slot)])
    normed_ring.share_back()
    attended_ring.share_back()
    attended_ring.share_far()
    normed_ring.end()

    def multiply(grads, part, width):
        def chunk(i, carry):
            rows = pl.ds(pl.multiple_of(i * WIDE, WIDE), WIDE)
            product = jnp.dot(all_normed[rows, :], grads[...], preferred_element_type=F32)
            part[i // 4, i % 4] = product.astype(BF16).reshape(4, ROWS, width)
            return carry

        lax.fori_loop(0, D // WIDE, chunk, 0)

    def half(lo):
        return pl.ds(pl.multiple_of(lo * HALF_ROWS, HALF_ROWS), HALF_ROWS)

    first_y, last_y = pl.ds(0, 2), pl.ds(2, 2)

    def scatter(grads, part, width, x_first, z_first):
        multiply(grads, part, width)
        x_sent, z_sent = [], []
        for o in STEPS:
            to = (x + o) % 4
            x_sent.append(
                copies.start(part.at[:, first_y, to], x_first.at[o - 1], at(to, y, z, c))
            )
            to = (z + o) % 4
            z_sent.append(
                copies.start(
                    part.at[to // 2, last_y, :, half(to % 2)], z_first.at[o - 1], at(x, y, to, c)
                )
            )
        return x_sent, z_sent

    def scatter_on(sent, part, x_first, z_first, x_summed, z_summed, then_z, then_x):
        x_sent, z_sent = sent
        wait_all(x_sent)
        x_summed[...] = added(part[:, first_y, x], x_first[0], x_first[1], x_first[2])
        z_then = []
        for o in STEPS:
            to = (z + o) % 4
            z_then.append(
                copies.start(
                    x_summed.at[to // 2, :, half(to % 2)], then_z.at[o - 1], at(x, y, to, c)
                )
            )
        wait_all(z_sent)
        z_summed[...] = added(
            part[z_hi, last_y, :, half(z_lo)], z_first[0], z_first[1], z_first[2]
        )
        x_then = [
            copies.start(z_summed.at[:, (x + o) % 4], then_x.at[o - 1], at((x + o) % 4, y, z, c))
            for o in STEPS
        ]
        return z_then, x_then

    finals = [
        (o, lo, other)
        for o in range(RING)
        for lo in range(2)
        for other in range(2)
        if o + lo + other
    ]

    def gather_sums(sent, x_summed, z_summed, then_z, then_x, whole, out, width, i):
        z_then, x_then = sent
        wait_all(z_then)
        whole[first_y] = added(x_summed[z_hi, :, half(z_lo)], then_z[0], then_z[1], then_z[2])
        wait_all(x_then)
        whole[last_y] = added(z_summed[:, x], then_x[0], then_x[1], then_x[2])
        own_place = out.at[half(z_lo), lanes(mine, width)]
        stay = pltpu.make_async_copy(whole.at[y], own_place, local.at[i])
        stay.start()
        last = [stay]
        for o, lo, other in finals:
            to = (y + o) % 4
            device = at(x, to, z_hi * 2 + (z_lo + lo) % 2, (c + other) % 2)
            last.append(copies.start(whole.at[to], own_place, device))
        return last

    wait_all(sent_query + sent_values)
    sent_a = scatter(grads_a, part_a, 2 * HEAD, x_first_a, z_first_a)

    wait_all(sent_keys)
    sent_b = scatter(grads_b, part_b, HEAD, x_first_b, z_first_b)

    def grad_chunk_b(i, total):
        rows, cols = pl.ds(pl.multiple_of(i * WIDE, WIDE), WIDE), lanes(i, WIDE)
        product = grad_normed[:, cols] + lax.dot_general(
            grad_keys[...], w_keys[rows, :], CONTRACT_COLUMNS, preferred_element_type=F32
        )
        grad_normed[:, cols] = product
        along = product * (tokens[:, cols].astype(F32) * inv_rms[...])
        return total + jnp.sum(along, axis=1, keepdims=True)

    total = lax.fori_loop(0, D // WIDE, grad_chunk_b, jnp.zeros((TOK_DEV, 1), F32))
    mean = total * (1.0 / D)

    def tokens_chunk(i, carry):
        cols = lanes(i, WIDE)
        normed_wide = tokens[:, cols].astype(F32) * inv_rms[...]
        branch = inv_rms[...] * (grad_normed[:, cols] - normed_wide * mean)
        grad_tokens[:, cols] = (upstream[:, cols].astype(F32) + branch).astype(BF16)
        return carry

    wait_all(keep + sent_cot)
    attended_ring.end()

    def out_part(i, carry):
        cols = lanes(i, WIDE)
        product = jnp.dot(cot_rows[...], all_attended[:, cols], preferred_element_type=F32)
        part_out[:, :, cols] = product.astype(BF16).reshape(4, ROWS, WIDE)
        return carry

    lax.fori_loop(0, INNER // WIDE, out_part, 0)
    y_sent_out = [
        copies.start(
            part_out.at[:, :, lanes((y + o) % 4, WIDE)],
            y_first_out.at[o - 1],
            at(x, (y + o) % 4, z, c),
        )
        for o in STEPS
    ]
    then_a = scatter_on(
        sent_a, part_a, x_first_a, z_first_a, x_summed_a, z_summed_a, then_z_a, then_x_a
    )
    wait_all(y_sent_out)
    y_summed_out[...] = added(
        part_out[:, :, lanes(y, WIDE)], y_first_out[0], y_first_out[1], y_first_out[2]
    )
    x_then_out = [
        copies.start(
            y_summed_out.at[(x + o) % 4], then_x_out.at[o - 1], at((x + o) % 4, y, z, c)
        )
        for o in STEPS
    ]
    lax.fori_loop(0, D // WIDE, tokens_chunk, 0)
    then_b = scatter_on(
        sent_b, part_b, x_first_b, z_first_b, x_summed_b, z_summed_b, then_z_b, then_x_b
    )
    last = gather_sums(
        then_a, x_summed_a, z_summed_a, then_z_a, then_x_a, whole_a, sum_a, 2 * HEAD, 10
    )

    wait_all(x_then_out)
    whole_out[...] = added(y_summed_out[x], then_x_out[0], then_x_out[1], then_x_out[2])
    final_at = copies.reserve(4)
    owner = 2 * z_lo + c
    holds_own = y == owner
    out_place = sum_out.at[:, lanes(y, WIDE)]
    outgoing = [
        remote(
            whole_out,
            out_place,
            send.at[final_at + 2 * lo + other],
            recv.at[final_at + y],
            at(x, owner, z_hi * 2 + (z_lo + lo) % 2, (c + other) % 2),
        )
        for lo in range(2)
        for other in range(2)
    ]
    for copy in outgoing[1:]:
        copy.start()

    @pl.when(jnp.logical_not(holds_own))
    def _():
        outgoing[0].start()

    @pl.when(holds_own)
    def _():
        stay = pltpu.make_async_copy(whole_out, out_place, local.at[12])
        stay.start()
        stay.wait()

    last += gather_sums(
        then_b, x_summed_b, z_summed_b, then_z_b, then_x_b, whole_b, sum_b, HEAD, 11
    )
    for copy in outgoing[1:]:
        copy.wait_send()

    @pl.when(jnp.logical_not(holds_own))
    def _():
        outgoing[0].wait_send()

    for source in range(RING):
        incoming = remote(
            whole_out,
            sum_out.at[:, lanes(source, WIDE)],
            send.at[final_at],
            recv.at[final_at + source],
            at(x, source, z_hi * 2 + y // 2, y % 2),
        )

        @pl.when(jnp.logical_not(holds_own & (y == source)))
        def _(incoming=incoming):
            incoming.wait_recv()

    wait_all(last)


def whole_layer(tokens, upstream, w_qkv, w_out, key_blocks, key_count):
    pair = (TOK_DEV, 2 * INNER)
    narrow = (TOK_DEV, INNER)
    full = (TOK_DEV, D)
    weight = (D, INNER)
    scratch = [
        (full, BF16),
        (full, BF16),
        (weight, BF16),
        (weight, BF16),
        (weight, BF16),
        (weight, BF16),
        ((TOK_DEV, 1), F32),
        (full, BF16),
        ((D, TOK_DEV), BF16),
        ((D, ALL_TOK), BF16),
        ((WIDE, ALL_TOK), BF16),
        ((ALL_TOK, INNER), BF16),
        (narrow, BF16),
        (pair, BF16),
        (pair, BF16),
        (pair, BF16),
        (narrow, BF16),
        ((LOCAL_HEADS, TOK_DEV, WINDOW), F32),
        (narrow, BF16),
        (narrow, BF16),
        (narrow, BF16),
        (narrow, BF16),
        (pair, F32),
        (pair, BF16),
        (pair, BF16),
        (pair, BF16),
        (pair, BF16),
        (full, F32),
        ((ALL_TOK, 2 * HEAD), BF16),
        ((ALL_TOK, HEAD), BF16),
        ((2, 4, 4, ROWS, 2 * HEAD), BF16),
        ((2, 4, 4, ROWS, HEAD), BF16),
        ((4, ROWS, INNER), BF16),
        ((3, 2, 2, ROWS, 2 * HEAD), BF16),
        ((3, 2, 4, HALF_ROWS, 2 * HEAD), BF16),
        ((3, 2, 2, ROWS, HEAD), BF16),
        ((3, 2, 4, HALF_ROWS, HEAD), BF16),
        ((3, 4, ROWS, WIDE), BF16),
        ((2, 2, ROWS, 2 * HEAD), BF16),
        ((2, 4, HALF_ROWS, 2 * HEAD), BF16),
        ((2, 2, ROWS, HEAD), BF16),
        ((2, 4, HALF_ROWS, HEAD), BF16),
        ((4, ROWS, WIDE), BF16),
        ((3, 2, HALF_ROWS, 2 * HEAD), BF16),
        ((3, 2, HALF_ROWS, 2 * HEAD), BF16),
        ((3, 2, HALF_ROWS, HEAD), BF16),
        ((3, 2, HALF_ROWS, HEAD), BF16),
        ((3, ROWS, WIDE), BF16),
        ((4, HALF_ROWS, 2 * HEAD), BF16),
        ((4, HALF_ROWS, HEAD), BF16),
        ((ROWS, WIDE), BF16),
    ]
    semaphores = 140
    anywhere = pl.BlockSpec(memory_space=pl.ANY)
    scalars = pl.BlockSpec(memory_space=pltpu.SMEM)
    vector = pl.BlockSpec(memory_space=pltpu.VMEM)
    return pl.pallas_call(
        layer_kernel,
        out_shape=(
            jax.ShapeDtypeStruct(full, BF16),
            jax.ShapeDtypeStruct(full, BF16),
            jax.ShapeDtypeStruct((ROWS, 2 * INNER), BF16),
            jax.ShapeDtypeStruct((ROWS, INNER), BF16),
            jax.ShapeDtypeStruct((ROWS, INNER), BF16),
        ),
        in_specs=[anywhere] * 4 + [scalars] * 2,
        out_specs=(vector,) * 5,
        scratch_shapes=[pltpu.VMEM(shape, dtype) for shape, dtype in scratch]
        + [
            pltpu.SemaphoreType.DMA((semaphores,)),
            pltpu.SemaphoreType.DMA((semaphores,)),
            pltpu.SemaphoreType.DMA((13,)),
        ],
        compiler_params=pltpu.CompilerParams(
            collective_id=0, has_side_effects=True, vmem_limit_bytes=VMEM_LIMIT
        ),
        name="whole_layer",
    )(tokens, upstream, w_qkv, w_out, key_blocks, key_count)


def finish_kernel(
    factor, layer_in, tokens_in, sum_a, sum_b, sum_out, layer_out, grad_tokens, grad_qkv, grad_out
):
    layer_out[...] = layer_in[...]
    grad_tokens[...] = tokens_in[...]
    for head in range(LOCAL_HEADS):
        cols = lanes(head)
        grad_qkv[:, cols] = sum_a[:, lanes(2 * head)].astype(F32) * factor
        grad_qkv[:, lanes(head + LOCAL_HEADS)] = sum_b[:, cols].astype(F32) * factor
        grad_qkv[:, lanes(head + 2 * LOCAL_HEADS)] = (
            sum_a[:, lanes(2 * head + 1)].astype(F32) * factor
        )
    grad_out[...] = sum_out[...].astype(F32) * factor


def finish(factor, *results):
    full = jax.ShapeDtypeStruct((TOK_DEV, D), BF16)
    outs = (
        full,
        full,
        jax.ShapeDtypeStruct((ROWS, 3 * INNER), F32),
        jax.ShapeDtypeStruct((ROWS, INNER), F32),
    )
    steps = 2

    def blocks(arrays):
        return tuple(
            pl.BlockSpec((a.shape[0] // steps, a.shape[1]), lambda i: (i, 0)) for a in arrays
        )

    return pl.pallas_call(
        functools.partial(finish_kernel, factor),
        grid=(steps,),
        out_shape=outs,
        in_specs=blocks(results),
        out_specs=blocks(outs),
        name="finish",
    )(*results)


def body(tokens, cotangent, w_qkv, w_out, key_blocks, key_count):
    factor = 1.0 / math.sqrt(lax.axis_size("dp") * lax.axis_size("seq") * TOK_DEV)
    results = whole_layer(
        tokens[0], cotangent[0], w_qkv, w_out, key_blocks.T, key_count
    )
    layer_out, grad_tokens, grad_w_qkv, grad_w_out = finish(factor, *results)
    return (layer_out[None], grad_tokens[None], grad_w_qkv, grad_w_out)


def solution(mesh):
    return jax.shard_map(
        body,
        mesh=mesh,
        in_specs=(P("dp", "seq", None), P("dp", "seq", None), P(), P(), P(), P()),
        out_specs=(P("dp", "seq", None), P("dp", "seq", None), P("seq", None), P("seq", None)),
        check_vma=False,
    )
```
